512 devices in a mesh: dom: 32 (over y, x), orient: 16 (over z, core).
Axes of the slice: x: 4, y: 8, z: 8, core: 2. Of those that a mesh axis runs over, the one named last changes fastest.
Arguments:
- particles: bfloat16 [256, 2, 8192], P('dom'), may hold values from -4 to 4
- references: bfloat16 [256, 2, 8192], P('orient'), may hold values from -1.7 to 1.7
- phases: float32 [16, 8192], replicated, may hold values from -3.1416 to 3.1416
- mask: int32 [256, 256], P('dom', 'orient'), may hold values from 0 to 1, as said below
- ctf_group: int32 [256], replicated, may hold values from 0 to 63
- ctf_table: float32 [64, 64], replicated, may hold values from 0.1 to 1
- shell_index: int32 [8192], replicated, may hold values from 0 to 63
- sigma2: float32 [64], replicated, may hold values from 8 to 32
Outputs:
- posterior: float32 [256, 16, 256], P('dom', None, 'orient')
- image_sums: float32 [256, 2, 8192], P('orient', None, 'dom')
- ctf_weights: float32 [256, 64], P('orient')
- shell_noise: float32 [64], replicated
The draws below stay inside these ranges and needn't reach their ends.
Inputs may be any that keep to these rules, and one draw needn't show every extreme that they name: `mask`: every particle allows at least one orientation.
All inputs are finite; a program needn't handle non-finite values.
Results may differ from the reference program's by a relative error of at most 0.0041.
Values may be sent and summed in bfloat16 or wider, within the bound.
A program may use at most 192 MiB of HBM per device.

```python
import math
import jax
import jax.numpy as jnp
from jax import lax

PIX = 8192
SHELLS = 64
GROUPS = 64
TRANS = 16
PARTICLES = 256
ORIENTS = 256


def pairing(key):
    target = jax.random.randint(jax.random.fold_in(key, 11), (PARTICLES,), 0, ORIENTS)
    forced = jax.random.randint(jax.random.fold_in(key, 13), (), 0, PARTICLES)
    return (target, forced)


def reference_planes(key):
    spread_part = jax.random.uniform(jax.random.fold_in(key, 21), (ORIENTS, PIX), jnp.float32, -1.0, 1.0)
    angle_plane = jax.random.uniform(jax.random.fold_in(key, 22), (ORIENTS, PIX), jnp.float32, -3.14159, 3.14159)
    amplitude = jnp.sqrt(2.0 * (1.0 + 0.4 * spread_part))
    return jnp.stack([amplitude * jnp.cos(angle_plane), amplitude * jnp.sin(angle_plane)], axis=1)


def phase_table(key):
    return jax.random.uniform(jax.random.fold_in(key, 31), (TRANS, PIX), jnp.float32, -3.14159, 3.14159)


def draw_references(key, part):
    return reference_planes(key).astype(jnp.bfloat16)


def draw_phases(key, part):
    return phase_table(key)


def draw_mask(key, part):
    target, forced = pairing(key)
    level_rows = jax.random.randint(jax.random.fold_in(key, 51), (PARTICLES, 1), 1, 5)
    roll_table = jax.random.randint(jax.random.fold_in(key, 52), (PARTICLES, ORIENTS), 0, 8)
    columns = jnp.arange(ORIENTS, dtype=jnp.int32)[None, :]
    allowed = (roll_table < level_rows) | (columns == target[:, None])
    return allowed.astype(jnp.int32)


def draw_particles(key, part):
    target, forced = pairing(key)
    planes = reference_planes(key)[target]
    angle_row = phase_table(key)[0]
    cosine = jnp.cos(angle_row)
    sine_part = jnp.sin(angle_row)
    real_part = planes[:, 0] * cosine + planes[:, 1] * sine_part
    imag_part = planes[:, 1] * cosine - planes[:, 0] * sine_part
    aligned = jnp.stack([real_part, imag_part], axis=1)
    level_rows = jax.random.randint(jax.random.fold_in(key, 43), (PARTICLES, 1, 1), 1, 4).astype(jnp.float32)
    strength = 0.4 + 0.2 * level_rows
    faint_level = 0.002 * (level_rows - 1.0)
    indices = jnp.arange(PARTICLES, dtype=jnp.int32)
    noise_part = jax.random.truncated_normal(jax.random.fold_in(key, 41), -6.0, 6.0, (PARTICLES, 2, PIX), jnp.float32)
    is_aligned = (indices == forced)[:, None, None]
    row_scale = jax.random.uniform(jax.random.fold_in(key, 42), (PARTICLES, 1, 1), jnp.float32, 0.15, 0.3)
    values = jnp.where(is_aligned, strength * aligned + 0.3 * noise_part, faint_level * aligned + row_scale * noise_part)
    return values.astype(jnp.bfloat16)


def place_ends(result, own_key, low, high):
    longest = result.shape.index(max(result.shape))
    spots = []
    for shift in (0, 1):
        where = [jax.random.randint(jax.random.fold_in(own_key, axis), (), 0, length) for axis, length in enumerate(result.shape)]
        where[longest] = (where[longest] + shift) % result.shape[longest]
        spots.append(tuple(where))
    return result.at[spots[0]].set(low).at[spots[1]].set(high)


def setup_inputs(seed: int = 0) -> dict:
    seeds = jax.random.split(jax.random.key(seed), 9)
    particles = draw_particles(jax.random.fold_in(seeds[8], 71), 0)
    references = draw_references(jax.random.fold_in(seeds[8], 71), 0)
    phases = draw_phases(jax.random.fold_in(seeds[8], 71), 0)
    mask = draw_mask(jax.random.fold_in(seeds[8], 71), 0)
    ctf_group = place_ends(jax.random.randint(seeds[4], (PARTICLES,), 0, GROUPS), jax.random.fold_in(seeds[4], 1), 0, GROUPS - 1).astype(jnp.int32)
    ctf_table = jnp.clip(jax.random.uniform(seeds[5], (GROUPS, SHELLS), jnp.float32, 0.1, 1.0), 0.1, 1.0)
    shell_index = place_ends(jax.random.randint(seeds[6], (PIX,), 0, SHELLS), jax.random.fold_in(seeds[6], 1), 0, SHELLS - 1).astype(jnp.int32)
    sigma2 = jnp.clip(jnp.exp(jax.random.uniform(seeds[7], (SHELLS,), jnp.float32, math.log(8.0), math.log(32.0))), 8.0, 32.0)
    return {"particles": particles, "references": references, "phases": phases, "mask": mask, "ctf_group": ctf_group, "ctf_table": ctf_table, "shell_index": shell_index, "sigma2": sigma2}


def shell_sum(values, shell_index):
    moved = jnp.moveaxis(values, -1, 0)
    summed = jax.ops.segment_sum(moved, shell_index, num_segments=SHELLS)
    return jnp.moveaxis(summed, 0, -1)


def make_image(planes, ctf_pix, angle_row):
    cosine = jnp.cos(angle_row)
    sine_part = jnp.sin(angle_row)
    real_part = planes[:, 0]
    imag_part = planes[:, 1]
    shifted = jnp.stack([real_part * cosine - imag_part * sine_part, real_part * sine_part + imag_part * cosine], axis=1)
    rounded = lax.optimization_barrier((ctf_pix[:, None, :] * shifted).astype(jnp.bfloat16))
    return rounded.astype(jnp.float32)


def reference(particles, references, phases, mask, ctf_group, ctf_table, shell_index, sigma2):
    highest = lax.Precision.HIGHEST
    ctf_rows = ctf_table[ctf_group]
    ctf_pix = ctf_rows[:, shell_index]
    sigma_pix = sigma2[shell_index]
    refs_wide = references.astype(jnp.float32)
    weighted = lax.optimization_barrier((refs_wide / sigma_pix).astype(jnp.bfloat16)).astype(jnp.float32)
    ref_norm = shell_sum(jnp.sum(refs_wide * refs_wide, axis=1), shell_index)
    energy = ref_norm / sigma2
    ctf_square = ctf_rows * ctf_rows
    quadratic = 0.5 * jnp.dot(ctf_square, energy.T, precision=highest)
    planes = particles.astype(jnp.float32)

    def score_one(index):
        images = make_image(planes, ctf_pix, phases[index])
        return jnp.einsum("pcx,ocx->po", images, weighted, precision=highest) - quadratic

    stacked = lax.map(score_one, jnp.arange(TRANS))
    scores = jnp.transpose(stacked, (1, 0, 2))
    scores = jnp.where((mask == 1)[:, None, :], scores, -1e30)
    peak = jnp.max(scores, axis=(1, 2), keepdims=True)
    exponent = jnp.exp(scores - peak)
    posterior = exponent / jnp.sum(exponent, axis=(1, 2), keepdims=True)
    post_wide = lax.optimization_barrier(posterior.astype(jnp.bfloat16)).astype(jnp.float32)

    def add_block(running, index):
        images = make_image(planes, ctf_pix, phases[index])
        return running + jnp.einsum("po,pcx->ocx", post_wide[:, index, :], images, precision=highest), None

    image_sums, unused = lax.scan(add_block, jnp.zeros((ORIENTS, 2, PIX), jnp.float32), jnp.arange(TRANS))
    ctf_weights = jnp.dot(jnp.sum(posterior, axis=1).T, ctf_square, precision=highest)
    part_norm = shell_sum(jnp.sum(planes * planes, axis=1), shell_index)
    term_one = jnp.sum(part_norm * jnp.sum(posterior, axis=(1, 2))[:, None], axis=0)
    term_two = -2.0 * shell_sum(jnp.sum(image_sums * refs_wide, axis=(0, 1)), shell_index)
    term_three = jnp.sum(ctf_weights * ref_norm, axis=0)
    shell_noise = (term_one + term_two + term_three) / (PARTICLES * PIX / SHELLS)
    return (posterior, image_sums, ctf_weights, shell_noise)
```

```python
import functools

import jax
import jax.numpy as jnp
from jax import lax
from jax.experimental import pallas as pl
from jax.experimental.pallas import tpu as pltpu
from jax.sharding import PartitionSpec as P

MESH_ID = pl.DeviceIdType.MESH


def _exchange_kernel(axis, n, width, x_ref, o_ref, held, send_sem, recv_sem):
    me = lax.axis_index(axis)
    barrier = pltpu.get_barrier_semaphore()

    def greet(k, carry):
        peer = lax.rem(me + k, n)
        pl.semaphore_signal(barrier, inc=1, device_id={axis: peer}, device_id_type=MESH_ID)
        return carry

    lax.fori_loop(1, n, greet, 0)
    pl.semaphore_wait(barrier, n - 1)

    def source(peer):
        if width is None:
            return x_ref
        return x_ref.at[:, pl.ds(pl.multiple_of(peer * width, width), width)]

    def copy(k):
        peer = lax.rem(me + k, n)
        return pltpu.make_async_remote_copy(
            src_ref=source(peer),
            dst_ref=held.at[me],
            send_sem=send_sem.at[k],
            recv_sem=recv_sem.at[k],
            device_id={axis: peer},
            device_id_type=MESH_ID,
        )

    def start(k, carry):
        copy(k).start()
        return carry

    lax.fori_loop(1, n, start, 0)
    if width is None:
        held[me] = x_ref[...]
    else:
        held[me] = x_ref[:, pl.ds(pl.multiple_of(me * width, width), width)]

    def finish(k, carry):
        copy(k).wait()
        return carry

    lax.fori_loop(1, n, finish, 0)
    o_ref[...] = held[...]


def exchange(x, axis, n, collective_id, width=None):
    block = x.shape if width is None else (x.shape[0], width)
    gathered = (n,) + block
    return pl.pallas_call(
        functools.partial(_exchange_kernel, axis, n, width),
        out_shape=jax.ShapeDtypeStruct(gathered, x.dtype),
        in_specs=[pl.BlockSpec(memory_space=pltpu.VMEM)],
        out_specs=pl.BlockSpec(memory_space=pltpu.VMEM),
        scratch_shapes=[
            pltpu.VMEM(gathered, x.dtype),
            pltpu.SemaphoreType.DMA((n,)),
            pltpu.SemaphoreType.DMA((n,)),
        ],
        compiler_params=pltpu.CompilerParams(collective_id=collective_id, has_side_effects=True),
    )(x)


def make_images(planes, ctf_pix, cosine, sine_part):
    real_part = planes[:, 0][:, None, :]
    imag_part = planes[:, 1][:, None, :]
    shifted_real = real_part * cosine[None] - imag_part * sine_part[None]
    shifted_imag = real_part * sine_part[None] + imag_part * cosine[None]
    factor = ctf_pix[:, None, :]
    return jnp.stack([factor * shifted_real, factor * shifted_imag], axis=2).astype(jnp.bfloat16)


def pad_rows(rows, lanes):
    r, c = rows.shape
    height = -(-r // 8) * 8
    return jnp.pad(rows, ((0, height - r), (0, lanes - c)))


def on_device(particles, references, phases, mask, ctf_group, ctf_table, shell_index, sigma2):
    highest = lax.Precision.HIGHEST
    part_dev = particles.shape[0]
    ori_dev = references.shape[0]
    pixels = shell_index.shape[0]
    shells = ctf_table.shape[1]
    trans_count = phases.shape[0]
    dom_size = lax.axis_size("dom")
    orient_size = lax.axis_size("orient")
    width = pixels // dom_size
    dom_index = lax.axis_index("dom")

    columns = exchange(particles.reshape(part_dev * 2, pixels), "dom", dom_size, 0, width=width)

    shell_pick = (shell_index[:, None] == jnp.arange(shells, dtype=jnp.int32)[None, :]).astype(
        jnp.float32
    )
    group_pick = (
        ctf_group[:, None] == jnp.arange(ctf_table.shape[0], dtype=jnp.int32)[None, :]
    ).astype(jnp.float32)
    ctf_all = jnp.dot(group_pick, ctf_table, precision=highest)
    ctf_rows = lax.dynamic_slice_in_dim(ctf_all, dom_index * part_dev, part_dev, 0)
    ctf_pix = jnp.dot(ctf_rows, shell_pick.T, precision=highest)
    sigma_pix = jnp.dot(shell_pick, sigma2, precision=highest)
    refs_wide = references.astype(jnp.float32)
    weighted = (refs_wide / sigma_pix).astype(jnp.bfloat16)
    ref_norm = jnp.dot(jnp.sum(refs_wide * refs_wide, axis=1), shell_pick, precision=highest)
    energy = ref_norm / sigma2
    ctf_square = ctf_rows * ctf_rows
    quadratic = 0.5 * jnp.dot(ctf_square, energy.T, precision=highest)
    planes = particles.astype(jnp.float32)
    cosines = jnp.cos(phases)
    sine_rows = jnp.sin(phases)

    images = make_images(planes, ctf_pix, cosines, sine_rows)
    cross = jnp.einsum("itpk,jpk->itj", images, weighted, preferred_element_type=jnp.float32)
    scores = cross - quadratic[:, None, :]
    scores = jnp.where((mask == 1)[:, None, :], scores, -1e30)
    local_peak = jnp.max(scores, axis=(1, 2))
    local_total = jnp.sum(jnp.exp(scores - local_peak[:, None, None]), axis=(1, 2))

    stats = exchange(pad_rows(jnp.stack([local_peak, local_total]), 128), "orient", orient_size, 1)
    peaks = stats[:, 0, :part_dev]
    totals = stats[:, 1, :part_dev]
    peak = jnp.max(peaks, axis=0)
    total = jnp.sum(totals * jnp.exp(peaks - peak[None, :]), axis=0)
    posterior = jnp.exp(scores - peak[:, None, None]) / total[:, None, None]
    post_half = posterior.astype(jnp.bfloat16)

    weight_rows = jnp.sum(posterior, axis=1)
    ctf_part = jnp.dot(weight_rows.T, ctf_square, precision=highest)
    part_norm = jnp.dot(jnp.sum(planes * planes, axis=1), shell_pick, precision=highest)
    term_one = jnp.sum(part_norm * jnp.sum(weight_rows, axis=1)[:, None], axis=0)
    term_three = jnp.sum(ctf_part * ref_norm, axis=0)
    local_sums = jnp.einsum("itj,itpk->jpk", post_half, images, preferred_element_type=jnp.float32)
    term_two = -2.0 * jnp.dot(jnp.sum(local_sums * refs_wide, axis=(0, 1)), shell_pick, precision=highest)
    terms = term_one + term_two + term_three

    lanes = trans_count * ori_dev
    post_rows = posterior.reshape(part_dev, lanes)
    packed = jnp.concatenate([post_rows, jnp.pad(terms, (0, lanes - shells))[None]], axis=0)
    packed = pad_rows(packed, lanes)
    gathered = exchange(packed, "dom", dom_size, 2)
    post_all = gathered[:, :part_dev, :].reshape(dom_size * part_dev, trans_count, ori_dev)
    dom_terms = jnp.sum(gathered[:, part_dev, :shells], axis=0)

    orient_terms = exchange(pad_rows(dom_terms[None], 128), "orient", orient_size, 3)
    shell_total = jnp.sum(orient_terms[:, 0, :shells], axis=0)

    ctf_weights = jnp.dot(jnp.sum(post_all, axis=1).T, ctf_all * ctf_all, precision=highest)

    start_pix = dom_index * width
    pick_cols = lax.dynamic_slice_in_dim(shell_pick, start_pix, width, 0)
    ctf_cols = jnp.dot(ctf_all, pick_cols.T, precision=highest)
    cos_cols = lax.dynamic_slice_in_dim(cosines, start_pix, width, 1)
    sin_cols = lax.dynamic_slice_in_dim(sine_rows, start_pix, width, 1)
    col_planes = columns.reshape(dom_size * part_dev, 2, width).astype(jnp.float32)
    col_images = make_images(col_planes, ctf_cols, cos_cols, sin_cols)
    image_sums = jnp.einsum(
        "itj,itpk->jpk", post_all.astype(jnp.bfloat16), col_images, preferred_element_type=jnp.float32
    )

    divisor = part_dev * dom_size * pixels / shells
    return (posterior, image_sums, ctf_weights, shell_total / divisor)


def solution(mesh):
    return jax.shard_map(
        on_device,
        mesh=mesh,
        in_specs=(
            P("dom", None, None),
            P("orient", None, None),
            P(),
            P("dom", "orient"),
            P(),
            P(),
            P(),
            P(),
        ),
        out_specs=(P("dom", None, "orient"), P("orient", None, "dom"), P("orient", None), P()),
        check_vma=False,
    )
```

```python
import functools

import jax
import jax.numpy as jnp
from jax import lax
from jax.experimental import pallas as pl
from jax.experimental.pallas import tpu as pltpu
from jax.sharding import PartitionSpec as P

MESH_ID = pl.DeviceIdType.MESH


def _exchange_kernel(axis, n, widths, *refs):
    count = len(widths)
    x_refs = refs[:count]
    o_refs = refs[count : 2 * count]
    held = refs[2 * count : 3 * count]
    send_sem, recv_sem = refs[3 * count :]
    me = lax.axis_index(axis)
    barrier = pltpu.get_barrier_semaphore()

    def greet(k, carry):
        peer = lax.rem(me + k, n)
        pl.semaphore_signal(barrier, inc=1, device_id={axis: peer}, device_id_type=MESH_ID)
        return carry

    lax.fori_loop(1, n, greet, 0)
    pl.semaphore_wait(barrier, n - 1)

    def part(index, peer):
        width = widths[index]
        if width is None:
            return x_refs[index]
        return x_refs[index].at[:, pl.ds(pl.multiple_of(peer * width, width), width)]

    def copy(index, k):
        peer = lax.rem(me + k, n)
        return pltpu.make_async_remote_copy(
            src_ref=part(index, peer),
            dst_ref=held[index].at[me],
            send_sem=send_sem.at[index, k],
            recv_sem=recv_sem.at[index, k],
            device_id={axis: peer},
            device_id_type=MESH_ID,
        )

    def start(k, carry):
        for index in range(count):
            copy(index, k).start()
        return carry

    lax.fori_loop(1, n, start, 0)
    for index in range(count):
        held[index][me] = part(index, me)[...]

    def finish(k, carry):
        for index in range(count):
            copy(index, k).wait()
        return carry

    lax.fori_loop(1, n, finish, 0)
    for index in range(count):
        o_refs[index][...] = held[index][...]


def exchange(payloads, axis, n, collective_id):
    widths = tuple(width for _, width in payloads)
    shapes = []
    for x, width in payloads:
        block = x.shape if width is None else (x.shape[0], width)
        shapes.append(jax.ShapeDtypeStruct((n,) + block, x.dtype))
    count = len(payloads)
    vmem = pl.BlockSpec(memory_space=pltpu.VMEM)
    return pl.pallas_call(
        functools.partial(_exchange_kernel, axis, n, widths),
        out_shape=tuple(shapes),
        in_specs=[vmem] * count,
        out_specs=tuple([vmem] * count),
        scratch_shapes=[pltpu.VMEM(shape.shape, shape.dtype) for shape in shapes]
        + [pltpu.SemaphoreType.DMA((count, n)), pltpu.SemaphoreType.DMA((count, n))],
        compiler_params=pltpu.CompilerParams(collective_id=collective_id, has_side_effects=True),
    )(*[x for x, _ in payloads])


def make_images(planes, ctf_pix, cosine, sine_part):
    real_part = planes[:, 0][:, None, :]
    imag_part = planes[:, 1][:, None, :]
    shifted_real = real_part * cosine[None] - imag_part * sine_part[None]
    shifted_imag = real_part * sine_part[None] + imag_part * cosine[None]
    factor = ctf_pix[:, None, :]
    return jnp.stack([factor * shifted_real, factor * shifted_imag], axis=2).astype(jnp.bfloat16)


def pad_rows(rows, lanes):
    r, c = rows.shape
    height = -(-r // 8) * 8
    return jnp.pad(rows, ((0, height - r), (0, lanes - c)))


def on_device(particles, references, phases, mask, ctf_group, ctf_table, shell_index, sigma2):
    highest = lax.Precision.HIGHEST
    part_dev = particles.shape[0]
    ori_dev = references.shape[0]
    pixels = shell_index.shape[0]
    shells = ctf_table.shape[1]
    trans_count = phases.shape[0]
    dom_size = lax.axis_size("dom")
    orient_size = lax.axis_size("orient")
    width = pixels // dom_size
    dom_index = lax.axis_index("dom")

    shell_pick = (shell_index[:, None] == jnp.arange(shells, dtype=jnp.int32)[None, :]).astype(
        jnp.float32
    )
    group_pick = (
        ctf_group[:, None] == jnp.arange(ctf_table.shape[0], dtype=jnp.int32)[None, :]
    ).astype(jnp.float32)
    ctf_all = jnp.dot(group_pick, ctf_table, precision=highest)
    ctf_rows = lax.dynamic_slice_in_dim(ctf_all, dom_index * part_dev, part_dev, 0)
    ctf_pix = jnp.dot(ctf_rows, shell_pick.T, precision=highest)
    sigma_pix = jnp.dot(shell_pick, sigma2, precision=highest)
    refs_wide = references.astype(jnp.float32)
    weighted = (refs_wide / sigma_pix).astype(jnp.bfloat16)
    ref_norm = jnp.dot(jnp.sum(refs_wide * refs_wide, axis=1), shell_pick, precision=highest)
    energy = ref_norm / sigma2
    ctf_square = ctf_rows * ctf_rows
    quadratic = 0.5 * jnp.dot(ctf_square, energy.T, precision=highest)
    planes = particles.astype(jnp.float32)
    cosines = jnp.cos(phases)
    sine_rows = jnp.sin(phases)

    images = make_images(planes, ctf_pix, cosines, sine_rows)
    cross = jnp.einsum("itpk,jpk->itj", images, weighted, preferred_element_type=jnp.float32)
    scores = cross - quadratic[:, None, :]
    scores = jnp.where((mask == 1)[:, None, :], scores, -1e30)
    local_peak = jnp.max(scores, axis=(1, 2))
    local_total = jnp.sum(jnp.exp(scores - local_peak[:, None, None]), axis=(1, 2))

    (stats,) = exchange([(pad_rows(jnp.stack([local_peak, local_total]), 128), None)], "orient", orient_size, 1)
    peaks = stats[:, 0, :part_dev]
    totals = stats[:, 1, :part_dev]
    peak = jnp.max(peaks, axis=0)
    total = jnp.sum(totals * jnp.exp(peaks - peak[None, :]), axis=0)
    posterior = jnp.exp(scores - peak[:, None, None]) / total[:, None, None]
    post_half = posterior.astype(jnp.bfloat16)

    weight_rows = jnp.sum(posterior, axis=1)
    ctf_part = jnp.dot(weight_rows.T, ctf_square, precision=highest)
    part_norm = jnp.dot(jnp.sum(planes * planes, axis=1), shell_pick, precision=highest)
    term_one = jnp.sum(part_norm * jnp.sum(weight_rows, axis=1)[:, None], axis=0)
    term_three = jnp.sum(ctf_part * ref_norm, axis=0)
    local_sums = jnp.einsum("itj,itpk->jpk", post_half, images, preferred_element_type=jnp.float32)
    term_two = -2.0 * jnp.dot(jnp.sum(local_sums * refs_wide, axis=(0, 1)), shell_pick, precision=highest)
    terms = term_one + term_two + term_three

    lanes = trans_count * ori_dev
    post_rows = posterior.reshape(part_dev, lanes)
    packed = jnp.concatenate([post_rows, jnp.pad(terms, (0, lanes - shells))[None]], axis=0)
    packed = pad_rows(packed, lanes)
    gathered, columns = exchange(
        [(packed, None), (particles.reshape(part_dev * 2, pixels), width)], "dom", dom_size, 2
    )
    post_all = gathered[:, :part_dev, :].reshape(dom_size * part_dev, trans_count, ori_dev)
    dom_terms = jnp.sum(gathered[:, part_dev, :shells], axis=0)

    (orient_terms,) = exchange([(pad_rows(dom_terms[None], 128), None)], "orient", orient_size, 3)
    shell_total = jnp.sum(orient_terms[:, 0, :shells], axis=0)

    ctf_weights = jnp.dot(jnp.sum(post_all, axis=1).T, ctf_all * ctf_all, precision=highest)

    start_pix = dom_index * width
    pick_cols = lax.dynamic_slice_in_dim(shell_pick, start_pix, width, 0)
    ctf_cols = jnp.dot(ctf_all, pick_cols.T, precision=highest)
    cos_cols = lax.dynamic_slice_in_dim(cosines, start_pix, width, 1)
    sin_cols = lax.dynamic_slice_in_dim(sine_rows, start_pix, width, 1)
    col_planes = columns.reshape(dom_size * part_dev, 2, width).astype(jnp.float32)
    col_images = make_images(col_planes, ctf_cols, cos_cols, sin_cols)
    image_sums = jnp.einsum(
        "itj,itpk->jpk", post_all.astype(jnp.bfloat16), col_images, preferred_element_type=jnp.float32
    )

    divisor = part_dev * dom_size * pixels / shells
    return (posterior, image_sums, ctf_weights, shell_total / divisor)


def solution(mesh):
    return jax.shard_map(
        on_device,
        mesh=mesh,
        in_specs=(
            P("dom", None, None),
            P("orient", None, None),
            P(),
            P("dom", "orient"),
            P(),
            P(),
            P(),
            P(),
        ),
        out_specs=(P("dom", None, "orient"), P("orient", None, "dom"), P("orient", None), P()),
        check_vma=False,
    )
```

```python
import functools

import jax
import jax.numpy as jnp
from jax import lax
from jax.experimental import pallas as pl
from jax.experimental.pallas import tpu as pltpu
from jax.sharding import PartitionSpec as P

MESH_ID = pl.DeviceIdType.MESH


def _exchange_kernel(axis, n, widths, *refs):
    count = len(widths)
    x_refs = refs[:count]
    o_refs = refs[count : 2 * count]
    held = refs[2 * count : 3 * count]
    send_sem, recv_sem = refs[3 * count :]
    me = lax.axis_index(axis)
    barrier = pltpu.get_barrier_semaphore()

    def greet(k, carry):
        peer = lax.rem(me + k, n)
        pl.semaphore_signal(barrier, inc=1, device_id={axis: peer}, device_id_type=MESH_ID)
        return carry

    lax.fori_loop(1, n, greet, 0)
    pl.semaphore_wait(barrier, n - 1)

    def part(index, peer):
        width = widths[index]
        if width is None:
            return x_refs[index]
        return x_refs[index].at[:, pl.ds(pl.multiple_of(peer * width, width), width)]

    def copy(index, k):
        peer = lax.rem(me + k, n)
        return pltpu.make_async_remote_copy(
            src_ref=part(index, peer),
            dst_ref=held[index].at[me],
            send_sem=send_sem.at[index, k],
            recv_sem=recv_sem.at[index, k],
            device_id={axis: peer},
            device_id_type=MESH_ID,
        )

    def start(k, carry):
        for index in range(count):
            copy(index, k).start()
        return carry

    lax.fori_loop(1, n, start, 0)
    for index in range(count):
        held[index][me] = part(index, me)[...]

    def finish(k, carry):
        for index in range(count):
            copy(index, k).wait()
        return carry

    lax.fori_loop(1, n, finish, 0)
    for index in range(count):
        o_refs[index][...] = held[index][...]


def exchange(payloads, axis, n, collective_id):
    widths = tuple(width for _, width in payloads)
    shapes = []
    for x, width in payloads:
        block = x.shape if width is None else (x.shape[0], width)
        shapes.append(jax.ShapeDtypeStruct((n,) + block, x.dtype))
    count = len(payloads)
    vmem = pl.BlockSpec(memory_space=pltpu.VMEM)
    return pl.pallas_call(
        functools.partial(_exchange_kernel, axis, n, widths),
        out_shape=tuple(shapes),
        in_specs=[vmem] * count,
        out_specs=tuple([vmem] * count),
        scratch_shapes=[pltpu.VMEM(shape.shape, shape.dtype) for shape in shapes]
        + [pltpu.SemaphoreType.DMA((count, n)), pltpu.SemaphoreType.DMA((count, n))],
        compiler_params=pltpu.CompilerParams(collective_id=collective_id, has_side_effects=True),
    )(*[x for x, _ in payloads])


def make_images(planes, ctf_pix, cosine, sine_part):
    real_part = planes[:, 0][:, None, :]
    imag_part = planes[:, 1][:, None, :]
    shifted_real = real_part * cosine[None] - imag_part * sine_part[None]
    shifted_imag = real_part * sine_part[None] + imag_part * cosine[None]
    factor = ctf_pix[:, None, :]
    return jnp.stack([factor * shifted_real, factor * shifted_imag], axis=2).astype(jnp.bfloat16)


def pad_rows(rows, lanes):
    r, c = rows.shape
    height = -(-r // 8) * 8
    return jnp.pad(rows, ((0, height - r), (0, lanes - c)))


def on_device(particles, references, phases, mask, ctf_group, ctf_table, shell_index, sigma2):
    highest = lax.Precision.HIGHEST
    part_dev = particles.shape[0]
    ori_dev = references.shape[0]
    pixels = shell_index.shape[0]
    shells = ctf_table.shape[1]
    trans_count = phases.shape[0]
    dom_size = lax.axis_size("dom")
    orient_size = lax.axis_size("orient")
    width = pixels // dom_size
    dom_index = lax.axis_index("dom")

    shell_pick = (shell_index[:, None] == jnp.arange(shells, dtype=jnp.int32)[None, :]).astype(
        jnp.float32
    )
    group_pick = (
        ctf_group[:, None] == jnp.arange(ctf_table.shape[0], dtype=jnp.int32)[None, :]
    ).astype(jnp.float32)
    ctf_all = jnp.dot(group_pick, ctf_table, precision=highest)
    ctf_rows = lax.dynamic_slice_in_dim(ctf_all, dom_index * part_dev, part_dev, 0)
    ctf_pix = jnp.dot(ctf_rows, shell_pick.T, precision=highest)
    sigma_pix = jnp.dot(shell_pick, sigma2, precision=highest)
    refs_wide = references.astype(jnp.float32)
    weighted = (refs_wide / sigma_pix).astype(jnp.bfloat16)
    ref_norm = jnp.dot(jnp.sum(refs_wide * refs_wide, axis=1), shell_pick, precision=highest)
    energy = ref_norm / sigma2
    ctf_square = ctf_rows * ctf_rows
    quadratic = 0.5 * jnp.dot(ctf_square, energy.T, precision=highest)
    planes = particles.astype(jnp.float32)
    cosines = jnp.cos(phases)
    sine_rows = jnp.sin(phases)

    images = make_images(planes, ctf_pix, cosines, sine_rows)
    cross = jnp.einsum("itpk,jpk->itj", images, weighted, preferred_element_type=jnp.float32)
    scores = cross - quadratic[:, None, :]
    scores = jnp.where((mask == 1)[:, None, :], scores, -1e30)
    local_peak = jnp.max(scores, axis=(1, 2))
    local_total = jnp.sum(jnp.exp(scores - local_peak[:, None, None]), axis=(1, 2))

    (stats,) = exchange([(pad_rows(jnp.stack([local_peak, local_total]), 128), None)], "orient", orient_size, 1)
    peaks = stats[:, 0, :part_dev]
    totals = stats[:, 1, :part_dev]
    peak = jnp.max(peaks, axis=0)
    total = jnp.sum(totals * jnp.exp(peaks - peak[None, :]), axis=0)
    posterior = jnp.exp(scores - peak[:, None, None]) / total[:, None, None]
    post_half = posterior.astype(jnp.bfloat16)

    weight_rows = jnp.sum(posterior, axis=1)
    ctf_part = jnp.dot(weight_rows.T, ctf_square, precision=highest)
    part_norm = jnp.dot(jnp.sum(planes * planes, axis=1), shell_pick, precision=highest)
    term_one = jnp.sum(part_norm * jnp.sum(weight_rows, axis=1)[:, None], axis=0)
    term_three = jnp.sum(ctf_part * ref_norm, axis=0)
    local_sums = jnp.einsum("itj,itpk->jpk", post_half, images, preferred_element_type=jnp.float32)
    term_two = -2.0 * jnp.dot(jnp.sum(local_sums * refs_wide, axis=(0, 1)), shell_pick, precision=highest)
    terms = term_one + term_two + term_three

    term_cols = -(-shells // part_dev)
    term_rows = jnp.pad(terms, (0, term_cols * part_dev - shells)).reshape(part_dev, term_cols)
    small = jnp.concatenate([weight_rows, term_rows], axis=1)
    small = jnp.pad(small, ((0, 0), (0, -(-small.shape[1] // 128) * 128 - small.shape[1])))
    half_rows = post_half.reshape(-1, 128)
    half_all, small_all, columns = exchange(
        [(half_rows, None), (small, None), (particles.reshape(part_dev * 2, pixels), width)],
        "dom",
        dom_size,
        2,
    )
    post_all = half_all.reshape(dom_size * part_dev, trans_count, ori_dev)
    weight_all = small_all[:, :, :ori_dev].reshape(dom_size * part_dev, ori_dev)
    dom_terms = jnp.sum(
        small_all[:, :, ori_dev : ori_dev + term_cols].reshape(dom_size, part_dev * term_cols)[:, :shells],
        axis=0,
    )

    (orient_terms,) = exchange([(pad_rows(dom_terms[None], 128), None)], "orient", orient_size, 3)
    shell_total = jnp.sum(orient_terms[:, 0, :shells], axis=0)

    ctf_weights = jnp.dot(weight_all.T, ctf_all * ctf_all, precision=highest)

    start_pix = dom_index * width
    pick_cols = lax.dynamic_slice_in_dim(shell_pick, start_pix, width, 0)
    ctf_cols = jnp.dot(ctf_all, pick_cols.T, precision=highest)
    cos_cols = lax.dynamic_slice_in_dim(cosines, start_pix, width, 1)
    sin_cols = lax.dynamic_slice_in_dim(sine_rows, start_pix, width, 1)
    col_planes = columns.reshape(dom_size * part_dev, 2, width).astype(jnp.float32)
    col_images = make_images(col_planes, ctf_cols, cos_cols, sin_cols)
    image_sums = jnp.einsum(
        "itj,itpk->jpk", post_all, col_images, preferred_element_type=jnp.float32
    )

    divisor = part_dev * dom_size * pixels / shells
    return (posterior, image_sums, ctf_weights, shell_total / divisor)


def solution(mesh):
    return jax.shard_map(
        on_device,
        mesh=mesh,
        in_specs=(
            P("dom", None, None),
            P("orient", None, None),
            P(),
            P("dom", "orient"),
            P(),
            P(),
            P(),
            P(),
        ),
        out_specs=(P("dom", None, "orient"), P("orient", None, "dom"), P("orient", None), P()),
        check_vma=False,
    )
```

```python
import functools

import jax
import jax.numpy as jnp
from jax import lax
from jax.experimental import pallas as pl
from jax.experimental.pallas import tpu as pltpu
from jax.sharding import PartitionSpec as P

MESH_ID = pl.DeviceIdType.MESH


def _exchange_kernel(axis, n, widths, *refs):
    count = len(widths)
    x_refs = refs[:count]
    o_refs = refs[count : 2 * count]
    held = refs[2 * count : 3 * count]
    send_sem, recv_sem = refs[3 * count :]
    me = lax.axis_index(axis)
    barrier = pltpu.get_barrier_semaphore()

    def greet(k, carry):
        peer = lax.rem(me + k, n)
        pl.semaphore_signal(barrier, inc=1, device_id={axis: peer}, device_id_type=MESH_ID)
        return carry

    lax.fori_loop(1, n, greet, 0)
    pl.semaphore_wait(barrier, n - 1)

    def part(index, peer):
        width = widths[index]
        if width is None:
            return x_refs[index]
        return x_refs[index].at[:, pl.ds(pl.multiple_of(peer * width, width), width)]

    def copy(index, k):
        peer = lax.rem(me + k, n)
        return pltpu.make_async_remote_copy(
            src_ref=part(index, peer),
            dst_ref=held[index].at[me],
            send_sem=send_sem.at[index, k],
            recv_sem=recv_sem.at[index, k],
            device_id={axis: peer},
            device_id_type=MESH_ID,
        )

    def start(k, carry):
        for index in range(count):
            copy(index, k).start()
        return carry

    lax.fori_loop(1, n, start, 0)
    for index in range(count):
        held[index][me] = part(index, me)[...]

    def finish(k, carry):
        for index in range(count):
            copy(index, k).wait()
        return carry

    lax.fori_loop(1, n, finish, 0)
    for index in range(count):
        o_refs[index][...] = held[index][...]


def exchange(payloads, axis, n, collective_id):
    widths = tuple(width for _, width in payloads)
    shapes = []
    for x, width in payloads:
        block = x.shape if width is None else (x.shape[0], width)
        shapes.append(jax.ShapeDtypeStruct((n,) + block, x.dtype))
    count = len(payloads)
    vmem = pl.BlockSpec(memory_space=pltpu.VMEM)
    return pl.pallas_call(
        functools.partial(_exchange_kernel, axis, n, widths),
        out_shape=tuple(shapes),
        in_specs=[vmem] * count,
        out_specs=tuple([vmem] * count),
        scratch_shapes=[pltpu.VMEM(shape.shape, shape.dtype) for shape in shapes]
        + [pltpu.SemaphoreType.DMA((count, n)), pltpu.SemaphoreType.DMA((count, n))],
        compiler_params=pltpu.CompilerParams(collective_id=collective_id, has_side_effects=True),
    )(*[x for x, _ in payloads])


def _spread_kernel(dom_n, orient_n, width, half_ref, small_ref, part_ref,
                   half_out, small_out, part_out, terms_out,
                   half_held, small_held, part_held, summed, terms_held,
                   send_sem, recv_sem, orient_send, orient_recv):
    me = lax.axis_index("dom")
    mine = lax.axis_index("orient")
    barrier = pltpu.get_barrier_semaphore()

    def greet_dom(k, carry):
        peer = lax.rem(me + k, dom_n)
        pl.semaphore_signal(barrier, inc=1, device_id={"dom": peer}, device_id_type=MESH_ID)
        return carry

    def greet_orient(k, carry):
        peer = lax.rem(mine + k, orient_n)
        pl.semaphore_signal(barrier, inc=1, device_id={"orient": peer}, device_id_type=MESH_ID)
        return carry

    lax.fori_loop(1, dom_n, greet_dom, 0)
    lax.fori_loop(1, orient_n, greet_orient, 0)
    pl.semaphore_wait(barrier, dom_n + orient_n - 2)

    def columns(peer):
        return part_ref.at[:, pl.ds(pl.multiple_of(peer * width, width), width)]

    sources = (lambda peer: half_ref, lambda peer: small_ref, columns)
    held = (half_held, small_held, part_held)

    def copy(index, k):
        peer = lax.rem(me + k, dom_n)
        return pltpu.make_async_remote_copy(
            src_ref=sources[index](peer),
            dst_ref=held[index].at[me],
            send_sem=send_sem.at[index, k],
            recv_sem=recv_sem.at[index, k],
            device_id={"dom": peer},
            device_id_type=MESH_ID,
        )

    def start(k, carry):
        for index in (1, 0, 2):
            copy(index, k).start()
        return carry

    lax.fori_loop(1, dom_n, start, 0)
    for index in range(3):
        held[index][me] = sources[index](me)[...]

    def finish(index):
        def body(k, carry):
            copy(index, k).wait()
            return carry

        lax.fori_loop(1, dom_n, body, 0)

    finish(1)
    summed[...] = jnp.sum(small_held[...], axis=0)
    finish(0)

    def orient_copy(k):
        peer = lax.rem(mine + k, orient_n)
        return pltpu.make_async_remote_copy(
            src_ref=summed,
            dst_ref=terms_held.at[mine],
            send_sem=orient_send.at[k],
            recv_sem=orient_recv.at[k],
            device_id={"orient": peer},
            device_id_type=MESH_ID,
        )

    def orient_start(k, carry):
        orient_copy(k).start()
        return carry

    lax.fori_loop(1, orient_n, orient_start, 0)
    terms_held[mine] = summed[...]
    finish(2)

    def orient_finish(k, carry):
        orient_copy(k).wait()
        return carry

    lax.fori_loop(1, orient_n, orient_finish, 0)
    half_out[...] = half_held[...]
    small_out[...] = small_held[...]
    part_out[...] = part_held[...]
    terms_out[...] = terms_held[...]


def spread(half_rows, small, part_rows, dom_n, orient_n, width, collective_id):
    shapes = (
        jax.ShapeDtypeStruct((dom_n,) + half_rows.shape, half_rows.dtype),
        jax.ShapeDtypeStruct((dom_n,) + small.shape, small.dtype),
        jax.ShapeDtypeStruct((dom_n, part_rows.shape[0], width), part_rows.dtype),
        jax.ShapeDtypeStruct((orient_n,) + small.shape, small.dtype),
    )
    vmem = pl.BlockSpec(memory_space=pltpu.VMEM)
    return pl.pallas_call(
        functools.partial(_spread_kernel, dom_n, orient_n, width),
        out_shape=shapes,
        in_specs=[vmem] * 3,
        out_specs=(vmem,) * 4,
        scratch_shapes=[
            pltpu.VMEM(shapes[0].shape, shapes[0].dtype),
            pltpu.VMEM(shapes[1].shape, shapes[1].dtype),
            pltpu.VMEM(shapes[2].shape, shapes[2].dtype),
            pltpu.VMEM(small.shape, small.dtype),
            pltpu.VMEM(shapes[3].shape, shapes[3].dtype),
            pltpu.SemaphoreType.DMA((3, dom_n)),
            pltpu.SemaphoreType.DMA((3, dom_n)),
            pltpu.SemaphoreType.DMA((orient_n,)),
            pltpu.SemaphoreType.DMA((orient_n,)),
        ],
        compiler_params=pltpu.CompilerParams(collective_id=collective_id, has_side_effects=True),
    )(half_rows, small, part_rows)


def make_images(planes, ctf_pix, cosine, sine_part):
    real_part = planes[:, 0][:, None, :]
    imag_part = planes[:, 1][:, None, :]
    shifted_real = real_part * cosine[None] - imag_part * sine_part[None]
    shifted_imag = real_part * sine_part[None] + imag_part * cosine[None]
    factor = ctf_pix[:, None, :]
    return jnp.stack([factor * shifted_real, factor * shifted_imag], axis=2).astype(jnp.bfloat16)


def pad_rows(rows, lanes):
    r, c = rows.shape
    height = -(-r // 8) * 8
    return jnp.pad(rows, ((0, height - r), (0, lanes - c)))


def on_device(particles, references, phases, mask, ctf_group, ctf_table, shell_index, sigma2):
    highest = lax.Precision.HIGHEST
    part_dev = particles.shape[0]
    ori_dev = references.shape[0]
    pixels = shell_index.shape[0]
    shells = ctf_table.shape[1]
    trans_count = phases.shape[0]
    dom_size = lax.axis_size("dom")
    orient_size = lax.axis_size("orient")
    width = pixels // dom_size
    dom_index = lax.axis_index("dom")

    shell_pick = (shell_index[:, None] == jnp.arange(shells, dtype=jnp.int32)[None, :]).astype(
        jnp.float32
    )
    group_pick = (
        ctf_group[:, None] == jnp.arange(ctf_table.shape[0], dtype=jnp.int32)[None, :]
    ).astype(jnp.float32)
    ctf_all = jnp.dot(group_pick, ctf_table, precision=highest)
    ctf_rows = lax.dynamic_slice_in_dim(ctf_all, dom_index * part_dev, part_dev, 0)
    ctf_pix = jnp.dot(ctf_rows, shell_pick.T, precision=highest)
    sigma_pix = jnp.dot(shell_pick, sigma2, precision=highest)
    refs_wide = references.astype(jnp.float32)
    weighted = (refs_wide / sigma_pix).astype(jnp.bfloat16)
    ref_norm = jnp.dot(jnp.sum(refs_wide * refs_wide, axis=1), shell_pick, precision=highest)
    energy = ref_norm / sigma2
    ctf_square = ctf_rows * ctf_rows
    quadratic = 0.5 * jnp.dot(ctf_square, energy.T, precision=highest)
    planes = particles.astype(jnp.float32)
    cosines = jnp.cos(phases)
    sine_rows = jnp.sin(phases)

    images = make_images(planes, ctf_pix, cosines, sine_rows)
    cross = jnp.einsum("itpk,jpk->itj", images, weighted, preferred_element_type=jnp.float32)
    scores = cross - quadratic[:, None, :]
    scores = jnp.where((mask == 1)[:, None, :], scores, -1e30)
    local_peak = jnp.max(scores, axis=(1, 2))
    local_total = jnp.sum(jnp.exp(scores - local_peak[:, None, None]), axis=(1, 2))

    (stats,) = exchange([(pad_rows(jnp.stack([local_peak, local_total]), 128), None)], "orient", orient_size, 1)
    peaks = stats[:, 0, :part_dev]
    totals = stats[:, 1, :part_dev]
    peak = jnp.max(peaks, axis=0)
    total = jnp.sum(totals * jnp.exp(peaks - peak[None, :]), axis=0)
    posterior = jnp.exp(scores - peak[:, None, None]) / total[:, None, None]
    post_half = posterior.astype(jnp.bfloat16)

    weight_rows = jnp.sum(posterior, axis=1)
    ctf_part = jnp.dot(weight_rows.T, ctf_square, precision=highest)
    part_norm = jnp.dot(jnp.sum(planes * planes, axis=1), shell_pick, precision=highest)
    term_one = jnp.sum(part_norm * jnp.sum(weight_rows, axis=1)[:, None], axis=0)
    term_three = jnp.sum(ctf_part * ref_norm, axis=0)
    local_sums = jnp.einsum("itj,itpk->jpk", post_half, images, preferred_element_type=jnp.float32)
    term_two = -2.0 * jnp.dot(jnp.sum(local_sums * refs_wide, axis=(0, 1)), shell_pick, precision=highest)
    terms = term_one + term_two + term_three

    term_cols = -(-shells // part_dev)
    term_rows = jnp.pad(terms, (0, term_cols * part_dev - shells)).reshape(part_dev, term_cols)
    small = jnp.concatenate([weight_rows, term_rows], axis=1)
    small = jnp.pad(small, ((0, 0), (0, -(-small.shape[1] // 128) * 128 - small.shape[1])))
    half_rows = post_half.reshape(-1, 128)
    half_all, small_all, columns, orient_small = spread(
        half_rows, small, particles.reshape(part_dev * 2, pixels), dom_size, orient_size, width, 2
    )
    post_all = half_all.reshape(dom_size * part_dev, trans_count, ori_dev)
    weight_all = small_all[:, :, :ori_dev].reshape(dom_size * part_dev, ori_dev)
    shell_total = jnp.sum(
        orient_small[:, :, ori_dev : ori_dev + term_cols].reshape(orient_size, part_dev * term_cols)[:, :shells],
        axis=0,
    )

    ctf_weights = jnp.dot(weight_all.T, ctf_all * ctf_all, precision=highest)

    start_pix = dom_index * width
    pick_cols = lax.dynamic_slice_in_dim(shell_pick, start_pix, width, 0)
    ctf_cols = jnp.dot(ctf_all, pick_cols.T, precision=highest)
    cos_cols = lax.dynamic_slice_in_dim(cosines, start_pix, width, 1)
    sin_cols = lax.dynamic_slice_in_dim(sine_rows, start_pix, width, 1)
    col_planes = columns.reshape(dom_size * part_dev, 2, width).astype(jnp.float32)
    col_images = make_images(col_planes, ctf_cols, cos_cols, sin_cols)
    image_sums = jnp.einsum(
        "itj,itpk->jpk", post_all, col_images, preferred_element_type=jnp.float32
    )

    divisor = part_dev * dom_size * pixels / shells
    return (posterior, image_sums, ctf_weights, shell_total / divisor)


def solution(mesh):
    return jax.shard_map(
        on_device,
        mesh=mesh,
        in_specs=(
            P("dom", None, None),
            P("orient", None, None),
            P(),
            P("dom", "orient"),
            P(),
            P(),
            P(),
            P(),
        ),
        out_specs=(P("dom", None, "orient"), P("orient", None, "dom"), P("orient", None), P()),
        check_vma=False,
    )
```

```python
import functools

import jax
import jax.numpy as jnp
from jax import lax
from jax.experimental import pallas as pl
from jax.experimental.pallas import tpu as pltpu
from jax.sharding import PartitionSpec as P

MESH_ID = pl.DeviceIdType.MESH


def _exchange_kernel(axis, n, widths, *refs):
    count = len(widths)
    x_refs = refs[:count]
    o_refs = refs[count : 2 * count]
    held = refs[2 * count : 3 * count]
    send_sem, recv_sem = refs[3 * count :]
    me = lax.axis_index(axis)
    barrier = pltpu.get_barrier_semaphore()

    def greet(k, carry):
        peer = lax.rem(me + k, n)
        pl.semaphore_signal(barrier, inc=1, device_id={axis: peer}, device_id_type=MESH_ID)
        return carry

    lax.fori_loop(1, n, greet, 0)
    pl.semaphore_wait(barrier, n - 1)

    def part(index, peer):
        width = widths[index]
        if width is None:
            return x_refs[index]
        return x_refs[index].at[:, pl.ds(pl.multiple_of(peer * width, width), width)]

    def copy(index, k):
        peer = lax.rem(me + k, n)
        return pltpu.make_async_remote_copy(
            src_ref=part(index, peer),
            dst_ref=held[index].at[me],
            send_sem=send_sem.at[index, k],
            recv_sem=recv_sem.at[index, k],
            device_id={axis: peer},
            device_id_type=MESH_ID,
        )

    def start(k, carry):
        for index in range(count):
            copy(index, k).start()
        return carry

    lax.fori_loop(1, n, start, 0)
    for index in range(count):
        held[index][me] = part(index, me)[...]

    def finish(k, carry):
        for index in range(count):
            copy(index, k).wait()
        return carry

    lax.fori_loop(1, n, finish, 0)
    for index in range(count):
        o_refs[index][...] = held[index][...]


def exchange(payloads, axis, n, collective_id):
    widths = tuple(width for _, width in payloads)
    shapes = []
    for x, width in payloads:
        block = x.shape if width is None else (x.shape[0], width)
        shapes.append(jax.ShapeDtypeStruct((n,) + block, x.dtype))
    count = len(payloads)
    vmem = pl.BlockSpec(memory_space=pltpu.VMEM)
    return pl.pallas_call(
        functools.partial(_exchange_kernel, axis, n, widths),
        out_shape=tuple(shapes),
        in_specs=[vmem] * count,
        out_specs=tuple([vmem] * count),
        scratch_shapes=[pltpu.VMEM(shape.shape, shape.dtype) for shape in shapes]
        + [pltpu.SemaphoreType.DMA((count, n)), pltpu.SemaphoreType.DMA((count, n))],
        compiler_params=pltpu.CompilerParams(collective_id=collective_id, has_side_effects=True),
    )(*[x for x, _ in payloads])


def _spread_kernel(dom_n, orient_n, width, half_ref, small_ref, part_ref,
                   half_out, small_out, part_out, terms_out,
                   half_held, small_held, part_held, summed, terms_held,
                   send_sem, recv_sem, orient_send, orient_recv):
    me = lax.axis_index("dom")
    mine = lax.axis_index("orient")
    barrier = pltpu.get_barrier_semaphore()

    def greet_dom(k, carry):
        peer = lax.rem(me + k, dom_n)
        pl.semaphore_signal(barrier, inc=1, device_id={"dom": peer}, device_id_type=MESH_ID)
        return carry

    def greet_orient(k, carry):
        peer = lax.rem(mine + k, orient_n)
        pl.semaphore_signal(barrier, inc=1, device_id={"orient": peer}, device_id_type=MESH_ID)
        return carry

    lax.fori_loop(1, dom_n, greet_dom, 0)
    lax.fori_loop(1, orient_n, greet_orient, 0)
    pl.semaphore_wait(barrier, dom_n + orient_n - 2)

    def columns(peer):
        return part_ref.at[:, pl.ds(pl.multiple_of(peer * width, width), width)]

    sources = (lambda peer: half_ref, lambda peer: small_ref, columns)
    held = (half_held, small_held, part_held)

    def copy(index, k):
        peer = lax.rem(me + k, dom_n)
        return pltpu.make_async_remote_copy(
            src_ref=sources[index](peer),
            dst_ref=held[index].at[me],
            send_sem=send_sem.at[index, k],
            recv_sem=recv_sem.at[index, k],
            device_id={"dom": peer},
            device_id_type=MESH_ID,
        )

    def start(k, carry):
        for index in (1, 0, 2):
            copy(index, k).start()
        return carry

    lax.fori_loop(1, dom_n, start, 0)
    for index in range(3):
        held[index][me] = sources[index](me)[...]

    def finish(index):
        def body(k, carry):
            copy(index, k).wait()
            return carry

        lax.fori_loop(1, dom_n, body, 0)

    finish(1)
    summed[...] = jnp.sum(small_held[...], axis=0)
    finish(0)

    def orient_copy(k):
        peer = lax.rem(mine + k, orient_n)
        return pltpu.make_async_remote_copy(
            src_ref=summed,
            dst_ref=terms_held.at[mine],
            send_sem=orient_send.at[k],
            recv_sem=orient_recv.at[k],
            device_id={"orient": peer},
            device_id_type=MESH_ID,
        )

    def orient_start(k, carry):
        orient_copy(k).start()
        return carry

    lax.fori_loop(1, orient_n, orient_start, 0)
    terms_held[mine] = summed[...]
    finish(2)

    def orient_finish(k, carry):
        orient_copy(k).wait()
        return carry

    lax.fori_loop(1, orient_n, orient_finish, 0)
    half_out[...] = half_held[...]
    small_out[...] = small_held[...]
    part_out[...] = part_held[...]
    terms_out[...] = terms_held[...]


def spread(half_rows, small, part_rows, dom_n, orient_n, width, collective_id):
    shapes = (
        jax.ShapeDtypeStruct((dom_n,) + half_rows.shape, half_rows.dtype),
        jax.ShapeDtypeStruct((dom_n,) + small.shape, small.dtype),
        jax.ShapeDtypeStruct((dom_n, part_rows.shape[0], width), part_rows.dtype),
        jax.ShapeDtypeStruct((orient_n,) + small.shape, small.dtype),
    )
    vmem = pl.BlockSpec(memory_space=pltpu.VMEM)
    return pl.pallas_call(
        functools.partial(_spread_kernel, dom_n, orient_n, width),
        out_shape=shapes,
        in_specs=[vmem] * 3,
        out_specs=(vmem,) * 4,
        scratch_shapes=[
            pltpu.VMEM(shapes[0].shape, shapes[0].dtype),
            pltpu.VMEM(shapes[1].shape, shapes[1].dtype),
            pltpu.VMEM(shapes[2].shape, shapes[2].dtype),
            pltpu.VMEM(small.shape, small.dtype),
            pltpu.VMEM(shapes[3].shape, shapes[3].dtype),
            pltpu.SemaphoreType.DMA((3, dom_n)),
            pltpu.SemaphoreType.DMA((3, dom_n)),
            pltpu.SemaphoreType.DMA((orient_n,)),
            pltpu.SemaphoreType.DMA((orient_n,)),
        ],
        compiler_params=pltpu.CompilerParams(collective_id=collective_id, has_side_effects=True),
    )(half_rows, small, part_rows)


def _sums_kernel(post_ref, part_ref, ctf_ref, cos_ref, sin_ref, real_out, imag_out):
    dom_n, rows, width = part_ref.shape
    count = rows // 2
    trans = cos_ref.shape[0]
    cosine = cos_ref[...][None]
    sine_part = sin_ref[...][None]

    def body(d, carry):
        acc_real, acc_imag = carry
        block = part_ref[d].astype(jnp.float32)
        real = block[:count][:, None, :]
        imag = block[count:][:, None, :]
        factor = ctf_ref[d][:, None, :]
        image_real = (factor * (real * cosine - imag * sine_part)).astype(jnp.bfloat16)
        image_imag = (factor * (real * sine_part + imag * cosine)).astype(jnp.bfloat16)
        weights = post_ref[d]
        acc_real = acc_real + jnp.dot(
            weights, image_real.reshape(count * trans, width), preferred_element_type=jnp.float32
        )
        acc_imag = acc_imag + jnp.dot(
            weights, image_imag.reshape(count * trans, width), preferred_element_type=jnp.float32
        )
        return acc_real, acc_imag

    zeros = jnp.zeros(real_out.shape, jnp.float32)
    acc_real, acc_imag = lax.fori_loop(0, dom_n, body, (zeros, zeros))
    real_out[...] = acc_real
    imag_out[...] = acc_imag


def column_sums(post_all, columns, ctf_cols, cos_cols, sin_cols):
    out = jax.ShapeDtypeStruct((post_all.shape[1], columns.shape[2]), jnp.float32)
    vmem = pl.BlockSpec(memory_space=pltpu.VMEM)
    real, imag = pl.pallas_call(
        _sums_kernel,
        out_shape=(out, out),
        in_specs=[vmem] * 5,
        out_specs=(vmem, vmem),
    )(post_all, columns, ctf_cols, cos_cols, sin_cols)
    return jnp.stack([real, imag], axis=1)


def make_images(planes, ctf_pix, cosine, sine_part):
    real_part = planes[:, 0][:, None, :]
    imag_part = planes[:, 1][:, None, :]
    shifted_real = real_part * cosine[None] - imag_part * sine_part[None]
    shifted_imag = real_part * sine_part[None] + imag_part * cosine[None]
    factor = ctf_pix[:, None, :]
    return jnp.stack([factor * shifted_real, factor * shifted_imag], axis=2).astype(jnp.bfloat16)


def pad_rows(rows, lanes):
    r, c = rows.shape
    height = -(-r // 8) * 8
    return jnp.pad(rows, ((0, height - r), (0, lanes - c)))


def on_device(particles, references, phases, mask, ctf_group, ctf_table, shell_index, sigma2):
    highest = lax.Precision.HIGHEST
    part_dev = particles.shape[0]
    ori_dev = references.shape[0]
    pixels = shell_index.shape[0]
    shells = ctf_table.shape[1]
    trans_count = phases.shape[0]
    dom_size = lax.axis_size("dom")
    orient_size = lax.axis_size("orient")
    width = pixels // dom_size
    dom_index = lax.axis_index("dom")

    shell_pick = (shell_index[:, None] == jnp.arange(shells, dtype=jnp.int32)[None, :]).astype(
        jnp.float32
    )
    group_pick = (
        ctf_group[:, None] == jnp.arange(ctf_table.shape[0], dtype=jnp.int32)[None, :]
    ).astype(jnp.float32)
    ctf_all = jnp.dot(group_pick, ctf_table, precision=highest)
    ctf_rows = lax.dynamic_slice_in_dim(ctf_all, dom_index * part_dev, part_dev, 0)
    ctf_pix = jnp.dot(ctf_rows, shell_pick.T, precision=highest)
    sigma_pix = jnp.dot(shell_pick, sigma2, precision=highest)
    refs_wide = references.astype(jnp.float32)
    weighted = (refs_wide / sigma_pix).astype(jnp.bfloat16)
    ref_norm = jnp.dot(jnp.sum(refs_wide * refs_wide, axis=1), shell_pick, precision=highest)
    energy = ref_norm / sigma2
    ctf_square = ctf_rows * ctf_rows
    quadratic = 0.5 * jnp.dot(ctf_square, energy.T, precision=highest)
    planes = particles.astype(jnp.float32)
    cosines = jnp.cos(phases)
    sine_rows = jnp.sin(phases)

    images = make_images(planes, ctf_pix, cosines, sine_rows)
    cross = jnp.einsum("itpk,jpk->itj", images, weighted, preferred_element_type=jnp.float32)
    scores = cross - quadratic[:, None, :]
    scores = jnp.where((mask == 1)[:, None, :], scores, -1e30)
    local_peak = jnp.max(scores, axis=(1, 2))
    local_total = jnp.sum(jnp.exp(scores - local_peak[:, None, None]), axis=(1, 2))

    (stats,) = exchange([(pad_rows(jnp.stack([local_peak, local_total]), 128), None)], "orient", orient_size, 1)
    peaks = stats[:, 0, :part_dev]
    totals = stats[:, 1, :part_dev]
    peak = jnp.max(peaks, axis=0)
    total = jnp.sum(totals * jnp.exp(peaks - peak[None, :]), axis=0)
    posterior = jnp.exp(scores - peak[:, None, None]) / total[:, None, None]
    post_half = posterior.astype(jnp.bfloat16)

    weight_rows = jnp.sum(posterior, axis=1)
    ctf_part = jnp.dot(weight_rows.T, ctf_square, precision=highest)
    part_norm = jnp.dot(jnp.sum(planes * planes, axis=1), shell_pick, precision=highest)
    term_one = jnp.sum(part_norm * jnp.sum(weight_rows, axis=1)[:, None], axis=0)
    term_three = jnp.sum(ctf_part * ref_norm, axis=0)
    local_sums = jnp.einsum("itj,itpk->jpk", post_half, images, preferred_element_type=jnp.float32)
    term_two = -2.0 * jnp.dot(jnp.sum(local_sums * refs_wide, axis=(0, 1)), shell_pick, precision=highest)
    terms = term_one + term_two + term_three

    term_cols = -(-shells // part_dev)
    term_rows = jnp.pad(terms, (0, term_cols * part_dev - shells)).reshape(part_dev, term_cols)
    small = jnp.concatenate([weight_rows, term_rows], axis=1)
    small = jnp.pad(small, ((0, 0), (0, -(-small.shape[1] // 128) * 128 - small.shape[1])))
    half_rows = jnp.transpose(post_half, (2, 0, 1)).reshape(ori_dev, part_dev * trans_count)
    half_all, small_all, columns, orient_small = spread(
        half_rows, small, jnp.transpose(particles, (1, 0, 2)).reshape(2 * part_dev, pixels), dom_size, orient_size, width, 2
    )
    weight_all = small_all[:, :, :ori_dev].reshape(dom_size * part_dev, ori_dev)
    shell_total = jnp.sum(
        orient_small[:, :, ori_dev : ori_dev + term_cols].reshape(orient_size, part_dev * term_cols)[:, :shells],
        axis=0,
    )

    ctf_weights = jnp.dot(weight_all.T, ctf_all * ctf_all, precision=highest)

    start_pix = dom_index * width
    pick_cols = lax.dynamic_slice_in_dim(shell_pick, start_pix, width, 0)
    ctf_cols = jnp.dot(ctf_all, pick_cols.T, precision=highest)
    cos_cols = lax.dynamic_slice_in_dim(cosines, start_pix, width, 1)
    sin_cols = lax.dynamic_slice_in_dim(sine_rows, start_pix, width, 1)
    image_sums = column_sums(
        half_all, columns, ctf_cols.reshape(dom_size, part_dev, width), cos_cols, sin_cols
    )

    divisor = part_dev * dom_size * pixels / shells
    return (posterior, image_sums, ctf_weights, shell_total / divisor)


def solution(mesh):
    return jax.shard_map(
        on_device,
        mesh=mesh,
        in_specs=(
            P("dom", None, None),
            P("orient", None, None),
            P(),
            P("dom", "orient"),
            P(),
            P(),
            P(),
            P(),
        ),
        out_specs=(P("dom", None, "orient"), P("orient", None, "dom"), P("orient", None), P()),
        check_vma=False,
    )
```

```python
import functools

import jax
import jax.numpy as jnp
from jax import lax
from jax.experimental import pallas as pl
from jax.experimental.pallas import tpu as pltpu
from jax.sharding import PartitionSpec as P

MESH_ID = pl.DeviceIdType.MESH


def _exchange_kernel(axis, n, widths, *refs):
    count = len(widths)
    x_refs = refs[:count]
    o_refs = refs[count : 2 * count]
    held = refs[2 * count : 3 * count]
    send_sem, recv_sem = refs[3 * count :]
    me = lax.axis_index(axis)
    barrier = pltpu.get_barrier_semaphore()

    def greet(k, carry):
        peer = lax.rem(me + k, n)
        pl.semaphore_signal(barrier, inc=1, device_id={axis: peer}, device_id_type=MESH_ID)
        return carry

    lax.fori_loop(1, n, greet, 0)
    pl.semaphore_wait(barrier, n - 1)

    def part(index, peer):
        width = widths[index]
        if width is None:
            return x_refs[index]
        return x_refs[index].at[:, pl.ds(pl.multiple_of(peer * width, width), width)]

    def copy(index, k):
        peer = lax.rem(me + k, n)
        return pltpu.make_async_remote_copy(
            src_ref=part(index, peer),
            dst_ref=held[index].at[me],
            send_sem=send_sem.at[index, k],
            recv_sem=recv_sem.at[index, k],
            device_id={axis: peer},
            device_id_type=MESH_ID,
        )

    def start(k, carry):
        for index in range(count):
            copy(index, k).start()
        return carry

    lax.fori_loop(1, n, start, 0)
    for index in range(count):
        held[index][me] = part(index, me)[...]

    def finish(k, carry):
        for index in range(count):
            copy(index, k).wait()
        return carry

    lax.fori_loop(1, n, finish, 0)
    for index in range(count):
        o_refs[index][...] = held[index][...]


def exchange(payloads, axis, n, collective_id):
    widths = tuple(width for _, width in payloads)
    shapes = []
    for x, width in payloads:
        block = x.shape if width is None else (x.shape[0], width)
        shapes.append(jax.ShapeDtypeStruct((n,) + block, x.dtype))
    count = len(payloads)
    vmem = pl.BlockSpec(memory_space=pltpu.VMEM)
    return pl.pallas_call(
        functools.partial(_exchange_kernel, axis, n, widths),
        out_shape=tuple(shapes),
        in_specs=[vmem] * count,
        out_specs=tuple([vmem] * count),
        scratch_shapes=[pltpu.VMEM(shape.shape, shape.dtype) for shape in shapes]
        + [pltpu.SemaphoreType.DMA((count, n)), pltpu.SemaphoreType.DMA((count, n))],
        compiler_params=pltpu.CompilerParams(collective_id=collective_id, has_side_effects=True),
    )(*[x for x, _ in payloads])


def _spread_kernel(dom_n, orient_n, half_ref, small_ref,
                   half_out, small_out, terms_out,
                   half_held, small_held, summed, terms_held,
                   send_sem, recv_sem, orient_send, orient_recv):
    me = lax.axis_index("dom")
    mine = lax.axis_index("orient")
    barrier = pltpu.get_barrier_semaphore()

    def greet_dom(k, carry):
        peer = lax.rem(me + k, dom_n)
        pl.semaphore_signal(barrier, inc=1, device_id={"dom": peer}, device_id_type=MESH_ID)
        return carry

    def greet_orient(k, carry):
        peer = lax.rem(mine + k, orient_n)
        pl.semaphore_signal(barrier, inc=1, device_id={"orient": peer}, device_id_type=MESH_ID)
        return carry

    lax.fori_loop(1, dom_n, greet_dom, 0)
    lax.fori_loop(1, orient_n, greet_orient, 0)
    pl.semaphore_wait(barrier, dom_n + orient_n - 2)

    sources = (half_ref, small_ref)
    held = (half_held, small_held)

    def copy(index, k):
        peer = lax.rem(me + k, dom_n)
        return pltpu.make_async_remote_copy(
            src_ref=sources[index],
            dst_ref=held[index].at[me],
            send_sem=send_sem.at[index, k],
            recv_sem=recv_sem.at[index, k],
            device_id={"dom": peer},
            device_id_type=MESH_ID,
        )

    def start(k, carry):
        for index in (1, 0):
            copy(index, k).start()
        return carry

    lax.fori_loop(1, dom_n, start, 0)
    for index in range(2):
        held[index][me] = sources[index][...]

    def finish(index):
        def body(k, carry):
            copy(index, k).wait()
            return carry

        lax.fori_loop(1, dom_n, body, 0)

    finish(1)
    summed[...] = jnp.sum(small_held[...], axis=0)
    finish(0)

    def orient_copy(k):
        peer = lax.rem(mine + k, orient_n)
        return pltpu.make_async_remote_copy(
            src_ref=summed,
            dst_ref=terms_held.at[mine],
            send_sem=orient_send.at[k],
            recv_sem=orient_recv.at[k],
            device_id={"orient": peer},
            device_id_type=MESH_ID,
        )

    def orient_start(k, carry):
        orient_copy(k).start()
        return carry

    lax.fori_loop(1, orient_n, orient_start, 0)
    terms_held[mine] = summed[...]

    def orient_finish(k, carry):
        orient_copy(k).wait()
        return carry

    lax.fori_loop(1, orient_n, orient_finish, 0)
    half_out[...] = half_held[...]
    small_out[...] = small_held[...]
    terms_out[...] = terms_held[...]


def spread(half_rows, small, dom_n, orient_n, collective_id):
    shapes = (
        jax.ShapeDtypeStruct((dom_n,) + half_rows.shape, half_rows.dtype),
        jax.ShapeDtypeStruct((dom_n,) + small.shape, small.dtype),
        jax.ShapeDtypeStruct((orient_n,) + small.shape, small.dtype),
    )
    vmem = pl.BlockSpec(memory_space=pltpu.VMEM)
    return pl.pallas_call(
        functools.partial(_spread_kernel, dom_n, orient_n),
        out_shape=shapes,
        in_specs=[vmem] * 2,
        out_specs=(vmem,) * 3,
        scratch_shapes=[
            pltpu.VMEM(shapes[0].shape, shapes[0].dtype),
            pltpu.VMEM(shapes[1].shape, shapes[1].dtype),
            pltpu.VMEM(small.shape, small.dtype),
            pltpu.VMEM(shapes[2].shape, shapes[2].dtype),
            pltpu.SemaphoreType.DMA((2, dom_n)),
            pltpu.SemaphoreType.DMA((2, dom_n)),
            pltpu.SemaphoreType.DMA((orient_n,)),
            pltpu.SemaphoreType.DMA((orient_n,)),
        ],
        compiler_params=pltpu.CompilerParams(collective_id=collective_id, has_side_effects=True),
    )(half_rows, small)


def make_images(planes, ctf_pix, cosine, sine_part):
    real_part = planes[:, 0][:, None, :]
    imag_part = planes[:, 1][:, None, :]
    shifted_real = real_part * cosine[None] - imag_part * sine_part[None]
    shifted_imag = real_part * sine_part[None] + imag_part * cosine[None]
    factor = ctf_pix[:, None, :]
    return jnp.stack([factor * shifted_real, factor * shifted_imag], axis=2).astype(jnp.bfloat16)


def pad_rows(rows, lanes):
    r, c = rows.shape
    height = -(-r // 8) * 8
    return jnp.pad(rows, ((0, height - r), (0, lanes - c)))


def on_device(particles, references, phases, mask, ctf_group, ctf_table, shell_index, sigma2):
    highest = lax.Precision.HIGHEST
    part_dev = particles.shape[0]
    ori_dev = references.shape[0]
    pixels = shell_index.shape[0]
    shells = ctf_table.shape[1]
    trans_count = phases.shape[0]
    dom_size = lax.axis_size("dom")
    orient_size = lax.axis_size("orient")
    width = pixels // dom_size
    dom_index = lax.axis_index("dom")

    part_rows = particles.reshape(part_dev * 2, dom_size, width)
    columns = lax.all_to_all(part_rows, "dom", 1, 0, tiled=True).reshape(dom_size, part_dev * 2, width)

    shell_pick = (shell_index[:, None] == jnp.arange(shells, dtype=jnp.int32)[None, :]).astype(
        jnp.float32
    )
    group_pick = (
        ctf_group[:, None] == jnp.arange(ctf_table.shape[0], dtype=jnp.int32)[None, :]
    ).astype(jnp.float32)
    ctf_all = jnp.dot(group_pick, ctf_table, precision=highest)
    ctf_rows = lax.dynamic_slice_in_dim(ctf_all, dom_index * part_dev, part_dev, 0)
    ctf_pix = jnp.dot(ctf_rows, shell_pick.T, precision=highest)
    sigma_pix = jnp.dot(shell_pick, sigma2, precision=highest)
    refs_wide = references.astype(jnp.float32)
    weighted = (refs_wide / sigma_pix).astype(jnp.bfloat16)
    ref_norm = jnp.dot(jnp.sum(refs_wide * refs_wide, axis=1), shell_pick, precision=highest)
    energy = ref_norm / sigma2
    ctf_square = ctf_rows * ctf_rows
    quadratic = 0.5 * jnp.dot(ctf_square, energy.T, precision=highest)
    planes = particles.astype(jnp.float32)
    cosines = jnp.cos(phases)
    sine_rows = jnp.sin(phases)

    images = make_images(planes, ctf_pix, cosines, sine_rows)
    cross = jnp.einsum("itpk,jpk->itj", images, weighted, preferred_element_type=jnp.float32)
    scores = cross - quadratic[:, None, :]
    scores = jnp.where((mask == 1)[:, None, :], scores, -1e30)
    local_peak = jnp.max(scores, axis=(1, 2))
    local_total = jnp.sum(jnp.exp(scores - local_peak[:, None, None]), axis=(1, 2))

    (stats,) = exchange([(pad_rows(jnp.stack([local_peak, local_total]), 128), None)], "orient", orient_size, 1)
    peaks = stats[:, 0, :part_dev]
    totals = stats[:, 1, :part_dev]
    peak = jnp.max(peaks, axis=0)
    total = jnp.sum(totals * jnp.exp(peaks - peak[None, :]), axis=0)
    posterior = jnp.exp(scores - peak[:, None, None]) / total[:, None, None]
    post_half = posterior.astype(jnp.bfloat16)

    weight_rows = jnp.sum(posterior, axis=1)
    ctf_part = jnp.dot(weight_rows.T, ctf_square, precision=highest)
    part_norm = jnp.dot(jnp.sum(planes * planes, axis=1), shell_pick, precision=highest)
    term_one = jnp.sum(part_norm * jnp.sum(weight_rows, axis=1)[:, None], axis=0)
    term_three = jnp.sum(ctf_part * ref_norm, axis=0)
    local_sums = jnp.einsum("itj,itpk->jpk", post_half, images, preferred_element_type=jnp.float32)
    term_two = -2.0 * jnp.dot(jnp.sum(local_sums * refs_wide, axis=(0, 1)), shell_pick, precision=highest)
    terms = term_one + term_two + term_three

    term_cols = -(-shells // part_dev)
    term_rows = jnp.pad(terms, (0, term_cols * part_dev - shells)).reshape(part_dev, term_cols)
    small = jnp.concatenate([weight_rows, term_rows], axis=1)
    small = jnp.pad(small, ((0, 0), (0, -(-small.shape[1] // 128) * 128 - small.shape[1])))
    half_rows = post_half.reshape(-1, 128)
    half_all, small_all, orient_small = spread(half_rows, small, dom_size, orient_size, 2)
    post_all = half_all.reshape(dom_size * part_dev, trans_count, ori_dev)
    weight_all = small_all[:, :, :ori_dev].reshape(dom_size * part_dev, ori_dev)
    shell_total = jnp.sum(
        orient_small[:, :, ori_dev : ori_dev + term_cols].reshape(orient_size, part_dev * term_cols)[:, :shells],
        axis=0,
    )

    ctf_weights = jnp.dot(weight_all.T, ctf_all * ctf_all, precision=highest)

    start_pix = dom_index * width
    pick_cols = lax.dynamic_slice_in_dim(shell_pick, start_pix, width, 0)
    ctf_cols = jnp.dot(ctf_all, pick_cols.T, precision=highest)
    cos_cols = lax.dynamic_slice_in_dim(cosines, start_pix, width, 1)
    sin_cols = lax.dynamic_slice_in_dim(sine_rows, start_pix, width, 1)
    col_planes = columns.reshape(dom_size * part_dev, 2, width).astype(jnp.float32)
    col_images = make_images(col_planes, ctf_cols, cos_cols, sin_cols)
    image_sums = jnp.einsum(
        "itj,itpk->jpk", post_all, col_images, preferred_element_type=jnp.float32
    )

    divisor = part_dev * dom_size * pixels / shells
    return (posterior, image_sums, ctf_weights, shell_total / divisor)


def solution(mesh):
    return jax.shard_map(
        on_device,
        mesh=mesh,
        in_specs=(
            P("dom", None, None),
            P("orient", None, None),
            P(),
            P("dom", "orient"),
            P(),
            P(),
            P(),
            P(),
        ),
        out_specs=(P("dom", None, "orient"), P("orient", None, "dom"), P("orient", None), P()),
        check_vma=False,
    )
```

```python
import functools

import jax
import jax.numpy as jnp
from jax import lax
from jax.experimental import pallas as pl
from jax.experimental.pallas import tpu as pltpu
from jax.sharding import PartitionSpec as P

MESH_ID = pl.DeviceIdType.MESH


def _exchange_kernel(axis, n, widths, *refs):
    count = len(widths)
    x_refs = refs[:count]
    o_refs = refs[count : 2 * count]
    held = refs[2 * count : 3 * count]
    send_sem, recv_sem = refs[3 * count :]
    me = lax.axis_index(axis)
    barrier = pltpu.get_barrier_semaphore()

    def greet(k, carry):
        peer = lax.rem(me + k, n)
        pl.semaphore_signal(barrier, inc=1, device_id={axis: peer}, device_id_type=MESH_ID)
        return carry

    lax.fori_loop(1, n, greet, 0)
    pl.semaphore_wait(barrier, n - 1)

    def part(index, peer):
        width = widths[index]
        if width is None:
            return x_refs[index]
        return x_refs[index].at[:, pl.ds(pl.multiple_of(peer * width, width), width)]

    def copy(index, k):
        peer = lax.rem(me + k, n)
        return pltpu.make_async_remote_copy(
            src_ref=part(index, peer),
            dst_ref=held[index].at[me],
            send_sem=send_sem.at[index, k],
            recv_sem=recv_sem.at[index, k],
            device_id={axis: peer},
            device_id_type=MESH_ID,
        )

    def start(k, carry):
        for index in range(count):
            copy(index, k).start()
        return carry

    lax.fori_loop(1, n, start, 0)
    for index in range(count):
        held[index][me] = part(index, me)[...]

    def finish(k, carry):
        for index in range(count):
            copy(index, k).wait()
        return carry

    lax.fori_loop(1, n, finish, 0)
    for index in range(count):
        o_refs[index][...] = held[index][...]


def exchange(payloads, axis, n, collective_id):
    widths = tuple(width for _, width in payloads)
    shapes = []
    for x, width in payloads:
        block = x.shape if width is None else (x.shape[0], width)
        shapes.append(jax.ShapeDtypeStruct((n,) + block, x.dtype))
    count = len(payloads)
    vmem = pl.BlockSpec(memory_space=pltpu.VMEM)
    return pl.pallas_call(
        functools.partial(_exchange_kernel, axis, n, widths),
        out_shape=tuple(shapes),
        in_specs=[vmem] * count,
        out_specs=tuple([vmem] * count),
        scratch_shapes=[pltpu.VMEM(shape.shape, shape.dtype) for shape in shapes]
        + [pltpu.SemaphoreType.DMA((count, n)), pltpu.SemaphoreType.DMA((count, n))],
        compiler_params=pltpu.CompilerParams(collective_id=collective_id, has_side_effects=True),
    )(*[x for x, _ in payloads])


def _score_kernel(orient_n, real_ref, imag_ref, ctf_ref, cos_ref, sin_ref, wr_ref, wi_ref,
                  quad_ref, mask_ref, scores_out, stats_out, stats, held, send_sem, recv_sem):
    me = lax.axis_index("orient")
    barrier = pltpu.get_barrier_semaphore()

    def greet(k, carry):
        peer = lax.rem(me + k, orient_n)
        pl.semaphore_signal(barrier, inc=1, device_id={"orient": peer}, device_id_type=MESH_ID)
        return carry

    lax.fori_loop(1, orient_n, greet, 0)

    trans = cos_ref.shape[0]
    real = real_ref[...]
    imag = imag_ref[...]
    factor = ctf_ref[...]
    quad = quad_ref[...]
    allowed = mask_ref[...] == 1
    dims = (((1,), (1,)), ((), ()))

    def score(t, peak):
        cosine = cos_ref[pl.ds(t, 1), :]
        sine_part = sin_ref[pl.ds(t, 1), :]
        image_real = (factor * (real * cosine - imag * sine_part)).astype(jnp.bfloat16)
        image_imag = (factor * (real * sine_part + imag * cosine)).astype(jnp.bfloat16)
        cross = lax.dot_general(image_real, wr_ref[...], dims, preferred_element_type=jnp.float32)
        cross = cross + lax.dot_general(image_imag, wi_ref[...], dims, preferred_element_type=jnp.float32)
        value = jnp.where(allowed, cross - quad, -1e30)
        scores_out[t] = value
        return jnp.maximum(peak, jnp.max(value, axis=1, keepdims=True))

    rows = quad.shape[0]
    peak = lax.fori_loop(0, trans, score, jnp.full((rows, 1), -jnp.inf, jnp.float32))

    def add(t, total):
        return total + jnp.sum(jnp.exp(scores_out[t] - peak), axis=1, keepdims=True)

    total = lax.fori_loop(0, trans, add, jnp.zeros((rows, 1), jnp.float32))
    lane = lax.broadcasted_iota(jnp.int32, stats.shape, 1)
    stats[...] = jnp.where(lane == 0, peak, jnp.where(lane == 1, total, 0.0))
    pl.semaphore_wait(barrier, orient_n - 1)

    def copy(k):
        peer = lax.rem(me + k, orient_n)
        return pltpu.make_async_remote_copy(
            src_ref=stats,
            dst_ref=held.at[me],
            send_sem=send_sem.at[k],
            recv_sem=recv_sem.at[k],
            device_id={"orient": peer},
            device_id_type=MESH_ID,
        )

    def start(k, carry):
        copy(k).start()
        return carry

    lax.fori_loop(1, orient_n, start, 0)
    held[me] = stats[...]

    def finish(k, carry):
        copy(k).wait()
        return carry

    lax.fori_loop(1, orient_n, finish, 0)
    stats_out[...] = held[...]


def local_scores(real, imag, factor, cosines, sine_rows, w_real, w_imag, quadratic, mask, orient_n, collective_id):
    rows = real.shape[0]
    trans = cosines.shape[0]
    stats_shape = (rows, 128)
    vmem = pl.BlockSpec(memory_space=pltpu.VMEM)
    return pl.pallas_call(
        functools.partial(_score_kernel, orient_n),
        out_shape=(
            jax.ShapeDtypeStruct((trans, rows, quadratic.shape[1]), jnp.float32),
            jax.ShapeDtypeStruct((orient_n,) + stats_shape, jnp.float32),
        ),
        in_specs=[vmem] * 9,
        out_specs=(vmem, vmem),
        scratch_shapes=[
            pltpu.VMEM(stats_shape, jnp.float32),
            pltpu.VMEM((orient_n,) + stats_shape, jnp.float32),
            pltpu.SemaphoreType.DMA((orient_n,)),
            pltpu.SemaphoreType.DMA((orient_n,)),
        ],
        compiler_params=pltpu.CompilerParams(collective_id=collective_id, has_side_effects=True),
    )(real, imag, factor, cosines, sine_rows, w_real, w_imag, quadratic, mask)


def _spread_kernel(dom_n, orient_n, width, half_ref, small_ref, part_ref,
                   half_out, small_out, part_out, terms_out,
                   half_held, small_held, part_held, summed, terms_held,
                   send_sem, recv_sem, orient_send, orient_recv):
    me = lax.axis_index("dom")
    mine = lax.axis_index("orient")
    barrier = pltpu.get_barrier_semaphore()

    def greet_dom(k, carry):
        peer = lax.rem(me + k, dom_n)
        pl.semaphore_signal(barrier, inc=1, device_id={"dom": peer}, device_id_type=MESH_ID)
        return carry

    def greet_orient(k, carry):
        peer = lax.rem(mine + k, orient_n)
        pl.semaphore_signal(barrier, inc=1, device_id={"orient": peer}, device_id_type=MESH_ID)
        return carry

    lax.fori_loop(1, dom_n, greet_dom, 0)
    lax.fori_loop(1, orient_n, greet_orient, 0)
    pl.semaphore_wait(barrier, dom_n + orient_n - 2)

    def columns(peer):
        return part_ref.at[:, pl.ds(pl.multiple_of(peer * width, width), width)]

    sources = (lambda peer: half_ref, lambda peer: small_ref, columns)
    held = (half_held, small_held, part_held)

    def copy(index, k):
        peer = lax.rem(me + k, dom_n)
        return pltpu.make_async_remote_copy(
            src_ref=sources[index](peer),
            dst_ref=held[index].at[me],
            send_sem=send_sem.at[index, k],
            recv_sem=recv_sem.at[index, k],
            device_id={"dom": peer},
            device_id_type=MESH_ID,
        )

    def start(k, carry):
        for index in (1, 0, 2):
            copy(index, k).start()
        return carry

    lax.fori_loop(1, dom_n, start, 0)
    for index in range(3):
        held[index][me] = sources[index](me)[...]

    def finish(index):
        def body(k, carry):
            copy(index, k).wait()
            return carry

        lax.fori_loop(1, dom_n, body, 0)

    finish(1)
    summed[...] = jnp.sum(small_held[...], axis=0)
    finish(0)

    def orient_copy(k):
        peer = lax.rem(mine + k, orient_n)
        return pltpu.make_async_remote_copy(
            src_ref=summed,
            dst_ref=terms_held.at[mine],
            send_sem=orient_send.at[k],
            recv_sem=orient_recv.at[k],
            device_id={"orient": peer},
            device_id_type=MESH_ID,
        )

    def orient_start(k, carry):
        orient_copy(k).start()
        return carry

    lax.fori_loop(1, orient_n, orient_start, 0)
    terms_held[mine] = summed[...]
    finish(2)

    def orient_finish(k, carry):
        orient_copy(k).wait()
        return carry

    lax.fori_loop(1, orient_n, orient_finish, 0)
    half_out[...] = half_held[...]
    small_out[...] = small_held[...]
    part_out[...] = part_held[...]
    terms_out[...] = terms_held[...]


def spread(half_rows, small, part_rows, dom_n, orient_n, width, collective_id):
    shapes = (
        jax.ShapeDtypeStruct((dom_n,) + half_rows.shape, half_rows.dtype),
        jax.ShapeDtypeStruct((dom_n,) + small.shape, small.dtype),
        jax.ShapeDtypeStruct((dom_n, part_rows.shape[0], width), part_rows.dtype),
        jax.ShapeDtypeStruct((orient_n,) + small.shape, small.dtype),
    )
    vmem = pl.BlockSpec(memory_space=pltpu.VMEM)
    return pl.pallas_call(
        functools.partial(_spread_kernel, dom_n, orient_n, width),
        out_shape=shapes,
        in_specs=[vmem] * 3,
        out_specs=(vmem,) * 4,
        scratch_shapes=[
            pltpu.VMEM(shapes[0].shape, shapes[0].dtype),
            pltpu.VMEM(shapes[1].shape, shapes[1].dtype),
            pltpu.VMEM(shapes[2].shape, shapes[2].dtype),
            pltpu.VMEM(small.shape, small.dtype),
            pltpu.VMEM(shapes[3].shape, shapes[3].dtype),
            pltpu.SemaphoreType.DMA((3, dom_n)),
            pltpu.SemaphoreType.DMA((3, dom_n)),
            pltpu.SemaphoreType.DMA((orient_n,)),
            pltpu.SemaphoreType.DMA((orient_n,)),
        ],
        compiler_params=pltpu.CompilerParams(collective_id=collective_id, has_side_effects=True),
    )(half_rows, small, part_rows)


def make_images(planes, ctf_pix, cosine, sine_part):
    real_part = planes[:, 0][:, None, :]
    imag_part = planes[:, 1][:, None, :]
    shifted_real = real_part * cosine[None] - imag_part * sine_part[None]
    shifted_imag = real_part * sine_part[None] + imag_part * cosine[None]
    factor = ctf_pix[:, None, :]
    return jnp.stack([factor * shifted_real, factor * shifted_imag], axis=2).astype(jnp.bfloat16)


def pad_rows(rows, lanes):
    r, c = rows.shape
    height = -(-r // 8) * 8
    return jnp.pad(rows, ((0, height - r), (0, lanes - c)))


def on_device(particles, references, phases, mask, ctf_group, ctf_table, shell_index, sigma2):
    highest = lax.Precision.HIGHEST
    part_dev = particles.shape[0]
    ori_dev = references.shape[0]
    pixels = shell_index.shape[0]
    shells = ctf_table.shape[1]
    trans_count = phases.shape[0]
    dom_size = lax.axis_size("dom")
    orient_size = lax.axis_size("orient")
    width = pixels // dom_size
    dom_index = lax.axis_index("dom")

    shell_pick = (shell_index[:, None] == jnp.arange(shells, dtype=jnp.int32)[None, :]).astype(
        jnp.float32
    )
    group_pick = (
        ctf_group[:, None] == jnp.arange(ctf_table.shape[0], dtype=jnp.int32)[None, :]
    ).astype(jnp.float32)
    ctf_all = jnp.dot(group_pick, ctf_table, precision=highest)
    ctf_rows = lax.dynamic_slice_in_dim(ctf_all, dom_index * part_dev, part_dev, 0)
    ctf_pix = jnp.dot(ctf_rows, shell_pick.T, precision=highest)
    sigma_pix = jnp.dot(shell_pick, sigma2, precision=highest)
    refs_wide = references.astype(jnp.float32)
    weighted = (refs_wide / sigma_pix).astype(jnp.bfloat16)
    ref_norm = jnp.dot(jnp.sum(refs_wide * refs_wide, axis=1), shell_pick, precision=highest)
    energy = ref_norm / sigma2
    ctf_square = ctf_rows * ctf_rows
    quadratic = 0.5 * jnp.dot(ctf_square, energy.T, precision=highest)
    planes = particles.astype(jnp.float32)
    cosines = jnp.cos(phases)
    sine_rows = jnp.sin(phases)

    by_trans, stats = local_scores(
        planes[:, 0], planes[:, 1], ctf_pix, cosines, sine_rows,
        weighted[:, 0], weighted[:, 1], quadratic, mask, orient_size, 1,
    )
    scores = jnp.transpose(by_trans, (1, 0, 2))
    peaks = stats[:, :, 0]
    totals = stats[:, :, 1]
    peak = jnp.max(peaks, axis=0)
    total = jnp.sum(totals * jnp.exp(peaks - peak[None, :]), axis=0)
    posterior = jnp.exp(scores - peak[:, None, None]) / total[:, None, None]
    post_half = posterior.astype(jnp.bfloat16)

    weight_rows = jnp.sum(posterior, axis=1)
    ctf_part = jnp.dot(weight_rows.T, ctf_square, precision=highest)
    part_norm = jnp.dot(jnp.sum(planes * planes, axis=1), shell_pick, precision=highest)
    term_one = jnp.sum(part_norm * jnp.sum(weight_rows, axis=1)[:, None], axis=0)
    term_three = jnp.sum(ctf_part * ref_norm, axis=0)
    images = make_images(planes, ctf_pix, cosines, sine_rows)
    local_sums = jnp.einsum("itj,itpk->jpk", post_half, images, preferred_element_type=jnp.float32)
    term_two = -2.0 * jnp.dot(jnp.sum(local_sums * refs_wide, axis=(0, 1)), shell_pick, precision=highest)
    terms = term_one + term_two + term_three

    term_cols = -(-shells // part_dev)
    term_rows = jnp.pad(terms, (0, term_cols * part_dev - shells)).reshape(part_dev, term_cols)
    small = jnp.concatenate([weight_rows, term_rows], axis=1)
    small = jnp.pad(small, ((0, 0), (0, -(-small.shape[1] // 128) * 128 - small.shape[1])))
    half_rows = post_half.reshape(-1, 128)
    half_all, small_all, columns, orient_small = spread(
        half_rows, small, particles.reshape(part_dev * 2, pixels), dom_size, orient_size, width, 2
    )
    post_all = half_all.reshape(dom_size * part_dev, trans_count, ori_dev)
    weight_all = small_all[:, :, :ori_dev].reshape(dom_size * part_dev, ori_dev)
    shell_total = jnp.sum(
        orient_small[:, :, ori_dev : ori_dev + term_cols].reshape(orient_size, part_dev * term_cols)[:, :shells],
        axis=0,
    )

    ctf_weights = jnp.dot(weight_all.T, ctf_all * ctf_all, precision=highest)

    start_pix = dom_index * width
    pick_cols = lax.dynamic_slice_in_dim(shell_pick, start_pix, width, 0)
    ctf_cols = jnp.dot(ctf_all, pick_cols.T, precision=highest)
    cos_cols = lax.dynamic_slice_in_dim(cosines, start_pix, width, 1)
    sin_cols = lax.dynamic_slice_in_dim(sine_rows, start_pix, width, 1)
    col_planes = columns.reshape(dom_size * part_dev, 2, width).astype(jnp.float32)
    col_images = make_images(col_planes, ctf_cols, cos_cols, sin_cols)
    image_sums = jnp.einsum(
        "itj,itpk->jpk", post_all, col_images, preferred_element_type=jnp.float32
    )

    divisor = part_dev * dom_size * pixels / shells
    return (posterior, image_sums, ctf_weights, shell_total / divisor)


def solution(mesh):
    return jax.shard_map(
        on_device,
        mesh=mesh,
        in_specs=(
            P("dom", None, None),
            P("orient", None, None),
            P(),
            P("dom", "orient"),
            P(),
            P(),
            P(),
            P(),
        ),
        out_specs=(P("dom", None, "orient"), P("orient", None, "dom"), P("orient", None), P()),
        check_vma=False,
    )
```

```python
import functools

import jax
import jax.numpy as jnp
from jax import lax
from jax.experimental import pallas as pl
from jax.experimental.pallas import tpu as pltpu
from jax.sharding import PartitionSpec as P

MESH_ID = pl.DeviceIdType.MESH


def _exchange_kernel(axis, n, widths, *refs):
    count = len(widths)
    x_refs = refs[:count]
    o_refs = refs[count : 2 * count]
    held = refs[2 * count : 3 * count]
    send_sem, recv_sem = refs[3 * count :]
    me = lax.axis_index(axis)
    barrier = pltpu.get_barrier_semaphore()

    def greet(k, carry):
        peer = lax.rem(me + k, n)
        pl.semaphore_signal(barrier, inc=1, device_id={axis: peer}, device_id_type=MESH_ID)
        return carry

    lax.fori_loop(1, n, greet, 0)
    pl.semaphore_wait(barrier, n - 1)

    def part(index, peer):
        width = widths[index]
        if width is None:
            return x_refs[index]
        return x_refs[index].at[:, pl.ds(pl.multiple_of(peer * width, width), width)]

    def copy(index, k):
        peer = lax.rem(me + k, n)
        return pltpu.make_async_remote_copy(
            src_ref=part(index, peer),
            dst_ref=held[index].at[me],
            send_sem=send_sem.at[index, k],
            recv_sem=recv_sem.at[index, k],
            device_id={axis: peer},
            device_id_type=MESH_ID,
        )

    def start(k, carry):
        for index in range(count):
            copy(index, k).start()
        return carry

    lax.fori_loop(1, n, start, 0)
    for index in range(count):
        held[index][me] = part(index, me)[...]

    def finish(k, carry):
        for index in range(count):
            copy(index, k).wait()
        return carry

    lax.fori_loop(1, n, finish, 0)
    for index in range(count):
        o_refs[index][...] = held[index][...]


def exchange(payloads, axis, n, collective_id):
    widths = tuple(width for _, width in payloads)
    shapes = []
    for x, width in payloads:
        block = x.shape if width is None else (x.shape[0], width)
        shapes.append(jax.ShapeDtypeStruct((n,) + block, x.dtype))
    count = len(payloads)
    vmem = pl.BlockSpec(memory_space=pltpu.VMEM)
    return pl.pallas_call(
        functools.partial(_exchange_kernel, axis, n, widths),
        out_shape=tuple(shapes),
        in_specs=[vmem] * count,
        out_specs=tuple([vmem] * count),
        scratch_shapes=[pltpu.VMEM(shape.shape, shape.dtype) for shape in shapes]
        + [pltpu.SemaphoreType.DMA((count, n)), pltpu.SemaphoreType.DMA((count, n))],
        compiler_params=pltpu.CompilerParams(collective_id=collective_id, has_side_effects=True),
    )(*[x for x, _ in payloads])


def _stats_kernel(dom_n, orient_n, width, stats_ref, part_ref, stats_out, part_out,
                  stats_held, part_held, orient_send, orient_recv, dom_send, dom_recv):
    me = lax.axis_index("dom")
    mine = lax.axis_index("orient")
    barrier = pltpu.get_barrier_semaphore()

    def greet_dom(k, carry):
        peer = lax.rem(me + k, dom_n)
        pl.semaphore_signal(barrier, inc=1, device_id={"dom": peer}, device_id_type=MESH_ID)
        return carry

    def greet_orient(k, carry):
        peer = lax.rem(mine + k, orient_n)
        pl.semaphore_signal(barrier, inc=1, device_id={"orient": peer}, device_id_type=MESH_ID)
        return carry

    lax.fori_loop(1, orient_n, greet_orient, 0)
    lax.fori_loop(1, dom_n, greet_dom, 0)
    pl.semaphore_wait(barrier, dom_n + orient_n - 2)

    def orient_copy(k):
        peer = lax.rem(mine + k, orient_n)
        return pltpu.make_async_remote_copy(
            src_ref=stats_ref,
            dst_ref=stats_held.at[mine],
            send_sem=orient_send.at[k],
            recv_sem=orient_recv.at[k],
            device_id={"orient": peer},
            device_id_type=MESH_ID,
        )

    def columns(peer):
        return part_ref.at[:, pl.ds(pl.multiple_of(peer * width, width), width)]

    def dom_copy(k):
        peer = lax.rem(me + k, dom_n)
        return pltpu.make_async_remote_copy(
            src_ref=columns(peer),
            dst_ref=part_held.at[me],
            send_sem=dom_send.at[k],
            recv_sem=dom_recv.at[k],
            device_id={"dom": peer},
            device_id_type=MESH_ID,
        )

    def orient_start(k, carry):
        orient_copy(k).start()
        return carry

    def dom_start(k, carry):
        dom_copy(k).start()
        return carry

    lax.fori_loop(1, orient_n, orient_start, 0)
    lax.fori_loop(1, dom_n, dom_start, 0)
    stats_held[mine] = stats_ref[...]
    part_held[me] = columns(me)[...]

    def orient_finish(k, carry):
        orient_copy(k).wait()
        return carry

    def dom_finish(k, carry):
        dom_copy(k).wait()
        return carry

    lax.fori_loop(1, orient_n, orient_finish, 0)
    lax.fori_loop(1, dom_n, dom_finish, 0)
    stats_out[...] = stats_held[...]
    part_out[...] = part_held[...]


def stats_and_columns(stats, part_rows, dom_n, orient_n, width, collective_id):
    shapes = (
        jax.ShapeDtypeStruct((orient_n,) + stats.shape, stats.dtype),
        jax.ShapeDtypeStruct((dom_n, part_rows.shape[0], width), part_rows.dtype),
    )
    vmem = pl.BlockSpec(memory_space=pltpu.VMEM)
    return pl.pallas_call(
        functools.partial(_stats_kernel, dom_n, orient_n, width),
        out_shape=shapes,
        in_specs=[vmem] * 2,
        out_specs=(vmem, vmem),
        scratch_shapes=[
            pltpu.VMEM(shapes[0].shape, shapes[0].dtype),
            pltpu.VMEM(shapes[1].shape, shapes[1].dtype),
            pltpu.SemaphoreType.DMA((orient_n,)),
            pltpu.SemaphoreType.DMA((orient_n,)),
            pltpu.SemaphoreType.DMA((dom_n,)),
            pltpu.SemaphoreType.DMA((dom_n,)),
        ],
        compiler_params=pltpu.CompilerParams(collective_id=collective_id, has_side_effects=True),
    )(stats, part_rows)


def _spread_kernel(dom_n, orient_n, half_ref, small_ref,
                   half_out, small_out, terms_out,
                   half_held, small_held, summed, terms_held,
                   send_sem, recv_sem, orient_send, orient_recv):
    me = lax.axis_index("dom")
    mine = lax.axis_index("orient")
    barrier = pltpu.get_barrier_semaphore()

    def greet_dom(k, carry):
        peer = lax.rem(me + k, dom_n)
        pl.semaphore_signal(barrier, inc=1, device_id={"dom": peer}, device_id_type=MESH_ID)
        return carry

    def greet_orient(k, carry):
        peer = lax.rem(mine + k, orient_n)
        pl.semaphore_signal(barrier, inc=1, device_id={"orient": peer}, device_id_type=MESH_ID)
        return carry

    lax.fori_loop(1, dom_n, greet_dom, 0)
    lax.fori_loop(1, orient_n, greet_orient, 0)
    pl.semaphore_wait(barrier, dom_n + orient_n - 2)

    sources = (half_ref, small_ref)
    held = (half_held, small_held)

    def copy(index, k):
        peer = lax.rem(me + k, dom_n)
        return pltpu.make_async_remote_copy(
            src_ref=sources[index],
            dst_ref=held[index].at[me],
            send_sem=send_sem.at[index, k],
            recv_sem=recv_sem.at[index, k],
            device_id={"dom": peer},
            device_id_type=MESH_ID,
        )

    def start(k, carry):
        for index in (1, 0):
            copy(index, k).start()
        return carry

    lax.fori_loop(1, dom_n, start, 0)
    for index in range(2):
        held[index][me] = sources[index][...]

    def finish(index):
        def body(k, carry):
            copy(index, k).wait()
            return carry

        lax.fori_loop(1, dom_n, body, 0)

    finish(1)
    summed[...] = jnp.sum(small_held[...], axis=0)
    finish(0)

    def orient_copy(k):
        peer = lax.rem(mine + k, orient_n)
        return pltpu.make_async_remote_copy(
            src_ref=summed,
            dst_ref=terms_held.at[mine],
            send_sem=orient_send.at[k],
            recv_sem=orient_recv.at[k],
            device_id={"orient": peer},
            device_id_type=MESH_ID,
        )

    def orient_start(k, carry):
        orient_copy(k).start()
        return carry

    lax.fori_loop(1, orient_n, orient_start, 0)
    terms_held[mine] = summed[...]

    def orient_finish(k, carry):
        orient_copy(k).wait()
        return carry

    lax.fori_loop(1, orient_n, orient_finish, 0)
    half_out[...] = half_held[...]
    small_out[...] = small_held[...]
    terms_out[...] = terms_held[...]


def spread(half_rows, small, dom_n, orient_n, collective_id):
    shapes = (
        jax.ShapeDtypeStruct((dom_n,) + half_rows.shape, half_rows.dtype),
        jax.ShapeDtypeStruct((dom_n,) + small.shape, small.dtype),
        jax.ShapeDtypeStruct((orient_n,) + small.shape, small.dtype),
    )
    vmem = pl.BlockSpec(memory_space=pltpu.VMEM)
    return pl.pallas_call(
        functools.partial(_spread_kernel, dom_n, orient_n),
        out_shape=shapes,
        in_specs=[vmem] * 2,
        out_specs=(vmem,) * 3,
        scratch_shapes=[
            pltpu.VMEM(shapes[0].shape, shapes[0].dtype),
            pltpu.VMEM(shapes[1].shape, shapes[1].dtype),
            pltpu.VMEM(small.shape, small.dtype),
            pltpu.VMEM(shapes[2].shape, shapes[2].dtype),
            pltpu.SemaphoreType.DMA((2, dom_n)),
            pltpu.SemaphoreType.DMA((2, dom_n)),
            pltpu.SemaphoreType.DMA((orient_n,)),
            pltpu.SemaphoreType.DMA((orient_n,)),
        ],
        compiler_params=pltpu.CompilerParams(collective_id=collective_id, has_side_effects=True),
    )(half_rows, small)


def make_images(planes, ctf_pix, cosine, sine_part):
    real_part = planes[:, 0][:, None, :]
    imag_part = planes[:, 1][:, None, :]
    shifted_real = real_part * cosine[None] - imag_part * sine_part[None]
    shifted_imag = real_part * sine_part[None] + imag_part * cosine[None]
    factor = ctf_pix[:, None, :]
    return jnp.stack([factor * shifted_real, factor * shifted_imag], axis=2).astype(jnp.bfloat16)


def pad_rows(rows, lanes):
    r, c = rows.shape
    height = -(-r // 8) * 8
    return jnp.pad(rows, ((0, height - r), (0, lanes - c)))


def on_device(particles, references, phases, mask, ctf_group, ctf_table, shell_index, sigma2):
    highest = lax.Precision.HIGHEST
    part_dev = particles.shape[0]
    ori_dev = references.shape[0]
    pixels = shell_index.shape[0]
    shells = ctf_table.shape[1]
    trans_count = phases.shape[0]
    dom_size = lax.axis_size("dom")
    orient_size = lax.axis_size("orient")
    width = pixels // dom_size
    dom_index = lax.axis_index("dom")

    shell_pick = (shell_index[:, None] == jnp.arange(shells, dtype=jnp.int32)[None, :]).astype(
        jnp.float32
    )
    group_pick = (
        ctf_group[:, None] == jnp.arange(ctf_table.shape[0], dtype=jnp.int32)[None, :]
    ).astype(jnp.float32)
    ctf_all = jnp.dot(group_pick, ctf_table, precision=highest)
    ctf_rows = lax.dynamic_slice_in_dim(ctf_all, dom_index * part_dev, part_dev, 0)
    ctf_pix = jnp.dot(ctf_rows, shell_pick.T, precision=highest)
    sigma_pix = jnp.dot(shell_pick, sigma2, precision=highest)
    refs_wide = references.astype(jnp.float32)
    weighted = (refs_wide / sigma_pix).astype(jnp.bfloat16)
    ref_norm = jnp.dot(jnp.sum(refs_wide * refs_wide, axis=1), shell_pick, precision=highest)
    energy = ref_norm / sigma2
    ctf_square = ctf_rows * ctf_rows
    quadratic = 0.5 * jnp.dot(ctf_square, energy.T, precision=highest)
    planes = particles.astype(jnp.float32)
    cosines = jnp.cos(phases)
    sine_rows = jnp.sin(phases)

    images = make_images(planes, ctf_pix, cosines, sine_rows)
    cross = jnp.einsum("itpk,jpk->itj", images, weighted, preferred_element_type=jnp.float32)
    scores = cross - quadratic[:, None, :]
    scores = jnp.where((mask == 1)[:, None, :], scores, -1e30)
    local_peak = jnp.max(scores, axis=(1, 2))
    local_total = jnp.sum(jnp.exp(scores - local_peak[:, None, None]), axis=(1, 2))

    stats, columns = stats_and_columns(
        pad_rows(jnp.stack([local_peak, local_total]), 128),
        particles.reshape(part_dev * 2, pixels),
        dom_size,
        orient_size,
        width,
        1,
    )
    peaks = stats[:, 0, :part_dev]
    totals = stats[:, 1, :part_dev]
    peak = jnp.max(peaks, axis=0)
    total = jnp.sum(totals * jnp.exp(peaks - peak[None, :]), axis=0)
    posterior = jnp.exp(scores - peak[:, None, None]) / total[:, None, None]
    post_half = posterior.astype(jnp.bfloat16)

    weight_rows = jnp.sum(posterior, axis=1)
    ctf_part = jnp.dot(weight_rows.T, ctf_square, precision=highest)
    part_norm = jnp.dot(jnp.sum(planes * planes, axis=1), shell_pick, precision=highest)
    term_one = jnp.sum(part_norm * jnp.sum(weight_rows, axis=1)[:, None], axis=0)
    term_three = jnp.sum(ctf_part * ref_norm, axis=0)
    local_sums = jnp.einsum("itj,itpk->jpk", post_half, images, preferred_element_type=jnp.float32)
    term_two = -2.0 * jnp.dot(jnp.sum(local_sums * refs_wide, axis=(0, 1)), shell_pick, precision=highest)
    terms = term_one + term_two + term_three

    term_cols = -(-shells // part_dev)
    term_rows = jnp.pad(terms, (0, term_cols * part_dev - shells)).reshape(part_dev, term_cols)
    small = jnp.concatenate([weight_rows, term_rows], axis=1)
    small = jnp.pad(small, ((0, 0), (0, -(-small.shape[1] // 128) * 128 - small.shape[1])))
    half_rows = post_half.reshape(-1, 128)
    half_all, small_all, orient_small = spread(half_rows, small, dom_size, orient_size, 2)
    post_all = half_all.reshape(dom_size * part_dev, trans_count, ori_dev)
    weight_all = small_all[:, :, :ori_dev].reshape(dom_size * part_dev, ori_dev)
    shell_total = jnp.sum(
        orient_small[:, :, ori_dev : ori_dev + term_cols].reshape(orient_size, part_dev * term_cols)[:, :shells],
        axis=0,
    )

    ctf_weights = jnp.dot(weight_all.T, ctf_all * ctf_all, precision=highest)

    start_pix = dom_index * width
    pick_cols = lax.dynamic_slice_in_dim(shell_pick, start_pix, width, 0)
    ctf_cols = jnp.dot(ctf_all, pick_cols.T, precision=highest)
    cos_cols = lax.dynamic_slice_in_dim(cosines, start_pix, width, 1)
    sin_cols = lax.dynamic_slice_in_dim(sine_rows, start_pix, width, 1)
    col_planes = columns.reshape(dom_size * part_dev, 2, width).astype(jnp.float32)
    col_images = make_images(col_planes, ctf_cols, cos_cols, sin_cols)
    image_sums = jnp.einsum(
        "itj,itpk->jpk", post_all, col_images, preferred_element_type=jnp.float32
    )

    divisor = part_dev * dom_size * pixels / shells
    return (posterior, image_sums, ctf_weights, shell_total / divisor)


def solution(mesh):
    return jax.shard_map(
        on_device,
        mesh=mesh,
        in_specs=(
            P("dom", None, None),
            P("orient", None, None),
            P(),
            P("dom", "orient"),
            P(),
            P(),
            P(),
            P(),
        ),
        out_specs=(P("dom", None, "orient"), P("orient", None, "dom"), P("orient", None), P()),
        check_vma=False,
    )
```

```python
import functools

import jax
import jax.numpy as jnp
from jax import lax
from jax.experimental import pallas as pl
from jax.experimental.pallas import tpu as pltpu
from jax.sharding import PartitionSpec as P

MESH_ID = pl.DeviceIdType.MESH


def _exchange_kernel(axis, n, widths, *refs):
    count = len(widths)
    x_refs = refs[:count]
    o_refs = refs[count : 2 * count]
    held = refs[2 * count : 3 * count]
    send_sem, recv_sem = refs[3 * count :]
    me = lax.axis_index(axis)
    barrier = pltpu.get_barrier_semaphore()

    def greet(k, carry):
        peer = lax.rem(me + k, n)
        pl.semaphore_signal(barrier, inc=1, device_id={axis: peer}, device_id_type=MESH_ID)
        return carry

    lax.fori_loop(1, n, greet, 0)
    pl.semaphore_wait(barrier, n - 1)

    def part(index, peer):
        width = widths[index]
        if width is None:
            return x_refs[index]
        return x_refs[index].at[:, pl.ds(pl.multiple_of(peer * width, width), width)]

    def copy(index, k):
        peer = lax.rem(me + k, n)
        return pltpu.make_async_remote_copy(
            src_ref=part(index, peer),
            dst_ref=held[index].at[me],
            send_sem=send_sem.at[index, k],
            recv_sem=recv_sem.at[index, k],
            device_id={axis: peer},
            device_id_type=MESH_ID,
        )

    def start(k, carry):
        for index in range(count):
            copy(index, k).start()
        return carry

    lax.fori_loop(1, n, start, 0)
    for index in range(count):
        held[index][me] = part(index, me)[...]

    def finish(k, carry):
        for index in range(count):
            copy(index, k).wait()
        return carry

    lax.fori_loop(1, n, finish, 0)
    for index in range(count):
        o_refs[index][...] = held[index][...]


def exchange(payloads, axis, n, collective_id):
    widths = tuple(width for _, width in payloads)
    shapes = []
    for x, width in payloads:
        block = x.shape if width is None else (x.shape[0], width)
        shapes.append(jax.ShapeDtypeStruct((n,) + block, x.dtype))
    count = len(payloads)
    vmem = pl.BlockSpec(memory_space=pltpu.VMEM)
    return pl.pallas_call(
        functools.partial(_exchange_kernel, axis, n, widths),
        out_shape=tuple(shapes),
        in_specs=[vmem] * count,
        out_specs=tuple([vmem] * count),
        scratch_shapes=[pltpu.VMEM(shape.shape, shape.dtype) for shape in shapes]
        + [pltpu.SemaphoreType.DMA((count, n)), pltpu.SemaphoreType.DMA((count, n))],
        compiler_params=pltpu.CompilerParams(collective_id=collective_id, has_side_effects=True),
    )(*[x for x, _ in payloads])


def _stats_kernel(dom_n, orient_n, width, stats_ref, part_ref, stats_out, part_out,
                  stats_held, part_held, orient_send, orient_recv, dom_send, dom_recv):
    me = lax.axis_index("dom")
    mine = lax.axis_index("orient")
    barrier = pltpu.get_barrier_semaphore()

    def greet_dom(k, carry):
        peer = lax.rem(me + k, dom_n)
        pl.semaphore_signal(barrier, inc=1, device_id={"dom": peer}, device_id_type=MESH_ID)
        return carry

    def greet_orient(k, carry):
        peer = lax.rem(mine + k, orient_n)
        pl.semaphore_signal(barrier, inc=1, device_id={"orient": peer}, device_id_type=MESH_ID)
        return carry

    lax.fori_loop(1, orient_n, greet_orient, 0)
    lax.fori_loop(1, dom_n, greet_dom, 0)
    pl.semaphore_wait(barrier, dom_n + orient_n - 2)

    def orient_copy(k):
        peer = lax.rem(mine + k, orient_n)
        return pltpu.make_async_remote_copy(
            src_ref=stats_ref,
            dst_ref=stats_held.at[mine],
            send_sem=orient_send.at[k],
            recv_sem=orient_recv.at[k],
            device_id={"orient": peer},
            device_id_type=MESH_ID,
        )

    def columns(peer):
        return part_ref.at[:, pl.ds(pl.multiple_of(peer * width, width), width)]

    def dom_copy(k):
        peer = lax.rem(me + k, dom_n)
        return pltpu.make_async_remote_copy(
            src_ref=columns(peer),
            dst_ref=part_held.at[me],
            send_sem=dom_send.at[k],
            recv_sem=dom_recv.at[k],
            device_id={"dom": peer},
            device_id_type=MESH_ID,
        )

    def orient_start(k, carry):
        orient_copy(k).start()
        return carry

    def dom_start(k, carry):
        dom_copy(k).start()
        return carry

    lax.fori_loop(1, orient_n, orient_start, 0)
    lax.fori_loop(1, dom_n, dom_start, 0)
    stats_held[mine] = stats_ref[...]
    part_held[me] = columns(me)[...]

    def orient_finish(k, carry):
        orient_copy(k).wait()
        return carry

    def dom_finish(k, carry):
        dom_copy(k).wait()
        return carry

    lax.fori_loop(1, orient_n, orient_finish, 0)
    lax.fori_loop(1, dom_n, dom_finish, 0)
    stats_out[...] = stats_held[...]
    part_out[...] = part_held[...]


def stats_and_columns(stats, part_rows, dom_n, orient_n, width, collective_id):
    shapes = (
        jax.ShapeDtypeStruct((orient_n,) + stats.shape, stats.dtype),
        jax.ShapeDtypeStruct((dom_n, part_rows.shape[0], width), part_rows.dtype),
    )
    vmem = pl.BlockSpec(memory_space=pltpu.VMEM)
    return pl.pallas_call(
        functools.partial(_stats_kernel, dom_n, orient_n, width),
        out_shape=shapes,
        in_specs=[vmem] * 2,
        out_specs=(vmem, vmem),
        scratch_shapes=[
            pltpu.VMEM(shapes[0].shape, shapes[0].dtype),
            pltpu.VMEM(shapes[1].shape, shapes[1].dtype),
            pltpu.SemaphoreType.DMA((orient_n,)),
            pltpu.SemaphoreType.DMA((orient_n,)),
            pltpu.SemaphoreType.DMA((dom_n,)),
            pltpu.SemaphoreType.DMA((dom_n,)),
        ],
        compiler_params=pltpu.CompilerParams(collective_id=collective_id, has_side_effects=True),
    )(stats, part_rows)


def _spread_kernel(dom_n, orient_n, half_ref, small_ref,
                   half_out, small_out, terms_out,
                   half_held, small_held, summed, terms_held,
                   send_sem, recv_sem, orient_send, orient_recv):
    me = lax.axis_index("dom")
    mine = lax.axis_index("orient")
    barrier = pltpu.get_barrier_semaphore()

    def greet_dom(k, carry):
        peer = lax.rem(me + k, dom_n)
        pl.semaphore_signal(barrier, inc=1, device_id={"dom": peer}, device_id_type=MESH_ID)
        return carry

    def greet_orient(k, carry):
        peer = lax.rem(mine + k, orient_n)
        pl.semaphore_signal(barrier, inc=1, device_id={"orient": peer}, device_id_type=MESH_ID)
        return carry

    lax.fori_loop(1, dom_n, greet_dom, 0)
    lax.fori_loop(1, orient_n, greet_orient, 0)
    pl.semaphore_wait(barrier, dom_n + orient_n - 2)

    sources = (half_ref, small_ref)
    held = (half_held, small_held)

    def copy(index, k):
        peer = lax.rem(me + k, dom_n)
        return pltpu.make_async_remote_copy(
            src_ref=sources[index],
            dst_ref=held[index].at[me],
            send_sem=send_sem.at[index, k],
            recv_sem=recv_sem.at[index, k],
            device_id={"dom": peer},
            device_id_type=MESH_ID,
        )

    def start(k, carry):
        for index in (1, 0):
            copy(index, k).start()
        return carry

    lax.fori_loop(1, dom_n, start, 0)
    for index in range(2):
        held[index][me] = sources[index][...]

    def finish(index):
        def body(k, carry):
            copy(index, k).wait()
            return carry

        lax.fori_loop(1, dom_n, body, 0)

    finish(1)
    summed[...] = jnp.sum(small_held[...], axis=0)
    finish(0)

    def orient_copy(k):
        peer = lax.rem(mine + k, orient_n)
        return pltpu.make_async_remote_copy(
            src_ref=summed,
            dst_ref=terms_held.at[mine],
            send_sem=orient_send.at[k],
            recv_sem=orient_recv.at[k],
            device_id={"orient": peer},
            device_id_type=MESH_ID,
        )

    def orient_start(k, carry):
        orient_copy(k).start()
        return carry

    lax.fori_loop(1, orient_n, orient_start, 0)
    terms_held[mine] = summed[...]

    def orient_finish(k, carry):
        orient_copy(k).wait()
        return carry

    lax.fori_loop(1, orient_n, orient_finish, 0)
    half_out[...] = half_held[...]
    small_out[...] = small_held[...]
    terms_out[...] = terms_held[...]


def spread(half_rows, small, dom_n, orient_n, collective_id):
    shapes = (
        jax.ShapeDtypeStruct((dom_n,) + half_rows.shape, half_rows.dtype),
        jax.ShapeDtypeStruct((dom_n,) + small.shape, small.dtype),
        jax.ShapeDtypeStruct((orient_n,) + small.shape, small.dtype),
    )
    vmem = pl.BlockSpec(memory_space=pltpu.VMEM)
    return pl.pallas_call(
        functools.partial(_spread_kernel, dom_n, orient_n),
        out_shape=shapes,
        in_specs=[vmem] * 2,
        out_specs=(vmem,) * 3,
        scratch_shapes=[
            pltpu.VMEM(shapes[0].shape, shapes[0].dtype),
            pltpu.VMEM(shapes[1].shape, shapes[1].dtype),
            pltpu.VMEM(small.shape, small.dtype),
            pltpu.VMEM(shapes[2].shape, shapes[2].dtype),
            pltpu.SemaphoreType.DMA((2, dom_n)),
            pltpu.SemaphoreType.DMA((2, dom_n)),
            pltpu.SemaphoreType.DMA((orient_n,)),
            pltpu.SemaphoreType.DMA((orient_n,)),
        ],
        compiler_params=pltpu.CompilerParams(collective_id=collective_id, has_side_effects=True),
    )(half_rows, small)


def make_images(planes, ctf_pix, cosine, sine_part):
    real_part = planes[:, 0][:, None, :]
    imag_part = planes[:, 1][:, None, :]
    shifted_real = real_part * cosine[None] - imag_part * sine_part[None]
    shifted_imag = real_part * sine_part[None] + imag_part * cosine[None]
    factor = ctf_pix[:, None, :]
    return jnp.stack([factor * shifted_real, factor * shifted_imag], axis=2).astype(jnp.bfloat16)


def pad_rows(rows, lanes):
    r, c = rows.shape
    height = -(-r // 8) * 8
    return jnp.pad(rows, ((0, height - r), (0, lanes - c)))


def on_device(particles, references, phases, mask, ctf_group, ctf_table, shell_index, sigma2):
    highest = lax.Precision.HIGHEST
    part_dev = particles.shape[0]
    ori_dev = references.shape[0]
    pixels = shell_index.shape[0]
    shells = ctf_table.shape[1]
    trans_count = phases.shape[0]
    dom_size = lax.axis_size("dom")
    orient_size = lax.axis_size("orient")
    width = pixels // dom_size
    dom_index = lax.axis_index("dom")

    shell_pick = (shell_index[:, None] == jnp.arange(shells, dtype=jnp.int32)[None, :]).astype(
        jnp.float32
    )
    group_pick = (
        ctf_group[:, None] == jnp.arange(ctf_table.shape[0], dtype=jnp.int32)[None, :]
    ).astype(jnp.float32)
    ctf_all = jnp.dot(group_pick, ctf_table, precision=highest)
    ctf_rows = lax.dynamic_slice_in_dim(ctf_all, dom_index * part_dev, part_dev, 0)
    ctf_pix = jnp.dot(ctf_rows, shell_pick.T, precision=highest)
    sigma_pix = jnp.dot(shell_pick, sigma2, precision=highest)
    refs_wide = references.astype(jnp.float32)
    weighted = (refs_wide / sigma_pix).astype(jnp.bfloat16)
    ref_norm = jnp.dot(jnp.sum(refs_wide * refs_wide, axis=1), shell_pick, precision=highest)
    energy = ref_norm / sigma2
    ctf_square = ctf_rows * ctf_rows
    quadratic = 0.5 * jnp.dot(ctf_square, energy.T, precision=highest)
    planes = particles.astype(jnp.float32)
    cosines = jnp.cos(phases)
    sine_rows = jnp.sin(phases)

    images = make_images(planes, ctf_pix, cosines, sine_rows)
    cross = jnp.einsum("itpk,jpk->itj", images, weighted, preferred_element_type=jnp.float32)
    scores = cross - quadratic[:, None, :]
    scores = jnp.where((mask == 1)[:, None, :], scores, -1e30)
    local_peak = jnp.max(scores, axis=(1, 2))
    local_total = jnp.sum(jnp.exp(scores - local_peak[:, None, None]), axis=(1, 2))

    stats, columns = stats_and_columns(
        pad_rows(jnp.stack([local_peak, local_total]), 128),
        particles.reshape(part_dev * 2, pixels),
        dom_size,
        orient_size,
        width,
        1,
    )
    peaks = stats[:, 0, :part_dev]
    totals = stats[:, 1, :part_dev]
    peak = jnp.max(peaks, axis=0)
    total = jnp.sum(totals * jnp.exp(peaks - peak[None, :]), axis=0)
    posterior = jnp.exp(scores - peak[:, None, None]) / total[:, None, None]
    post_half = posterior.astype(jnp.bfloat16)

    weight_rows = jnp.sum(posterior, axis=1)
    ctf_part = jnp.dot(weight_rows.T, ctf_square, precision=highest)
    part_norm = jnp.dot(jnp.sum(planes * planes, axis=1), shell_pick, precision=highest)
    term_one = jnp.sum(part_norm * jnp.sum(weight_rows, axis=1)[:, None], axis=0)
    term_three = jnp.sum(ctf_part * ref_norm, axis=0)
    local_sums = jnp.einsum("itj,itpk->jpk", post_half, images, preferred_element_type=jnp.float32)
    term_two = -2.0 * jnp.dot(jnp.sum(local_sums * refs_wide, axis=(0, 1)), shell_pick, precision=highest)
    terms = term_one + term_two + term_three

    term_cols = -(-shells // part_dev)
    term_rows = jnp.pad(terms, (0, term_cols * part_dev - shells)).reshape(part_dev, term_cols)
    small = jnp.concatenate([weight_rows, term_rows], axis=1)
    small = jnp.pad(small, ((0, 0), (0, -(-small.shape[1] // 128) * 128 - small.shape[1])))
    half_rows = jnp.transpose(post_half, (1, 2, 0)).reshape(trans_count, ori_dev * part_dev)
    half_all, small_all, orient_small = spread(half_rows, small, dom_size, orient_size, 2)
    post_all = jnp.transpose(
        half_all.reshape(dom_size, trans_count, ori_dev, part_dev), (1, 2, 0, 3)
    ).reshape(trans_count, ori_dev, dom_size * part_dev)
    weight_all = small_all[:, :, :ori_dev].reshape(dom_size * part_dev, ori_dev)
    shell_total = jnp.sum(
        orient_small[:, :, ori_dev : ori_dev + term_cols].reshape(orient_size, part_dev * term_cols)[:, :shells],
        axis=0,
    )

    ctf_weights = jnp.dot(weight_all.T, ctf_all * ctf_all, precision=highest)

    start_pix = dom_index * width
    pick_cols = lax.dynamic_slice_in_dim(shell_pick, start_pix, width, 0)
    ctf_cols = jnp.dot(ctf_all, pick_cols.T, precision=highest)
    cos_cols = lax.dynamic_slice_in_dim(cosines, start_pix, width, 1)
    sin_cols = lax.dynamic_slice_in_dim(sine_rows, start_pix, width, 1)
    col_planes = columns.reshape(dom_size * part_dev, 2, width).astype(jnp.float32)
    col_images = make_images(col_planes, ctf_cols, cos_cols, sin_cols)
    image_sums = jnp.einsum(
        "tji,itpk->jpk", post_all, col_images, preferred_element_type=jnp.float32
    )

    divisor = part_dev * dom_size * pixels / shells
    return (posterior, image_sums, ctf_weights, shell_total / divisor)


def solution(mesh):
    return jax.shard_map(
        on_device,
        mesh=mesh,
        in_specs=(
            P("dom", None, None),
            P("orient", None, None),
            P(),
            P("dom", "orient"),
            P(),
            P(),
            P(),
            P(),
        ),
        out_specs=(P("dom", None, "orient"), P("orient", None, "dom"), P("orient", None), P()),
        check_vma=False,
    )
```

```python
import functools

import jax
import jax.numpy as jnp
from jax import lax
from jax.experimental import pallas as pl
from jax.experimental.pallas import tpu as pltpu
from jax.sharding import PartitionSpec as P

MESH_ID = pl.DeviceIdType.MESH


def _exchange_kernel(axis, n, widths, *refs):
    count = len(widths)
    x_refs = refs[:count]
    o_refs = refs[count : 2 * count]
    held = refs[2 * count : 3 * count]
    send_sem, recv_sem = refs[3 * count :]
    me = lax.axis_index(axis)
    barrier = pltpu.get_barrier_semaphore()

    def greet(k, carry):
        peer = lax.rem(me + k, n)
        pl.semaphore_signal(barrier, inc=1, device_id={axis: peer}, device_id_type=MESH_ID)
        return carry

    lax.fori_loop(1, n, greet, 0)
    pl.semaphore_wait(barrier, n - 1)

    def part(index, peer):
        width = widths[index]
        if width is None:
            return x_refs[index]
        return x_refs[index].at[:, pl.ds(pl.multiple_of(peer * width, width), width)]

    def copy(index, k):
        peer = lax.rem(me + k, n)
        return pltpu.make_async_remote_copy(
            src_ref=part(index, peer),
            dst_ref=held[index].at[me],
            send_sem=send_sem.at[index, k],
            recv_sem=recv_sem.at[index, k],
            device_id={axis: peer},
            device_id_type=MESH_ID,
        )

    def start(k, carry):
        for index in range(count):
            copy(index, k).start()
        return carry

    lax.fori_loop(1, n, start, 0)
    for index in range(count):
        held[index][me] = part(index, me)[...]

    def finish(k, carry):
        for index in range(count):
            copy(index, k).wait()
        return carry

    lax.fori_loop(1, n, finish, 0)
    for index in range(count):
        o_refs[index][...] = held[index][...]


def exchange(payloads, axis, n, collective_id):
    widths = tuple(width for _, width in payloads)
    shapes = []
    for x, width in payloads:
        block = x.shape if width is None else (x.shape[0], width)
        shapes.append(jax.ShapeDtypeStruct((n,) + block, x.dtype))
    count = len(payloads)
    vmem = pl.BlockSpec(memory_space=pltpu.VMEM)
    return pl.pallas_call(
        functools.partial(_exchange_kernel, axis, n, widths),
        out_shape=tuple(shapes),
        in_specs=[vmem] * count,
        out_specs=tuple([vmem] * count),
        scratch_shapes=[pltpu.VMEM(shape.shape, shape.dtype) for shape in shapes]
        + [pltpu.SemaphoreType.DMA((count, n)), pltpu.SemaphoreType.DMA((count, n))],
        compiler_params=pltpu.CompilerParams(collective_id=collective_id, has_side_effects=True),
    )(*[x for x, _ in payloads])


def _stats_kernel(dom_n, orient_n, width, stats_ref, part_ref, stats_out, part_out,
                  stats_held, part_held, orient_send, orient_recv, dom_send, dom_recv):
    me = lax.axis_index("dom")
    mine = lax.axis_index("orient")
    barrier = pltpu.get_barrier_semaphore()

    def greet_dom(k, carry):
        peer = lax.rem(me + k, dom_n)
        pl.semaphore_signal(barrier, inc=1, device_id={"dom": peer}, device_id_type=MESH_ID)
        return carry

    def greet_orient(k, carry):
        peer = lax.rem(mine + k, orient_n)
        pl.semaphore_signal(barrier, inc=1, device_id={"orient": peer}, device_id_type=MESH_ID)
        return carry

    lax.fori_loop(1, orient_n, greet_orient, 0)
    lax.fori_loop(1, dom_n, greet_dom, 0)
    pl.semaphore_wait(barrier, dom_n + orient_n - 2)

    def orient_copy(k):
        peer = lax.rem(mine + k, orient_n)
        return pltpu.make_async_remote_copy(
            src_ref=stats_ref,
            dst_ref=stats_held.at[mine],
            send_sem=orient_send.at[k],
            recv_sem=orient_recv.at[k],
            device_id={"orient": peer},
            device_id_type=MESH_ID,
        )

    def columns(peer):
        return part_ref.at[:, pl.ds(pl.multiple_of(peer * width, width), width)]

    def dom_copy(k):
        peer = lax.rem(me + k, dom_n)
        return pltpu.make_async_remote_copy(
            src_ref=columns(peer),
            dst_ref=part_held.at[me],
            send_sem=dom_send.at[k],
            recv_sem=dom_recv.at[k],
            device_id={"dom": peer},
            device_id_type=MESH_ID,
        )

    def orient_start(k, carry):
        orient_copy(k).start()
        return carry

    def dom_start(k, carry):
        dom_copy(k).start()
        return carry

    lax.fori_loop(1, orient_n, orient_start, 0)
    lax.fori_loop(1, dom_n, dom_start, 0)
    stats_held[mine] = stats_ref[...]
    part_held[me] = columns(me)[...]

    def orient_finish(k, carry):
        orient_copy(k).wait()
        return carry

    def dom_finish(k, carry):
        dom_copy(k).wait()
        return carry

    lax.fori_loop(1, orient_n, orient_finish, 0)
    lax.fori_loop(1, dom_n, dom_finish, 0)
    stats_out[...] = stats_held[...]
    part_out[...] = part_held[...]


def stats_and_columns(stats, part_rows, dom_n, orient_n, width, collective_id):
    shapes = (
        jax.ShapeDtypeStruct((orient_n,) + stats.shape, stats.dtype),
        jax.ShapeDtypeStruct((dom_n, part_rows.shape[0], width), part_rows.dtype),
    )
    vmem = pl.BlockSpec(memory_space=pltpu.VMEM)
    return pl.pallas_call(
        functools.partial(_stats_kernel, dom_n, orient_n, width),
        out_shape=shapes,
        in_specs=[vmem] * 2,
        out_specs=(vmem, vmem),
        scratch_shapes=[
            pltpu.VMEM(shapes[0].shape, shapes[0].dtype),
            pltpu.VMEM(shapes[1].shape, shapes[1].dtype),
            pltpu.SemaphoreType.DMA((orient_n,)),
            pltpu.SemaphoreType.DMA((orient_n,)),
            pltpu.SemaphoreType.DMA((dom_n,)),
            pltpu.SemaphoreType.DMA((dom_n,)),
        ],
        compiler_params=pltpu.CompilerParams(collective_id=collective_id, has_side_effects=True),
    )(stats, part_rows)


def _spread_kernel(dom_n, orient_n, half_ref, small_ref,
                   half_out, small_out, terms_out,
                   half_held, small_held, summed, terms_held,
                   send_sem, recv_sem, orient_send, orient_recv):
    me = lax.axis_index("dom")
    mine = lax.axis_index("orient")
    barrier = pltpu.get_barrier_semaphore()

    def greet_dom(k, carry):
        peer = lax.rem(me + k, dom_n)
        pl.semaphore_signal(barrier, inc=1, device_id={"dom": peer}, device_id_type=MESH_ID)
        return carry

    def greet_orient(k, carry):
        peer = lax.rem(mine + k, orient_n)
        pl.semaphore_signal(barrier, inc=1, device_id={"orient": peer}, device_id_type=MESH_ID)
        return carry

    lax.fori_loop(1, dom_n, greet_dom, 0)
    lax.fori_loop(1, orient_n, greet_orient, 0)
    pl.semaphore_wait(barrier, dom_n + orient_n - 2)

    sources = (half_ref, small_ref)
    held = (half_held, small_held)

    def copy(index, k):
        peer = lax.rem(me + k, dom_n)
        return pltpu.make_async_remote_copy(
            src_ref=sources[index],
            dst_ref=held[index].at[me],
            send_sem=send_sem.at[index, k],
            recv_sem=recv_sem.at[index, k],
            device_id={"dom": peer},
            device_id_type=MESH_ID,
        )

    def start(k, carry):
        for index in (1, 0):
            copy(index, k).start()
        return carry

    lax.fori_loop(1, dom_n, start, 0)
    for index in range(2):
        held[index][me] = sources[index][...]

    def finish(index):
        def body(k, carry):
            copy(index, k).wait()
            return carry

        lax.fori_loop(1, dom_n, body, 0)

    finish(1)
    summed[...] = jnp.sum(small_held[...], axis=0)
    finish(0)

    def orient_copy(k):
        peer = lax.rem(mine + k, orient_n)
        return pltpu.make_async_remote_copy(
            src_ref=summed,
            dst_ref=terms_held.at[mine],
            send_sem=orient_send.at[k],
            recv_sem=orient_recv.at[k],
            device_id={"orient": peer},
            device_id_type=MESH_ID,
        )

    def orient_start(k, carry):
        orient_copy(k).start()
        return carry

    lax.fori_loop(1, orient_n, orient_start, 0)
    terms_held[mine] = summed[...]

    def orient_finish(k, carry):
        orient_copy(k).wait()
        return carry

    lax.fori_loop(1, orient_n, orient_finish, 0)
    half_out[...] = half_held[...]
    small_out[...] = small_held[...]
    terms_out[...] = terms_held[...]


def spread(half_rows, small, dom_n, orient_n, collective_id):
    shapes = (
        jax.ShapeDtypeStruct((dom_n,) + half_rows.shape, half_rows.dtype),
        jax.ShapeDtypeStruct((dom_n,) + small.shape, small.dtype),
        jax.ShapeDtypeStruct((orient_n,) + small.shape, small.dtype),
    )
    vmem = pl.BlockSpec(memory_space=pltpu.VMEM)
    return pl.pallas_call(
        functools.partial(_spread_kernel, dom_n, orient_n),
        out_shape=shapes,
        in_specs=[vmem] * 2,
        out_specs=(vmem,) * 3,
        scratch_shapes=[
            pltpu.VMEM(shapes[0].shape, shapes[0].dtype),
            pltpu.VMEM(shapes[1].shape, shapes[1].dtype),
            pltpu.VMEM(small.shape, small.dtype),
            pltpu.VMEM(shapes[2].shape, shapes[2].dtype),
            pltpu.SemaphoreType.DMA((2, dom_n)),
            pltpu.SemaphoreType.DMA((2, dom_n)),
            pltpu.SemaphoreType.DMA((orient_n,)),
            pltpu.SemaphoreType.DMA((orient_n,)),
        ],
        compiler_params=pltpu.CompilerParams(collective_id=collective_id, has_side_effects=True),
    )(half_rows, small)


def make_images(planes, ctf_pix, cosine, sine_part):
    real_part = planes[:, 0][:, None, :]
    imag_part = planes[:, 1][:, None, :]
    shifted_real = real_part * cosine[None] - imag_part * sine_part[None]
    shifted_imag = real_part * sine_part[None] + imag_part * cosine[None]
    factor = ctf_pix[:, None, :]
    return jnp.stack([factor * shifted_real, factor * shifted_imag], axis=2).astype(jnp.bfloat16)


def pad_rows(rows, lanes):
    r, c = rows.shape
    height = -(-r // 8) * 8
    return jnp.pad(rows, ((0, height - r), (0, lanes - c)))


def on_device(particles, references, phases, mask, ctf_group, ctf_table, shell_index, sigma2):
    highest = lax.Precision.HIGHEST
    part_dev = particles.shape[0]
    ori_dev = references.shape[0]
    pixels = shell_index.shape[0]
    shells = ctf_table.shape[1]
    trans_count = phases.shape[0]
    dom_size = lax.axis_size("dom")
    orient_size = lax.axis_size("orient")
    width = pixels // dom_size
    dom_index = lax.axis_index("dom")

    shell_pick = (shell_index[:, None] == jnp.arange(shells, dtype=jnp.int32)[None, :]).astype(
        jnp.float32
    )
    group_pick = (
        ctf_group[:, None] == jnp.arange(ctf_table.shape[0], dtype=jnp.int32)[None, :]
    ).astype(jnp.float32)
    ctf_all = jnp.dot(group_pick, ctf_table, precision=highest)
    ctf_rows = lax.dynamic_slice_in_dim(ctf_all, dom_index * part_dev, part_dev, 0)
    per_pixel = jnp.dot(
        jnp.concatenate([ctf_rows, sigma2[None]], axis=0), shell_pick.T, precision=highest
    )
    ctf_pix = per_pixel[:part_dev]
    sigma_pix = per_pixel[part_dev]
    refs_wide = references.astype(jnp.float32)
    weighted = (refs_wide / sigma_pix).astype(jnp.bfloat16)
    planes = particles.astype(jnp.float32)
    norms = jnp.dot(
        jnp.concatenate([jnp.sum(refs_wide * refs_wide, axis=1), jnp.sum(planes * planes, axis=1)], axis=0),
        shell_pick,
        precision=highest,
    )
    ref_norm = norms[:ori_dev]
    part_norm = norms[ori_dev:]
    energy = ref_norm / sigma2
    ctf_square = ctf_rows * ctf_rows
    quadratic = 0.5 * jnp.dot(ctf_square, energy.T, precision=highest)
    cosines = jnp.cos(phases)
    sine_rows = jnp.sin(phases)

    images = make_images(planes, ctf_pix, cosines, sine_rows)
    cross = jnp.einsum("itpk,jpk->itj", images, weighted, preferred_element_type=jnp.float32)
    scores = cross - quadratic[:, None, :]
    scores = jnp.where((mask == 1)[:, None, :], scores, -1e30)
    local_peak = jnp.max(scores, axis=(1, 2))
    local_total = jnp.sum(jnp.exp(scores - local_peak[:, None, None]), axis=(1, 2))

    stats, columns = stats_and_columns(
        pad_rows(jnp.stack([local_peak, local_total]), 128),
        particles.reshape(part_dev * 2, pixels),
        dom_size,
        orient_size,
        width,
        1,
    )
    peaks = stats[:, 0, :part_dev]
    totals = stats[:, 1, :part_dev]
    peak = jnp.max(peaks, axis=0)
    total = jnp.sum(totals * jnp.exp(peaks - peak[None, :]), axis=0)
    posterior = jnp.exp(scores - peak[:, None, None]) / total[:, None, None]
    post_half = posterior.astype(jnp.bfloat16)

    weight_rows = jnp.sum(posterior, axis=1)
    ctf_part = jnp.dot(weight_rows.T, ctf_square, precision=highest)
    term_one = jnp.sum(part_norm * jnp.sum(weight_rows, axis=1)[:, None], axis=0)
    term_three = jnp.sum(ctf_part * ref_norm, axis=0)
    local_sums = jnp.einsum("itj,itpk->jpk", post_half, images, preferred_element_type=jnp.float32)
    term_two = -2.0 * jnp.dot(jnp.sum(local_sums * refs_wide, axis=(0, 1)), shell_pick, precision=highest)
    terms = term_one + term_two + term_three

    term_cols = -(-shells // part_dev)
    term_rows = jnp.pad(terms, (0, term_cols * part_dev - shells)).reshape(part_dev, term_cols)
    small = jnp.concatenate([weight_rows, term_rows], axis=1)
    small = jnp.pad(small, ((0, 0), (0, -(-small.shape[1] // 128) * 128 - small.shape[1])))
    half_rows = post_half.reshape(-1, 128)
    half_all, small_all, orient_small = spread(half_rows, small, dom_size, orient_size, 2)
    post_all = half_all.reshape(dom_size * part_dev, trans_count, ori_dev)
    weight_all = small_all[:, :, :ori_dev].reshape(dom_size * part_dev, ori_dev)
    shell_total = jnp.sum(
        orient_small[:, :, ori_dev : ori_dev + term_cols].reshape(orient_size, part_dev * term_cols)[:, :shells],
        axis=0,
    )

    ctf_weights = jnp.dot(weight_all.T, ctf_all * ctf_all, precision=highest)

    start_pix = dom_index * width
    pick_cols = lax.dynamic_slice_in_dim(shell_pick, start_pix, width, 0)
    ctf_cols = jnp.dot(ctf_all, pick_cols.T, precision=highest)
    cos_cols = lax.dynamic_slice_in_dim(cosines, start_pix, width, 1)
    sin_cols = lax.dynamic_slice_in_dim(sine_rows, start_pix, width, 1)
    col_planes = columns.reshape(dom_size * part_dev, 2, width).astype(jnp.float32)
    col_images = make_images(col_planes, ctf_cols, cos_cols, sin_cols)
    image_sums = jnp.einsum(
        "itj,itpk->jpk", post_all, col_images, preferred_element_type=jnp.float32
    )

    divisor = part_dev * dom_size * pixels / shells
    return (posterior, image_sums, ctf_weights, shell_total / divisor)


def solution(mesh):
    return jax.shard_map(
        on_device,
        mesh=mesh,
        in_specs=(
            P("dom", None, None),
            P("orient", None, None),
            P(),
            P("dom", "orient"),
            P(),
            P(),
            P(),
            P(),
        ),
        out_specs=(P("dom", None, "orient"), P("orient", None, "dom"), P("orient", None), P()),
        check_vma=False,
    )
```

```python
import functools

import jax
import jax.numpy as jnp
from jax import lax
from jax.experimental import pallas as pl
from jax.experimental.pallas import tpu as pltpu
from jax.sharding import PartitionSpec as P

MESH_ID = pl.DeviceIdType.MESH


def _exchange_kernel(axis, n, widths, *refs):
    count = len(widths)
    x_refs = refs[:count]
    o_refs = refs[count : 2 * count]
    held = refs[2 * count : 3 * count]
    send_sem, recv_sem = refs[3 * count :]
    me = lax.axis_index(axis)
    barrier = pltpu.get_barrier_semaphore()

    def greet(k, carry):
        peer = lax.rem(me + k, n)
        pl.semaphore_signal(barrier, inc=1, device_id={axis: peer}, device_id_type=MESH_ID)
        return carry

    lax.fori_loop(1, n, greet, 0)
    pl.semaphore_wait(barrier, n - 1)

    def part(index, peer):
        width = widths[index]
        if width is None:
            return x_refs[index]
        return x_refs[index].at[:, pl.ds(pl.multiple_of(peer * width, width), width)]

    def copy(index, k):
        peer = lax.rem(me + k, n)
        return pltpu.make_async_remote_copy(
            src_ref=part(index, peer),
            dst_ref=held[index].at[me],
            send_sem=send_sem.at[index, k],
            recv_sem=recv_sem.at[index, k],
            device_id={axis: peer},
            device_id_type=MESH_ID,
        )

    def start(k, carry):
        for index in range(count):
            copy(index, k).start()
        return carry

    lax.fori_loop(1, n, start, 0)
    for index in range(count):
        held[index][me] = part(index, me)[...]

    def finish(k, carry):
        for index in range(count):
            copy(index, k).wait()
        return carry

    lax.fori_loop(1, n, finish, 0)
    for index in range(count):
        o_refs[index][...] = held[index][...]


def exchange(payloads, axis, n, collective_id):
    widths = tuple(width for _, width in payloads)
    shapes = []
    for x, width in payloads:
        block = x.shape if width is None else (x.shape[0], width)
        shapes.append(jax.ShapeDtypeStruct((n,) + block, x.dtype))
    count = len(payloads)
    vmem = pl.BlockSpec(memory_space=pltpu.VMEM)
    return pl.pallas_call(
        functools.partial(_exchange_kernel, axis, n, widths),
        out_shape=tuple(shapes),
        in_specs=[vmem] * count,
        out_specs=tuple([vmem] * count),
        scratch_shapes=[pltpu.VMEM(shape.shape, shape.dtype) for shape in shapes]
        + [pltpu.SemaphoreType.DMA((count, n)), pltpu.SemaphoreType.DMA((count, n))],
        compiler_params=pltpu.CompilerParams(collective_id=collective_id, has_side_effects=True),
    )(*[x for x, _ in payloads])


def _stats_kernel(dom_n, orient_n, width, stats_ref, part_ref, stats_held, part_held,
                  orient_send, orient_recv, dom_send, dom_recv):
    me = lax.axis_index("dom")
    mine = lax.axis_index("orient")
    barrier = pltpu.get_barrier_semaphore()

    def greet_dom(k, carry):
        peer = lax.rem(me + k, dom_n)
        pl.semaphore_signal(barrier, inc=1, device_id={"dom": peer}, device_id_type=MESH_ID)
        return carry

    def greet_orient(k, carry):
        peer = lax.rem(mine + k, orient_n)
        pl.semaphore_signal(barrier, inc=1, device_id={"orient": peer}, device_id_type=MESH_ID)
        return carry

    lax.fori_loop(1, orient_n, greet_orient, 0)
    lax.fori_loop(1, dom_n, greet_dom, 0)
    pl.semaphore_wait(barrier, dom_n + orient_n - 2)

    def orient_copy(k):
        peer = lax.rem(mine + k, orient_n)
        return pltpu.make_async_remote_copy(
            src_ref=stats_ref,
            dst_ref=stats_held.at[mine],
            send_sem=orient_send.at[k],
            recv_sem=orient_recv.at[k],
            device_id={"orient": peer},
            device_id_type=MESH_ID,
        )

    def columns(peer):
        return part_ref.at[:, pl.ds(pl.multiple_of(peer * width, width), width)]

    def dom_copy(k):
        peer = lax.rem(me + k, dom_n)
        return pltpu.make_async_remote_copy(
            src_ref=columns(peer),
            dst_ref=part_held.at[me],
            send_sem=dom_send.at[k],
            recv_sem=dom_recv.at[k],
            device_id={"dom": peer},
            device_id_type=MESH_ID,
        )

    def orient_start(k, carry):
        orient_copy(k).start()
        return carry

    def dom_start(k, carry):
        dom_copy(k).start()
        return carry

    lax.fori_loop(1, orient_n, orient_start, 0)
    lax.fori_loop(1, dom_n, dom_start, 0)
    stats_held[mine] = stats_ref[...]
    part_held[me] = columns(me)[...]

    def orient_finish(k, carry):
        orient_copy(k).wait()
        return carry

    def dom_finish(k, carry):
        dom_copy(k).wait()
        return carry

    lax.fori_loop(1, orient_n, orient_finish, 0)
    lax.fori_loop(1, dom_n, dom_finish, 0)


def stats_and_columns(stats, part_rows, dom_n, orient_n, width, collective_id):
    shapes = (
        jax.ShapeDtypeStruct((orient_n,) + stats.shape, stats.dtype),
        jax.ShapeDtypeStruct((dom_n, part_rows.shape[0], width), part_rows.dtype),
    )
    vmem = pl.BlockSpec(memory_space=pltpu.VMEM)
    return pl.pallas_call(
        functools.partial(_stats_kernel, dom_n, orient_n, width),
        out_shape=shapes,
        in_specs=[vmem] * 2,
        out_specs=(vmem, vmem),
        scratch_shapes=[
            pltpu.SemaphoreType.DMA((orient_n,)),
            pltpu.SemaphoreType.DMA((orient_n,)),
            pltpu.SemaphoreType.DMA((dom_n,)),
            pltpu.SemaphoreType.DMA((dom_n,)),
        ],
        compiler_params=pltpu.CompilerParams(collective_id=collective_id, has_side_effects=True),
    )(stats, part_rows)


def _spread_kernel(dom_n, orient_n, half_ref, small_ref,
                   half_held, small_held, terms_held, summed,
                   send_sem, recv_sem, orient_send, orient_recv):
    me = lax.axis_index("dom")
    mine = lax.axis_index("orient")
    barrier = pltpu.get_barrier_semaphore()

    def greet_dom(k, carry):
        peer = lax.rem(me + k, dom_n)
        pl.semaphore_signal(barrier, inc=1, device_id={"dom": peer}, device_id_type=MESH_ID)
        return carry

    def greet_orient(k, carry):
        peer = lax.rem(mine + k, orient_n)
        pl.semaphore_signal(barrier, inc=1, device_id={"orient": peer}, device_id_type=MESH_ID)
        return carry

    lax.fori_loop(1, dom_n, greet_dom, 0)
    lax.fori_loop(1, orient_n, greet_orient, 0)
    pl.semaphore_wait(barrier, dom_n + orient_n - 2)

    sources = (half_ref, small_ref)
    held = (half_held, small_held)

    def copy(index, k):
        peer = lax.rem(me + k, dom_n)
        return pltpu.make_async_remote_copy(
            src_ref=sources[index],
            dst_ref=held[index].at[me],
            send_sem=send_sem.at[index, k],
            recv_sem=recv_sem.at[index, k],
            device_id={"dom": peer},
            device_id_type=MESH_ID,
        )

    def start(k, carry):
        for index in (1, 0):
            copy(index, k).start()
        return carry

    lax.fori_loop(1, dom_n, start, 0)
    for index in range(2):
        held[index][me] = sources[index][...]

    def finish(index):
        def body(k, carry):
            copy(index, k).wait()
            return carry

        lax.fori_loop(1, dom_n, body, 0)

    finish(1)
    summed[...] = jnp.sum(small_held[...], axis=0)
    finish(0)

    def orient_copy(k):
        peer = lax.rem(mine + k, orient_n)
        return pltpu.make_async_remote_copy(
            src_ref=summed,
            dst_ref=terms_held.at[mine],
            send_sem=orient_send.at[k],
            recv_sem=orient_recv.at[k],
            device_id={"orient": peer},
            device_id_type=MESH_ID,
        )

    def orient_start(k, carry):
        orient_copy(k).start()
        return carry

    lax.fori_loop(1, orient_n, orient_start, 0)
    terms_held[mine] = summed[...]

    def orient_finish(k, carry):
        orient_copy(k).wait()
        return carry

    lax.fori_loop(1, orient_n, orient_finish, 0)


def spread(half_rows, small, dom_n, orient_n, collective_id):
    shapes = (
        jax.ShapeDtypeStruct((dom_n,) + half_rows.shape, half_rows.dtype),
        jax.ShapeDtypeStruct((dom_n,) + small.shape, small.dtype),
        jax.ShapeDtypeStruct((orient_n,) + small.shape, small.dtype),
    )
    vmem = pl.BlockSpec(memory_space=pltpu.VMEM)
    return pl.pallas_call(
        functools.partial(_spread_kernel, dom_n, orient_n),
        out_shape=shapes,
        in_specs=[vmem] * 2,
        out_specs=(vmem,) * 3,
        scratch_shapes=[
            pltpu.VMEM(small.shape, small.dtype),
            pltpu.SemaphoreType.DMA((2, dom_n)),
            pltpu.SemaphoreType.DMA((2, dom_n)),
            pltpu.SemaphoreType.DMA((orient_n,)),
            pltpu.SemaphoreType.DMA((orient_n,)),
        ],
        compiler_params=pltpu.CompilerParams(collective_id=collective_id, has_side_effects=True),
    )(half_rows, small)


def make_images(planes, ctf_pix, cosine, sine_part):
    real_part = planes[:, 0][:, None, :]
    imag_part = planes[:, 1][:, None, :]
    shifted_real = real_part * cosine[None] - imag_part * sine_part[None]
    shifted_imag = real_part * sine_part[None] + imag_part * cosine[None]
    factor = ctf_pix[:, None, :]
    return jnp.stack([factor * shifted_real, factor * shifted_imag], axis=2).astype(jnp.bfloat16)


def pad_rows(rows, lanes):
    r, c = rows.shape
    height = -(-r // 8) * 8
    return jnp.pad(rows, ((0, height - r), (0, lanes - c)))


def on_device(particles, references, phases, mask, ctf_group, ctf_table, shell_index, sigma2):
    highest = lax.Precision.HIGHEST
    part_dev = particles.shape[0]
    ori_dev = references.shape[0]
    pixels = shell_index.shape[0]
    shells = ctf_table.shape[1]
    trans_count = phases.shape[0]
    dom_size = lax.axis_size("dom")
    orient_size = lax.axis_size("orient")
    width = pixels // dom_size
    dom_index = lax.axis_index("dom")

    shell_pick = (shell_index[:, None] == jnp.arange(shells, dtype=jnp.int32)[None, :]).astype(
        jnp.float32
    )
    group_pick = (
        ctf_group[:, None] == jnp.arange(ctf_table.shape[0], dtype=jnp.int32)[None, :]
    ).astype(jnp.float32)
    ctf_all = jnp.dot(group_pick, ctf_table, precision=highest)
    ctf_rows = lax.dynamic_slice_in_dim(ctf_all, dom_index * part_dev, part_dev, 0)
    per_pixel = jnp.dot(
        jnp.concatenate([ctf_rows, sigma2[None]], axis=0), shell_pick.T, precision=highest
    )
    ctf_pix = per_pixel[:part_dev]
    sigma_pix = per_pixel[part_dev]
    refs_wide = references.astype(jnp.float32)
    weighted = (refs_wide / sigma_pix).astype(jnp.bfloat16)
    planes = particles.astype(jnp.float32)
    norms = jnp.dot(
        jnp.concatenate([jnp.sum(refs_wide * refs_wide, axis=1), jnp.sum(planes * planes, axis=1)], axis=0),
        shell_pick,
        precision=highest,
    )
    ref_norm = norms[:ori_dev]
    part_norm = norms[ori_dev:]
    energy = ref_norm / sigma2
    ctf_square = ctf_rows * ctf_rows
    quadratic = 0.5 * jnp.dot(ctf_square, energy.T, precision=highest)
    cosines = jnp.cos(phases)
    sine_rows = jnp.sin(phases)

    images = make_images(planes, ctf_pix, cosines, sine_rows)
    cross = jnp.einsum("itpk,jpk->itj", images, weighted, preferred_element_type=jnp.float32)
    scores = cross - quadratic[:, None, :]
    scores = jnp.where((mask == 1)[:, None, :], scores, -1e30)
    local_peak = jnp.max(scores, axis=(1, 2))
    local_total = jnp.sum(jnp.exp(scores - local_peak[:, None, None]), axis=(1, 2))

    stats, columns = stats_and_columns(
        pad_rows(jnp.stack([local_peak, local_total]), 128),
        particles.reshape(part_dev * 2, pixels),
        dom_size,
        orient_size,
        width,
        1,
    )
    peaks = stats[:, 0, :part_dev]
    totals = stats[:, 1, :part_dev]
    peak = jnp.max(peaks, axis=0)
    total = jnp.sum(totals * jnp.exp(peaks - peak[None, :]), axis=0)
    posterior = jnp.exp(scores - peak[:, None, None]) / total[:, None, None]
    post_half = posterior.astype(jnp.bfloat16)

    weight_rows = jnp.sum(posterior, axis=1)
    ctf_part = jnp.dot(weight_rows.T, ctf_square, precision=highest)
    term_one = jnp.sum(part_norm * jnp.sum(weight_rows, axis=1)[:, None], axis=0)
    term_three = jnp.sum(ctf_part * ref_norm, axis=0)
    local_sums = jnp.einsum("itj,itpk->jpk", post_half, images, preferred_element_type=jnp.float32)
    term_two = -2.0 * jnp.dot(jnp.sum(local_sums * refs_wide, axis=(0, 1)), shell_pick, precision=highest)
    terms = term_one + term_two + term_three

    term_cols = -(-shells // part_dev)
    term_rows = jnp.pad(terms, (0, term_cols * part_dev - shells)).reshape(part_dev, term_cols)
    small = jnp.concatenate([weight_rows, term_rows], axis=1)
    small = jnp.pad(small, ((0, 0), (0, -(-small.shape[1] // 128) * 128 - small.shape[1])))
    half_rows = post_half.reshape(-1, 128)
    half_all, small_all, orient_small = spread(half_rows, small, dom_size, orient_size, 2)
    post_all = half_all.reshape(dom_size * part_dev, trans_count, ori_dev)
    weight_all = small_all[:, :, :ori_dev].reshape(dom_size * part_dev, ori_dev)
    shell_total = jnp.sum(
        orient_small[:, :, ori_dev : ori_dev + term_cols].reshape(orient_size, part_dev * term_cols)[:, :shells],
        axis=0,
    )

    ctf_weights = jnp.dot(weight_all.T, ctf_all * ctf_all, precision=highest)

    start_pix = dom_index * width
    pick_cols = lax.dynamic_slice_in_dim(shell_pick, start_pix, width, 0)
    ctf_cols = jnp.dot(ctf_all, pick_cols.T, precision=highest)
    cos_cols = lax.dynamic_slice_in_dim(cosines, start_pix, width, 1)
    sin_cols = lax.dynamic_slice_in_dim(sine_rows, start_pix, width, 1)
    col_planes = columns.reshape(dom_size * part_dev, 2, width).astype(jnp.float32)
    col_images = make_images(col_planes, ctf_cols, cos_cols, sin_cols)
    image_sums = jnp.einsum(
        "itj,itpk->jpk", post_all, col_images, preferred_element_type=jnp.float32
    )

    divisor = part_dev * dom_size * pixels / shells
    return (posterior, image_sums, ctf_weights, shell_total / divisor)


def solution(mesh):
    return jax.shard_map(
        on_device,
        mesh=mesh,
        in_specs=(
            P("dom", None, None),
            P("orient", None, None),
            P(),
            P("dom", "orient"),
            P(),
            P(),
            P(),
            P(),
        ),
        out_specs=(P("dom", None, "orient"), P("orient", None, "dom"), P("orient", None), P()),
        check_vma=False,
    )
```

```python
import functools

import jax
import jax.numpy as jnp
from jax import lax
from jax.experimental import pallas as pl
from jax.experimental.pallas import tpu as pltpu
from jax.sharding import PartitionSpec as P

MESH_ID = pl.DeviceIdType.MESH


def _exchange_kernel(axis, n, widths, *refs):
    count = len(widths)
    x_refs = refs[:count]
    o_refs = refs[count : 2 * count]
    held = refs[2 * count : 3 * count]
    send_sem, recv_sem = refs[3 * count :]
    me = lax.axis_index(axis)
    barrier = pltpu.get_barrier_semaphore()

    def greet(k, carry):
        peer = lax.rem(me + k, n)
        pl.semaphore_signal(barrier, inc=1, device_id={axis: peer}, device_id_type=MESH_ID)
        return carry

    lax.fori_loop(1, n, greet, 0)
    pl.semaphore_wait(barrier, n - 1)

    def part(index, peer):
        width = widths[index]
        if width is None:
            return x_refs[index]
        return x_refs[index].at[:, pl.ds(pl.multiple_of(peer * width, width), width)]

    def copy(index, k):
        peer = lax.rem(me + k, n)
        return pltpu.make_async_remote_copy(
            src_ref=part(index, peer),
            dst_ref=held[index].at[me],
            send_sem=send_sem.at[index, k],
            recv_sem=recv_sem.at[index, k],
            device_id={axis: peer},
            device_id_type=MESH_ID,
        )

    def start(k, carry):
        for index in range(count):
            copy(index, k).start()
        return carry

    lax.fori_loop(1, n, start, 0)
    for index in range(count):
        held[index][me] = part(index, me)[...]

    def finish(k, carry):
        for index in range(count):
            copy(index, k).wait()
        return carry

    lax.fori_loop(1, n, finish, 0)
    for index in range(count):
        o_refs[index][...] = held[index][...]


def exchange(payloads, axis, n, collective_id):
    widths = tuple(width for _, width in payloads)
    shapes = []
    for x, width in payloads:
        block = x.shape if width is None else (x.shape[0], width)
        shapes.append(jax.ShapeDtypeStruct((n,) + block, x.dtype))
    count = len(payloads)
    vmem = pl.BlockSpec(memory_space=pltpu.VMEM)
    return pl.pallas_call(
        functools.partial(_exchange_kernel, axis, n, widths),
        out_shape=tuple(shapes),
        in_specs=[vmem] * count,
        out_specs=tuple([vmem] * count),
        scratch_shapes=[pltpu.VMEM(shape.shape, shape.dtype) for shape in shapes]
        + [pltpu.SemaphoreType.DMA((count, n)), pltpu.SemaphoreType.DMA((count, n))],
        compiler_params=pltpu.CompilerParams(collective_id=collective_id, has_side_effects=True),
    )(*[x for x, _ in payloads])


def _stats_kernel(dom_n, orient_n, width, stats_ref, part_ref, stats_out, part_out,
                  stats_held, part_held, orient_send, orient_recv, dom_send, dom_recv):
    me = lax.axis_index("dom")
    mine = lax.axis_index("orient")
    barrier = pltpu.get_barrier_semaphore()

    def greet_dom(k, carry):
        peer = lax.rem(me + k, dom_n)
        pl.semaphore_signal(barrier, inc=1, device_id={"dom": peer}, device_id_type=MESH_ID)
        return carry

    def greet_orient(k, carry):
        peer = lax.rem(mine + k, orient_n)
        pl.semaphore_signal(barrier, inc=1, device_id={"orient": peer}, device_id_type=MESH_ID)
        return carry

    lax.fori_loop(1, orient_n, greet_orient, 0)
    lax.fori_loop(1, dom_n, greet_dom, 0)
    pl.semaphore_wait(barrier, dom_n + orient_n - 2)

    def orient_copy(k):
        peer = lax.rem(mine + k, orient_n)
        return pltpu.make_async_remote_copy(
            src_ref=stats_ref,
            dst_ref=stats_held.at[mine],
            send_sem=orient_send.at[k],
            recv_sem=orient_recv.at[k],
            device_id={"orient": peer},
            device_id_type=MESH_ID,
        )

    def columns(peer):
        return part_ref.at[:, pl.ds(pl.multiple_of(peer * width, width), width)]

    def dom_copy(k):
        peer = lax.rem(me + k, dom_n)
        return pltpu.make_async_remote_copy(
            src_ref=columns(peer),
            dst_ref=part_held.at[me],
            send_sem=dom_send.at[k],
            recv_sem=dom_recv.at[k],
            device_id={"dom": peer},
            device_id_type=MESH_ID,
        )

    def orient_start(k, carry):
        orient_copy(k).start()
        return carry

    def dom_start(k, carry):
        dom_copy(k).start()
        return carry

    lax.fori_loop(1, orient_n, orient_start, 0)
    lax.fori_loop(1, dom_n, dom_start, 0)
    stats_held[mine] = stats_ref[...]
    part_held[me] = columns(me)[...]

    def orient_finish(k, carry):
        orient_copy(k).wait()
        return carry

    def dom_finish(k, carry):
        dom_copy(k).wait()
        return carry

    lax.fori_loop(1, orient_n, orient_finish, 0)
    lax.fori_loop(1, dom_n, dom_finish, 0)
    stats_out[...] = stats_held[...]
    part_out[...] = part_held[...]


def stats_and_columns(stats, part_rows, dom_n, orient_n, width, collective_id):
    shapes = (
        jax.ShapeDtypeStruct((orient_n,) + stats.shape, stats.dtype),
        jax.ShapeDtypeStruct((dom_n, part_rows.shape[0], width), part_rows.dtype),
    )
    vmem = pl.BlockSpec(memory_space=pltpu.VMEM)
    return pl.pallas_call(
        functools.partial(_stats_kernel, dom_n, orient_n, width),
        out_shape=shapes,
        in_specs=[vmem] * 2,
        out_specs=(vmem, vmem),
        scratch_shapes=[
            pltpu.VMEM(shapes[0].shape, shapes[0].dtype),
            pltpu.VMEM(shapes[1].shape, shapes[1].dtype),
            pltpu.SemaphoreType.DMA((orient_n,)),
            pltpu.SemaphoreType.DMA((orient_n,)),
            pltpu.SemaphoreType.DMA((dom_n,)),
            pltpu.SemaphoreType.DMA((dom_n,)),
        ],
        compiler_params=pltpu.CompilerParams(collective_id=collective_id, has_side_effects=True),
    )(stats, part_rows)


def _spread_kernel(dom_n, orient_n, half_ref, small_ref,
                   half_out, small_out, terms_out,
                   half_held, small_held, summed, terms_held,
                   send_sem, recv_sem, orient_send, orient_recv):
    me = lax.axis_index("dom")
    mine = lax.axis_index("orient")
    barrier = pltpu.get_barrier_semaphore()

    def greet_dom(k, carry):
        peer = lax.rem(me + k, dom_n)
        pl.semaphore_signal(barrier, inc=1, device_id={"dom": peer}, device_id_type=MESH_ID)
        return carry

    def greet_orient(k, carry):
        peer = lax.rem(mine + k, orient_n)
        pl.semaphore_signal(barrier, inc=1, device_id={"orient": peer}, device_id_type=MESH_ID)
        return carry

    lax.fori_loop(1, dom_n, greet_dom, 0)
    lax.fori_loop(1, orient_n, greet_orient, 0)
    pl.semaphore_wait(barrier, dom_n + orient_n - 2)

    sources = (half_ref, small_ref)
    held = (half_held, small_held)

    def copy(index, k):
        peer = lax.rem(me + k, dom_n)
        return pltpu.make_async_remote_copy(
            src_ref=sources[index],
            dst_ref=held[index].at[me],
            send_sem=send_sem.at[index, k],
            recv_sem=recv_sem.at[index, k],
            device_id={"dom": peer},
            device_id_type=MESH_ID,
        )

    def start(k, carry):
        for index in (1, 0):
            copy(index, k).start()
        return carry

    lax.fori_loop(1, dom_n, start, 0)
    for index in range(2):
        held[index][me] = sources[index][...]

    def finish(index):
        def body(k, carry):
            copy(index, k).wait()
            return carry

        lax.fori_loop(1, dom_n, body, 0)

    finish(1)
    total = jnp.sum(small_held[...], axis=0)
    summed[...] = total
    terms_held[mine] = total

    def orient_copy(k):
        peer = lax.rem(mine + k, orient_n)
        return pltpu.make_async_remote_copy(
            src_ref=summed,
            dst_ref=terms_held.at[mine],
            send_sem=orient_send.at[k],
            recv_sem=orient_recv.at[k],
            device_id={"orient": peer},
            device_id_type=MESH_ID,
        )

    def orient_start(k, carry):
        orient_copy(k).start()
        return carry

    lax.fori_loop(1, orient_n, orient_start, 0)
    finish(0)

    def orient_finish(k, carry):
        orient_copy(k).wait()
        return carry

    lax.fori_loop(1, orient_n, orient_finish, 0)
    half_out[...] = half_held[...]
    small_out[...] = small_held[...]
    terms_out[...] = terms_held[...]


def spread(half_rows, small, dom_n, orient_n, collective_id):
    shapes = (
        jax.ShapeDtypeStruct((dom_n,) + half_rows.shape, half_rows.dtype),
        jax.ShapeDtypeStruct((dom_n,) + small.shape, small.dtype),
        jax.ShapeDtypeStruct((orient_n,) + small.shape, small.dtype),
    )
    vmem = pl.BlockSpec(memory_space=pltpu.VMEM)
    return pl.pallas_call(
        functools.partial(_spread_kernel, dom_n, orient_n),
        out_shape=shapes,
        in_specs=[vmem] * 2,
        out_specs=(vmem,) * 3,
        scratch_shapes=[
            pltpu.VMEM(shapes[0].shape, shapes[0].dtype),
            pltpu.VMEM(shapes[1].shape, shapes[1].dtype),
            pltpu.VMEM(small.shape, small.dtype),
            pltpu.VMEM(shapes[2].shape, shapes[2].dtype),
            pltpu.SemaphoreType.DMA((2, dom_n)),
            pltpu.SemaphoreType.DMA((2, dom_n)),
            pltpu.SemaphoreType.DMA((orient_n,)),
            pltpu.SemaphoreType.DMA((orient_n,)),
        ],
        compiler_params=pltpu.CompilerParams(collective_id=collective_id, has_side_effects=True),
    )(half_rows, small)


def make_images(planes, ctf_pix, cosine, sine_part):
    real_part = planes[:, 0][:, None, :]
    imag_part = planes[:, 1][:, None, :]
    shifted_real = real_part * cosine[None] - imag_part * sine_part[None]
    shifted_imag = real_part * sine_part[None] + imag_part * cosine[None]
    factor = ctf_pix[:, None, :]
    return jnp.stack([factor * shifted_real, factor * shifted_imag], axis=2).astype(jnp.bfloat16)


def pad_rows(rows, lanes):
    r, c = rows.shape
    height = -(-r // 8) * 8
    return jnp.pad(rows, ((0, height - r), (0, lanes - c)))


def on_device(particles, references, phases, mask, ctf_group, ctf_table, shell_index, sigma2):
    highest = lax.Precision.HIGHEST
    part_dev = particles.shape[0]
    ori_dev = references.shape[0]
    pixels = shell_index.shape[0]
    shells = ctf_table.shape[1]
    trans_count = phases.shape[0]
    dom_size = lax.axis_size("dom")
    orient_size = lax.axis_size("orient")
    width = pixels // dom_size
    dom_index = lax.axis_index("dom")

    shell_pick = (shell_index[:, None] == jnp.arange(shells, dtype=jnp.int32)[None, :]).astype(
        jnp.float32
    )
    group_pick = (
        ctf_group[:, None] == jnp.arange(ctf_table.shape[0], dtype=jnp.int32)[None, :]
    ).astype(jnp.float32)
    ctf_all = jnp.dot(group_pick, ctf_table, precision=highest)
    ctf_rows = lax.dynamic_slice_in_dim(ctf_all, dom_index * part_dev, part_dev, 0)
    per_pixel = jnp.dot(
        jnp.concatenate([ctf_rows, sigma2[None]], axis=0), shell_pick.T, precision=highest
    )
    ctf_pix = per_pixel[:part_dev]
    sigma_pix = per_pixel[part_dev]
    refs_wide = references.astype(jnp.float32)
    weighted = (refs_wide / sigma_pix).astype(jnp.bfloat16)
    planes = particles.astype(jnp.float32)
    norms = jnp.dot(
        jnp.concatenate([jnp.sum(refs_wide * refs_wide, axis=1), jnp.sum(planes * planes, axis=1)], axis=0),
        shell_pick,
        precision=highest,
    )
    ref_norm = norms[:ori_dev]
    part_norm = norms[ori_dev:]
    energy = ref_norm / sigma2
    ctf_square = ctf_rows * ctf_rows
    quadratic = 0.5 * jnp.dot(ctf_square, energy.T, precision=highest)
    cosines = jnp.cos(phases)
    sine_rows = jnp.sin(phases)

    images = make_images(planes, ctf_pix, cosines, sine_rows)
    cross = jnp.einsum("itpk,jpk->itj", images, weighted, preferred_element_type=jnp.float32)
    scores = cross - quadratic[:, None, :]
    scores = jnp.where((mask == 1)[:, None, :], scores, -1e30)
    local_peak = jnp.max(scores, axis=(1, 2))
    local_total = jnp.sum(jnp.exp(scores - local_peak[:, None, None]), axis=(1, 2))

    stats, columns = stats_and_columns(
        pad_rows(jnp.stack([local_peak, local_total]), 128),
        particles.reshape(part_dev * 2, pixels),
        dom_size,
        orient_size,
        width,
        1,
    )
    peaks = stats[:, 0, :part_dev]
    totals = stats[:, 1, :part_dev]
    peak = jnp.max(peaks, axis=0)
    total = jnp.sum(totals * jnp.exp(peaks - peak[None, :]), axis=0)
    posterior = jnp.exp(scores - peak[:, None, None]) / total[:, None, None]
    post_half = posterior.astype(jnp.bfloat16)

    weight_rows = jnp.sum(posterior, axis=1)
    ctf_part = jnp.dot(weight_rows.T, ctf_square, precision=highest)
    term_one = jnp.sum(part_norm * jnp.sum(weight_rows, axis=1)[:, None], axis=0)
    term_three = jnp.sum(ctf_part * ref_norm, axis=0)
    local_sums = jnp.einsum("itj,itpk->jpk", post_half, images, preferred_element_type=jnp.float32)
    term_two = -2.0 * jnp.dot(jnp.sum(local_sums * refs_wide, axis=(0, 1)), shell_pick, precision=highest)
    terms = term_one + term_two + term_three

    term_cols = -(-shells // part_dev)
    term_rows = jnp.pad(terms, (0, term_cols * part_dev - shells)).reshape(part_dev, term_cols)
    small = jnp.concatenate([weight_rows, term_rows], axis=1)
    small = jnp.pad(small, ((0, 0), (0, -(-small.shape[1] // 128) * 128 - small.shape[1])))
    half_rows = post_half.reshape(-1, 128)
    half_all, small_all, orient_small = spread(half_rows, small, dom_size, orient_size, 2)
    post_all = half_all.reshape(dom_size * part_dev, trans_count, ori_dev)
    weight_all = small_all[:, :, :ori_dev].reshape(dom_size * part_dev, ori_dev)
    shell_total = jnp.sum(
        orient_small[:, :, ori_dev : ori_dev + term_cols].reshape(orient_size, part_dev * term_cols)[:, :shells],
        axis=0,
    )

    ctf_weights = jnp.dot(weight_all.T, ctf_all * ctf_all, precision=highest)

    start_pix = dom_index * width
    pick_cols = lax.dynamic_slice_in_dim(shell_pick, start_pix, width, 0)
    ctf_cols = jnp.dot(ctf_all, pick_cols.T, precision=highest)
    cos_cols = lax.dynamic_slice_in_dim(cosines, start_pix, width, 1)
    sin_cols = lax.dynamic_slice_in_dim(sine_rows, start_pix, width, 1)
    col_planes = columns.reshape(dom_size * part_dev, 2, width).astype(jnp.float32)
    col_images = make_images(col_planes, ctf_cols, cos_cols, sin_cols)
    image_sums = jnp.einsum(
        "itj,itpk->jpk", post_all, col_images, preferred_element_type=jnp.float32
    )

    divisor = part_dev * dom_size * pixels / shells
    return (posterior, image_sums, ctf_weights, shell_total / divisor)


def solution(mesh):
    return jax.shard_map(
        on_device,
        mesh=mesh,
        in_specs=(
            P("dom", None, None),
            P("orient", None, None),
            P(),
            P("dom", "orient"),
            P(),
            P(),
            P(),
            P(),
        ),
        out_specs=(P("dom", None, "orient"), P("orient", None, "dom"), P("orient", None), P()),
        check_vma=False,
    )
```

```python
import functools

import jax
import jax.numpy as jnp
from jax import lax
from jax.experimental import pallas as pl
from jax.experimental.pallas import tpu as pltpu
from jax.sharding import PartitionSpec as P

MESH_ID = pl.DeviceIdType.MESH


def _exchange_kernel(axis, n, widths, *refs):
    count = len(widths)
    x_refs = refs[:count]
    o_refs = refs[count : 2 * count]
    held = refs[2 * count : 3 * count]
    send_sem, recv_sem = refs[3 * count :]
    me = lax.axis_index(axis)
    barrier = pltpu.get_barrier_semaphore()

    def greet(k, carry):
        peer = lax.rem(me + k, n)
        pl.semaphore_signal(barrier, inc=1, device_id={axis: peer}, device_id_type=MESH_ID)
        return carry

    lax.fori_loop(1, n, greet, 0)
    pl.semaphore_wait(barrier, n - 1)

    def part(index, peer):
        width = widths[index]
        if width is None:
            return x_refs[index]
        return x_refs[index].at[:, pl.ds(pl.multiple_of(peer * width, width), width)]

    def copy(index, k):
        peer = lax.rem(me + k, n)
        return pltpu.make_async_remote_copy(
            src_ref=part(index, peer),
            dst_ref=held[index].at[me],
            send_sem=send_sem.at[index, k],
            recv_sem=recv_sem.at[index, k],
            device_id={axis: peer},
            device_id_type=MESH_ID,
        )

    def start(k, carry):
        for index in range(count):
            copy(index, k).start()
        return carry

    lax.fori_loop(1, n, start, 0)
    for index in range(count):
        held[index][me] = part(index, me)[...]

    def finish(k, carry):
        for index in range(count):
            copy(index, k).wait()
        return carry

    lax.fori_loop(1, n, finish, 0)
    for index in range(count):
        o_refs[index][...] = held[index][...]


def exchange(payloads, axis, n, collective_id):
    widths = tuple(width for _, width in payloads)
    shapes = []
    for x, width in payloads:
        block = x.shape if width is None else (x.shape[0], width)
        shapes.append(jax.ShapeDtypeStruct((n,) + block, x.dtype))
    count = len(payloads)
    vmem = pl.BlockSpec(memory_space=pltpu.VMEM)
    return pl.pallas_call(
        functools.partial(_exchange_kernel, axis, n, widths),
        out_shape=tuple(shapes),
        in_specs=[vmem] * count,
        out_specs=tuple([vmem] * count),
        scratch_shapes=[pltpu.VMEM(shape.shape, shape.dtype) for shape in shapes]
        + [pltpu.SemaphoreType.DMA((count, n)), pltpu.SemaphoreType.DMA((count, n))],
        compiler_params=pltpu.CompilerParams(collective_id=collective_id, has_side_effects=True),
    )(*[x for x, _ in payloads])


def _stats_kernel(dom_n, orient_n, width, stats_ref, part_ref, stats_out, part_out,
                  stats_held, part_held, orient_send, orient_recv, dom_send, dom_recv):
    me = lax.axis_index("dom")
    mine = lax.axis_index("orient")
    barrier = pltpu.get_barrier_semaphore()

    def greet_dom(k, carry):
        peer = lax.rem(me + k, dom_n)
        pl.semaphore_signal(barrier, inc=1, device_id={"dom": peer}, device_id_type=MESH_ID)
        return carry

    def greet_orient(k, carry):
        peer = lax.rem(mine + k, orient_n)
        pl.semaphore_signal(barrier, inc=1, device_id={"orient": peer}, device_id_type=MESH_ID)
        return carry

    lax.fori_loop(1, orient_n, greet_orient, 0)
    lax.fori_loop(1, dom_n, greet_dom, 0)
    pl.semaphore_wait(barrier, dom_n + orient_n - 2)

    def orient_copy(k):
        peer = lax.rem(mine + k, orient_n)
        return pltpu.make_async_remote_copy(
            src_ref=stats_ref,
            dst_ref=stats_held.at[mine],
            send_sem=orient_send.at[k],
            recv_sem=orient_recv.at[k],
            device_id={"orient": peer},
            device_id_type=MESH_ID,
        )

    def columns(peer):
        return part_ref.at[:, pl.ds(pl.multiple_of(peer * width, width), width // 2)]

    def dom_copy(k):
        peer = lax.rem(me + k, dom_n)
        return pltpu.make_async_remote_copy(
            src_ref=columns(peer),
            dst_ref=part_held.at[me],
            send_sem=dom_send.at[k],
            recv_sem=dom_recv.at[k],
            device_id={"dom": peer},
            device_id_type=MESH_ID,
        )

    def orient_start(k, carry):
        orient_copy(k).start()
        return carry

    def dom_start(k, carry):
        dom_copy(k).start()
        return carry

    lax.fori_loop(1, orient_n, orient_start, 0)
    lax.fori_loop(1, dom_n, dom_start, 0)
    stats_held[mine] = stats_ref[...]
    part_held[me] = columns(me)[...]

    def orient_finish(k, carry):
        orient_copy(k).wait()
        return carry

    def dom_finish(k, carry):
        dom_copy(k).wait()
        return carry

    lax.fori_loop(1, orient_n, orient_finish, 0)
    lax.fori_loop(1, dom_n, dom_finish, 0)
    stats_out[...] = stats_held[...]
    part_out[...] = part_held[...]


def stats_and_columns(stats, part_rows, dom_n, orient_n, width, collective_id):
    shapes = (
        jax.ShapeDtypeStruct((orient_n,) + stats.shape, stats.dtype),
        jax.ShapeDtypeStruct((dom_n, part_rows.shape[0], width // 2), part_rows.dtype),
    )
    vmem = pl.BlockSpec(memory_space=pltpu.VMEM)
    return pl.pallas_call(
        functools.partial(_stats_kernel, dom_n, orient_n, width),
        out_shape=shapes,
        in_specs=[vmem] * 2,
        out_specs=(vmem, vmem),
        scratch_shapes=[
            pltpu.VMEM(shapes[0].shape, shapes[0].dtype),
            pltpu.VMEM(shapes[1].shape, shapes[1].dtype),
            pltpu.SemaphoreType.DMA((orient_n,)),
            pltpu.SemaphoreType.DMA((orient_n,)),
            pltpu.SemaphoreType.DMA((dom_n,)),
            pltpu.SemaphoreType.DMA((dom_n,)),
        ],
        compiler_params=pltpu.CompilerParams(collective_id=collective_id, has_side_effects=True),
    )(stats, part_rows)


def _spread_kernel(dom_n, orient_n, width, half_ref, small_ref, part_ref,
                   half_out, small_out, part_out, terms_out,
                   half_held, small_held, part_held, summed, terms_held,
                   send_sem, recv_sem, orient_send, orient_recv):
    me = lax.axis_index("dom")
    mine = lax.axis_index("orient")
    barrier = pltpu.get_barrier_semaphore()

    def greet_dom(k, carry):
        peer = lax.rem(me + k, dom_n)
        pl.semaphore_signal(barrier, inc=1, device_id={"dom": peer}, device_id_type=MESH_ID)
        return carry

    def greet_orient(k, carry):
        peer = lax.rem(mine + k, orient_n)
        pl.semaphore_signal(barrier, inc=1, device_id={"orient": peer}, device_id_type=MESH_ID)
        return carry

    lax.fori_loop(1, dom_n, greet_dom, 0)
    lax.fori_loop(1, orient_n, greet_orient, 0)
    pl.semaphore_wait(barrier, dom_n + orient_n - 2)

    half_width = width // 2

    def columns(peer):
        return part_ref.at[:, pl.ds(pl.multiple_of(peer * width + half_width, half_width), half_width)]

    sources = (lambda peer: half_ref, lambda peer: small_ref, columns)
    held = (half_held, small_held, part_held)

    def copy(index, k):
        peer = lax.rem(me + k, dom_n)
        return pltpu.make_async_remote_copy(
            src_ref=sources[index](peer),
            dst_ref=held[index].at[me],
            send_sem=send_sem.at[index, k],
            recv_sem=recv_sem.at[index, k],
            device_id={"dom": peer},
            device_id_type=MESH_ID,
        )

    def start(k, carry):
        for index in (1, 0, 2):
            copy(index, k).start()
        return carry

    lax.fori_loop(1, dom_n, start, 0)
    for index in range(3):
        held[index][me] = sources[index](me)[...]

    def finish(index):
        def body(k, carry):
            copy(index, k).wait()
            return carry

        lax.fori_loop(1, dom_n, body, 0)

    finish(1)
    summed[...] = jnp.sum(small_held[...], axis=0)
    finish(0)

    def orient_copy(k):
        peer = lax.rem(mine + k, orient_n)
        return pltpu.make_async_remote_copy(
            src_ref=summed,
            dst_ref=terms_held.at[mine],
            send_sem=orient_send.at[k],
            recv_sem=orient_recv.at[k],
            device_id={"orient": peer},
            device_id_type=MESH_ID,
        )

    def orient_start(k, carry):
        orient_copy(k).start()
        return carry

    lax.fori_loop(1, orient_n, orient_start, 0)
    terms_held[mine] = summed[...]
    finish(2)

    def orient_finish(k, carry):
        orient_copy(k).wait()
        return carry

    lax.fori_loop(1, orient_n, orient_finish, 0)
    half_out[...] = half_held[...]
    small_out[...] = small_held[...]
    part_out[...] = part_held[...]
    terms_out[...] = terms_held[...]


def spread(half_rows, small, part_rows, dom_n, orient_n, width, collective_id):
    shapes = (
        jax.ShapeDtypeStruct((dom_n,) + half_rows.shape, half_rows.dtype),
        jax.ShapeDtypeStruct((dom_n,) + small.shape, small.dtype),
        jax.ShapeDtypeStruct((dom_n, part_rows.shape[0], width // 2), part_rows.dtype),
        jax.ShapeDtypeStruct((orient_n,) + small.shape, small.dtype),
    )
    vmem = pl.BlockSpec(memory_space=pltpu.VMEM)
    return pl.pallas_call(
        functools.partial(_spread_kernel, dom_n, orient_n, width),
        out_shape=shapes,
        in_specs=[vmem] * 3,
        out_specs=(vmem,) * 4,
        scratch_shapes=[
            pltpu.VMEM(shapes[0].shape, shapes[0].dtype),
            pltpu.VMEM(shapes[1].shape, shapes[1].dtype),
            pltpu.VMEM(shapes[2].shape, shapes[2].dtype),
            pltpu.VMEM(small.shape, small.dtype),
            pltpu.VMEM(shapes[3].shape, shapes[3].dtype),
            pltpu.SemaphoreType.DMA((3, dom_n)),
            pltpu.SemaphoreType.DMA((3, dom_n)),
            pltpu.SemaphoreType.DMA((orient_n,)),
            pltpu.SemaphoreType.DMA((orient_n,)),
        ],
        compiler_params=pltpu.CompilerParams(collective_id=collective_id, has_side_effects=True),
    )(half_rows, small, part_rows)


def make_images(planes, ctf_pix, cosine, sine_part):
    real_part = planes[:, 0][:, None, :]
    imag_part = planes[:, 1][:, None, :]
    shifted_real = real_part * cosine[None] - imag_part * sine_part[None]
    shifted_imag = real_part * sine_part[None] + imag_part * cosine[None]
    factor = ctf_pix[:, None, :]
    return jnp.stack([factor * shifted_real, factor * shifted_imag], axis=2).astype(jnp.bfloat16)


def pad_rows(rows, lanes):
    r, c = rows.shape
    height = -(-r // 8) * 8
    return jnp.pad(rows, ((0, height - r), (0, lanes - c)))


def on_device(particles, references, phases, mask, ctf_group, ctf_table, shell_index, sigma2):
    highest = lax.Precision.HIGHEST
    part_dev = particles.shape[0]
    ori_dev = references.shape[0]
    pixels = shell_index.shape[0]
    shells = ctf_table.shape[1]
    trans_count = phases.shape[0]
    dom_size = lax.axis_size("dom")
    orient_size = lax.axis_size("orient")
    width = pixels // dom_size
    dom_index = lax.axis_index("dom")

    shell_pick = (shell_index[:, None] == jnp.arange(shells, dtype=jnp.int32)[None, :]).astype(
        jnp.float32
    )
    group_pick = (
        ctf_group[:, None] == jnp.arange(ctf_table.shape[0], dtype=jnp.int32)[None, :]
    ).astype(jnp.float32)
    ctf_all = jnp.dot(group_pick, ctf_table, precision=highest)
    ctf_rows = lax.dynamic_slice_in_dim(ctf_all, dom_index * part_dev, part_dev, 0)
    per_pixel = jnp.dot(
        jnp.concatenate([ctf_rows, sigma2[None]], axis=0), shell_pick.T, precision=highest
    )
    ctf_pix = per_pixel[:part_dev]
    sigma_pix = per_pixel[part_dev]
    refs_wide = references.astype(jnp.float32)
    weighted = (refs_wide / sigma_pix).astype(jnp.bfloat16)
    planes = particles.astype(jnp.float32)
    norms = jnp.dot(
        jnp.concatenate([jnp.sum(refs_wide * refs_wide, axis=1), jnp.sum(planes * planes, axis=1)], axis=0),
        shell_pick,
        precision=highest,
    )
    ref_norm = norms[:ori_dev]
    part_norm = norms[ori_dev:]
    energy = ref_norm / sigma2
    ctf_square = ctf_rows * ctf_rows
    quadratic = 0.5 * jnp.dot(ctf_square, energy.T, precision=highest)
    cosines = jnp.cos(phases)
    sine_rows = jnp.sin(phases)

    images = make_images(planes, ctf_pix, cosines, sine_rows)
    cross = jnp.einsum("itpk,jpk->itj", images, weighted, preferred_element_type=jnp.float32)
    scores = cross - quadratic[:, None, :]
    scores = jnp.where((mask == 1)[:, None, :], scores, -1e30)
    local_peak = jnp.max(scores, axis=(1, 2))
    local_total = jnp.sum(jnp.exp(scores - local_peak[:, None, None]), axis=(1, 2))

    part_rows = particles.reshape(part_dev * 2, pixels)
    stats, columns_a = stats_and_columns(
        pad_rows(jnp.stack([local_peak, local_total]), 128),
        part_rows,
        dom_size,
        orient_size,
        width,
        1,
    )
    peaks = stats[:, 0, :part_dev]
    totals = stats[:, 1, :part_dev]
    peak = jnp.max(peaks, axis=0)
    total = jnp.sum(totals * jnp.exp(peaks - peak[None, :]), axis=0)
    posterior = jnp.exp(scores - peak[:, None, None]) / total[:, None, None]
    post_half = posterior.astype(jnp.bfloat16)

    weight_rows = jnp.sum(posterior, axis=1)
    ctf_part = jnp.dot(weight_rows.T, ctf_square, precision=highest)
    term_one = jnp.sum(part_norm * jnp.sum(weight_rows, axis=1)[:, None], axis=0)
    term_three = jnp.sum(ctf_part * ref_norm, axis=0)
    local_sums = jnp.einsum("itj,itpk->jpk", post_half, images, preferred_element_type=jnp.float32)
    term_two = -2.0 * jnp.dot(jnp.sum(local_sums * refs_wide, axis=(0, 1)), shell_pick, precision=highest)
    terms = term_one + term_two + term_three

    term_cols = -(-shells // part_dev)
    term_rows = jnp.pad(terms, (0, term_cols * part_dev - shells)).reshape(part_dev, term_cols)
    small = jnp.concatenate([weight_rows, term_rows], axis=1)
    small = jnp.pad(small, ((0, 0), (0, -(-small.shape[1] // 128) * 128 - small.shape[1])))
    half_rows = post_half.reshape(-1, 128)
    half_all, small_all, columns_b, orient_small = spread(
        half_rows, small, part_rows, dom_size, orient_size, width, 2
    )
    columns = jnp.concatenate([columns_a, columns_b], axis=2)
    post_all = half_all.reshape(dom_size * part_dev, trans_count, ori_dev)
    weight_all = small_all[:, :, :ori_dev].reshape(dom_size * part_dev, ori_dev)
    shell_total = jnp.sum(
        orient_small[:, :, ori_dev : ori_dev + term_cols].reshape(orient_size, part_dev * term_cols)[:, :shells],
        axis=0,
    )

    ctf_weights = jnp.dot(weight_all.T, ctf_all * ctf_all, precision=highest)

    start_pix = dom_index * width
    pick_cols = lax.dynamic_slice_in_dim(shell_pick, start_pix, width, 0)
    ctf_cols = jnp.dot(ctf_all, pick_cols.T, precision=highest)
    cos_cols = lax.dynamic_slice_in_dim(cosines, start_pix, width, 1)
    sin_cols = lax.dynamic_slice_in_dim(sine_rows, start_pix, width, 1)
    col_planes = columns.reshape(dom_size * part_dev, 2, width).astype(jnp.float32)
    col_images = make_images(col_planes, ctf_cols, cos_cols, sin_cols)
    image_sums = jnp.einsum(
        "itj,itpk->jpk", post_all, col_images, preferred_element_type=jnp.float32
    )

    divisor = part_dev * dom_size * pixels / shells
    return (posterior, image_sums, ctf_weights, shell_total / divisor)


def solution(mesh):
    return jax.shard_map(
        on_device,
        mesh=mesh,
        in_specs=(
            P("dom", None, None),
            P("orient", None, None),
            P(),
            P("dom", "orient"),
            P(),
            P(),
            P(),
            P(),
        ),
        out_specs=(P("dom", None, "orient"), P("orient", None, "dom"), P("orient", None), P()),
        check_vma=False,
    )
```

```python
import functools

import jax
import jax.numpy as jnp
from jax import lax
from jax.experimental import pallas as pl
from jax.experimental.pallas import tpu as pltpu
from jax.sharding import PartitionSpec as P

MESH_ID = pl.DeviceIdType.MESH


def _exchange_kernel(axis, n, widths, *refs):
    count = len(widths)
    x_refs = refs[:count]
    o_refs = refs[count : 2 * count]
    held = refs[2 * count : 3 * count]
    send_sem, recv_sem = refs[3 * count :]
    me = lax.axis_index(axis)
    barrier = pltpu.get_barrier_semaphore()

    def greet(k, carry):
        peer = lax.rem(me + k, n)
        pl.semaphore_signal(barrier, inc=1, device_id={axis: peer}, device_id_type=MESH_ID)
        return carry

    lax.fori_loop(1, n, greet, 0)
    pl.semaphore_wait(barrier, n - 1)

    def part(index, peer):
        width = widths[index]
        if width is None:
            return x_refs[index]
        return x_refs[index].at[:, pl.ds(pl.multiple_of(peer * width, width), width)]

    def copy(index, k):
        peer = lax.rem(me + k, n)
        return pltpu.make_async_remote_copy(
            src_ref=part(index, peer),
            dst_ref=held[index].at[me],
            send_sem=send_sem.at[index, k],
            recv_sem=recv_sem.at[index, k],
            device_id={axis: peer},
            device_id_type=MESH_ID,
        )

    def start(k, carry):
        for index in range(count):
            copy(index, k).start()
        return carry

    lax.fori_loop(1, n, start, 0)
    for index in range(count):
        held[index][me] = part(index, me)[...]

    def finish(k, carry):
        for index in range(count):
            copy(index, k).wait()
        return carry

    lax.fori_loop(1, n, finish, 0)
    for index in range(count):
        o_refs[index][...] = held[index][...]


def exchange(payloads, axis, n, collective_id):
    widths = tuple(width for _, width in payloads)
    shapes = []
    for x, width in payloads:
        block = x.shape if width is None else (x.shape[0], width)
        shapes.append(jax.ShapeDtypeStruct((n,) + block, x.dtype))
    count = len(payloads)
    vmem = pl.BlockSpec(memory_space=pltpu.VMEM)
    return pl.pallas_call(
        functools.partial(_exchange_kernel, axis, n, widths),
        out_shape=tuple(shapes),
        in_specs=[vmem] * count,
        out_specs=tuple([vmem] * count),
        scratch_shapes=[pltpu.VMEM(shape.shape, shape.dtype) for shape in shapes]
        + [pltpu.SemaphoreType.DMA((count, n)), pltpu.SemaphoreType.DMA((count, n))],
        compiler_params=pltpu.CompilerParams(collective_id=collective_id, has_side_effects=True),
    )(*[x for x, _ in payloads])


def _stats_kernel(dom_n, orient_n, width, stats_ref, part_ref, stats_out, part_out,
                  stats_held, part_held, orient_send, orient_recv, dom_send, dom_recv,
                  pass_send, pass_recv):
    me = lax.axis_index("dom")
    mine = lax.axis_index("orient")
    core = lax.rem(mine, 2)
    partner = mine + 1 - 2 * core
    half = width // 2
    barrier = pltpu.get_barrier_semaphore()

    def greet_dom(k, carry):
        peer = lax.rem(me + k, dom_n)
        pl.semaphore_signal(barrier, inc=1, device_id={"dom": peer}, device_id_type=MESH_ID)
        return carry

    def greet_orient(k, carry):
        peer = lax.rem(mine + k, orient_n)
        pl.semaphore_signal(barrier, inc=1, device_id={"orient": peer}, device_id_type=MESH_ID)
        return carry

    lax.fori_loop(1, orient_n, greet_orient, 0)
    lax.fori_loop(1, dom_n, greet_dom, 0)
    pl.semaphore_wait(barrier, dom_n + orient_n - 2)

    def orient_copy(k):
        peer = lax.rem(mine + k, orient_n)
        return pltpu.make_async_remote_copy(
            src_ref=stats_ref,
            dst_ref=stats_held.at[mine],
            send_sem=orient_send.at[k],
            recv_sem=orient_recv.at[k],
            device_id={"orient": peer},
            device_id_type=MESH_ID,
        )

    lanes = pl.ds(pl.multiple_of(core * half, half), half)

    def dom_copy(k):
        peer = lax.rem(me + k, dom_n)
        return pltpu.make_async_remote_copy(
            src_ref=part_ref.at[:, pl.ds(pl.multiple_of(peer * width + core * half, half), half)],
            dst_ref=part_held.at[me, :, lanes],
            send_sem=dom_send.at[k],
            recv_sem=dom_recv.at[k],
            device_id={"dom": peer},
            device_id_type=MESH_ID,
        )

    def pass_copy(k):
        source = lax.rem(me + dom_n - k, dom_n)
        return pltpu.make_async_remote_copy(
            src_ref=part_held.at[source, :, lanes],
            dst_ref=part_held.at[source, :, lanes],
            send_sem=pass_send.at[k],
            recv_sem=pass_recv.at[k],
            device_id={"orient": partner},
            device_id_type=MESH_ID,
        )

    def orient_start(k, carry):
        orient_copy(k).start()
        return carry

    def dom_start(k, carry):
        dom_copy(k).start()
        return carry

    lax.fori_loop(1, orient_n, orient_start, 0)
    lax.fori_loop(1, dom_n, dom_start, 0)
    stats_held[mine] = stats_ref[...]
    part_held[me] = part_ref[:, pl.ds(pl.multiple_of(me * width, width), width)]

    def pass_on(k, carry):
        dom_copy(k).wait_recv()
        pass_copy(k).start()
        return carry

    lax.fori_loop(1, dom_n, pass_on, 0)

    def orient_finish(k, carry):
        orient_copy(k).wait()
        return carry

    def dom_finish(k, carry):
        dom_copy(k).wait_send()
        pass_copy(k).wait()
        return carry

    lax.fori_loop(1, orient_n, orient_finish, 0)
    lax.fori_loop(1, dom_n, dom_finish, 0)
    stats_out[...] = stats_held[...]
    part_out[...] = part_held[...]


def stats_and_columns(stats, part_rows, dom_n, orient_n, width, collective_id):
    shapes = (
        jax.ShapeDtypeStruct((orient_n,) + stats.shape, stats.dtype),
        jax.ShapeDtypeStruct((dom_n, part_rows.shape[0], width), part_rows.dtype),
    )
    vmem = pl.BlockSpec(memory_space=pltpu.VMEM)
    return pl.pallas_call(
        functools.partial(_stats_kernel, dom_n, orient_n, width),
        out_shape=shapes,
        in_specs=[vmem] * 2,
        out_specs=(vmem, vmem),
        scratch_shapes=[
            pltpu.VMEM(shapes[0].shape, shapes[0].dtype),
            pltpu.VMEM(shapes[1].shape, shapes[1].dtype),
            pltpu.SemaphoreType.DMA((orient_n,)),
            pltpu.SemaphoreType.DMA((orient_n,)),
            pltpu.SemaphoreType.DMA((dom_n,)),
            pltpu.SemaphoreType.DMA((dom_n,)),
            pltpu.SemaphoreType.DMA((dom_n,)),
            pltpu.SemaphoreType.DMA((dom_n,)),
        ],
        compiler_params=pltpu.CompilerParams(collective_id=collective_id, has_side_effects=True),
    )(stats, part_rows)


def _spread_kernel(dom_n, orient_n, half_ref, small_ref,
                   half_out, small_out, terms_out,
                   half_held, small_held, summed, terms_held,
                   send_sem, recv_sem, orient_send, orient_recv):
    me = lax.axis_index("dom")
    mine = lax.axis_index("orient")
    barrier = pltpu.get_barrier_semaphore()

    def greet_dom(k, carry):
        peer = lax.rem(me + k, dom_n)
        pl.semaphore_signal(barrier, inc=1, device_id={"dom": peer}, device_id_type=MESH_ID)
        return carry

    def greet_orient(k, carry):
        peer = lax.rem(mine + k, orient_n)
        pl.semaphore_signal(barrier, inc=1, device_id={"orient": peer}, device_id_type=MESH_ID)
        return carry

    lax.fori_loop(1, dom_n, greet_dom, 0)
    lax.fori_loop(1, orient_n, greet_orient, 0)
    pl.semaphore_wait(barrier, dom_n + orient_n - 2)

    sources = (half_ref, small_ref)
    held = (half_held, small_held)

    def copy(index, k):
        peer = lax.rem(me + k, dom_n)
        return pltpu.make_async_remote_copy(
            src_ref=sources[index],
            dst_ref=held[index].at[me],
            send_sem=send_sem.at[index, k],
            recv_sem=recv_sem.at[index, k],
            device_id={"dom": peer},
            device_id_type=MESH_ID,
        )

    def start(k, carry):
        for index in (1, 0):
            copy(index, k).start()
        return carry

    lax.fori_loop(1, dom_n, start, 0)
    for index in range(2):
        held[index][me] = sources[index][...]

    def finish(index):
        def body(k, carry):
            copy(index, k).wait()
            return carry

        lax.fori_loop(1, dom_n, body, 0)

    finish(1)
    summed[...] = jnp.sum(small_held[...], axis=0)
    finish(0)

    def orient_copy(k):
        peer = lax.rem(mine + k, orient_n)
        return pltpu.make_async_remote_copy(
            src_ref=summed,
            dst_ref=terms_held.at[mine],
            send_sem=orient_send.at[k],
            recv_sem=orient_recv.at[k],
            device_id={"orient": peer},
            device_id_type=MESH_ID,
        )

    def orient_start(k, carry):
        orient_copy(k).start()
        return carry

    lax.fori_loop(1, orient_n, orient_start, 0)
    terms_held[mine] = summed[...]

    def orient_finish(k, carry):
        orient_copy(k).wait()
        return carry

    lax.fori_loop(1, orient_n, orient_finish, 0)
    half_out[...] = half_held[...]
    small_out[...] = small_held[...]
    terms_out[...] = terms_held[...]


def spread(half_rows, small, dom_n, orient_n, collective_id):
    shapes = (
        jax.ShapeDtypeStruct((dom_n,) + half_rows.shape, half_rows.dtype),
        jax.ShapeDtypeStruct((dom_n,) + small.shape, small.dtype),
        jax.ShapeDtypeStruct((orient_n,) + small.shape, small.dtype),
    )
    vmem = pl.BlockSpec(memory_space=pltpu.VMEM)
    return pl.pallas_call(
        functools.partial(_spread_kernel, dom_n, orient_n),
        out_shape=shapes,
        in_specs=[vmem] * 2,
        out_specs=(vmem,) * 3,
        scratch_shapes=[
            pltpu.VMEM(shapes[0].shape, shapes[0].dtype),
            pltpu.VMEM(shapes[1].shape, shapes[1].dtype),
            pltpu.VMEM(small.shape, small.dtype),
            pltpu.VMEM(shapes[2].shape, shapes[2].dtype),
            pltpu.SemaphoreType.DMA((2, dom_n)),
            pltpu.SemaphoreType.DMA((2, dom_n)),
            pltpu.SemaphoreType.DMA((orient_n,)),
            pltpu.SemaphoreType.DMA((orient_n,)),
        ],
        compiler_params=pltpu.CompilerParams(collective_id=collective_id, has_side_effects=True),
    )(half_rows, small)


def make_images(planes, ctf_pix, cosine, sine_part):
    real_part = planes[:, 0][:, None, :]
    imag_part = planes[:, 1][:, None, :]
    shifted_real = real_part * cosine[None] - imag_part * sine_part[None]
    shifted_imag = real_part * sine_part[None] + imag_part * cosine[None]
    factor = ctf_pix[:, None, :]
    return jnp.stack([factor * shifted_real, factor * shifted_imag], axis=2).astype(jnp.bfloat16)


def pad_rows(rows, lanes):
    r, c = rows.shape
    height = -(-r // 8) * 8
    return jnp.pad(rows, ((0, height - r), (0, lanes - c)))


def on_device(particles, references, phases, mask, ctf_group, ctf_table, shell_index, sigma2):
    highest = lax.Precision.HIGHEST
    part_dev = particles.shape[0]
    ori_dev = references.shape[0]
    pixels = shell_index.shape[0]
    shells = ctf_table.shape[1]
    trans_count = phases.shape[0]
    dom_size = lax.axis_size("dom")
    orient_size = lax.axis_size("orient")
    width = pixels // dom_size
    dom_index = lax.axis_index("dom")

    shell_pick = (shell_index[:, None] == jnp.arange(shells, dtype=jnp.int32)[None, :]).astype(
        jnp.float32
    )
    group_pick = (
        ctf_group[:, None] == jnp.arange(ctf_table.shape[0], dtype=jnp.int32)[None, :]
    ).astype(jnp.float32)
    ctf_all = jnp.dot(group_pick, ctf_table, precision=highest)
    ctf_rows = lax.dynamic_slice_in_dim(ctf_all, dom_index * part_dev, part_dev, 0)
    per_pixel = jnp.dot(
        jnp.concatenate([ctf_rows, sigma2[None]], axis=0), shell_pick.T, precision=highest
    )
    ctf_pix = per_pixel[:part_dev]
    sigma_pix = per_pixel[part_dev]
    refs_wide = references.astype(jnp.float32)
    weighted = (refs_wide / sigma_pix).astype(jnp.bfloat16)
    planes = particles.astype(jnp.float32)
    norms = jnp.dot(
        jnp.concatenate([jnp.sum(refs_wide * refs_wide, axis=1), jnp.sum(planes * planes, axis=1)], axis=0),
        shell_pick,
        precision=highest,
    )
    ref_norm = norms[:ori_dev]
    part_norm = norms[ori_dev:]
    energy = ref_norm / sigma2
    ctf_square = ctf_rows * ctf_rows
    quadratic = 0.5 * jnp.dot(ctf_square, energy.T, precision=highest)
    cosines = jnp.cos(phases)
    sine_rows = jnp.sin(phases)

    images = make_images(planes, ctf_pix, cosines, sine_rows)
    cross = jnp.einsum("itpk,jpk->itj", images, weighted, preferred_element_type=jnp.float32)
    scores = cross - quadratic[:, None, :]
    scores = jnp.where((mask == 1)[:, None, :], scores, -1e30)
    local_peak = jnp.max(scores, axis=(1, 2))
    local_total = jnp.sum(jnp.exp(scores - local_peak[:, None, None]), axis=(1, 2))

    stats, columns = stats_and_columns(
        pad_rows(jnp.stack([local_peak, local_total]), 128),
        particles.reshape(part_dev * 2, pixels),
        dom_size,
        orient_size,
        width,
        1,
    )
    peaks = stats[:, 0, :part_dev]
    totals = stats[:, 1, :part_dev]
    peak = jnp.max(peaks, axis=0)
    total = jnp.sum(totals * jnp.exp(peaks - peak[None, :]), axis=0)
    posterior = jnp.exp(scores - peak[:, None, None]) / total[:, None, None]
    post_half = posterior.astype(jnp.bfloat16)

    weight_rows = jnp.sum(posterior, axis=1)
    ctf_part = jnp.dot(weight_rows.T, ctf_square, precision=highest)
    term_one = jnp.sum(part_norm * jnp.sum(weight_rows, axis=1)[:, None], axis=0)
    term_three = jnp.sum(ctf_part * ref_norm, axis=0)
    local_sums = jnp.einsum("itj,itpk->jpk", post_half, images, preferred_element_type=jnp.float32)
    term_two = -2.0 * jnp.dot(jnp.sum(local_sums * refs_wide, axis=(0, 1)), shell_pick, precision=highest)
    terms = term_one + term_two + term_three

    term_cols = -(-shells // part_dev)
    term_rows = jnp.pad(terms, (0, term_cols * part_dev - shells)).reshape(part_dev, term_cols)
    small = jnp.concatenate([weight_rows, term_rows], axis=1)
    small = jnp.pad(small, ((0, 0), (0, -(-small.shape[1] // 128) * 128 - small.shape[1])))
    half_rows = post_half.reshape(-1, 128)
    half_all, small_all, orient_small = spread(half_rows, small, dom_size, orient_size, 2)
    post_all = half_all.reshape(dom_size * part_dev, trans_count, ori_dev)
    weight_all = small_all[:, :, :ori_dev].reshape(dom_size * part_dev, ori_dev)
    shell_total = jnp.sum(
        orient_small[:, :, ori_dev : ori_dev + term_cols].reshape(orient_size, part_dev * term_cols)[:, :shells],
        axis=0,
    )

    ctf_weights = jnp.dot(weight_all.T, ctf_all * ctf_all, precision=highest)

    start_pix = dom_index * width
    pick_cols = lax.dynamic_slice_in_dim(shell_pick, start_pix, width, 0)
    ctf_cols = jnp.dot(ctf_all, pick_cols.T, precision=highest)
    cos_cols = lax.dynamic_slice_in_dim(cosines, start_pix, width, 1)
    sin_cols = lax.dynamic_slice_in_dim(sine_rows, start_pix, width, 1)
    col_planes = columns.reshape(dom_size * part_dev, 2, width).astype(jnp.float32)
    col_images = make_images(col_planes, ctf_cols, cos_cols, sin_cols)
    image_sums = jnp.einsum(
        "itj,itpk->jpk", post_all, col_images, preferred_element_type=jnp.float32
    )

    divisor = part_dev * dom_size * pixels / shells
    return (posterior, image_sums, ctf_weights, shell_total / divisor)


def solution(mesh):
    return jax.shard_map(
        on_device,
        mesh=mesh,
        in_specs=(
            P("dom", None, None),
            P("orient", None, None),
            P(),
            P("dom", "orient"),
            P(),
            P(),
            P(),
            P(),
        ),
        out_specs=(P("dom", None, "orient"), P("orient", None, "dom"), P("orient", None), P()),
        check_vma=False,
    )
```

```python
import functools

import jax
import jax.numpy as jnp
from jax import lax
from jax.experimental import pallas as pl
from jax.experimental.pallas import tpu as pltpu
from jax.sharding import PartitionSpec as P

MESH_ID = pl.DeviceIdType.MESH


def _exchange_kernel(axis, n, widths, *refs):
    count = len(widths)
    x_refs = refs[:count]
    o_refs = refs[count : 2 * count]
    held = refs[2 * count : 3 * count]
    send_sem, recv_sem = refs[3 * count :]
    me = lax.axis_index(axis)
    barrier = pltpu.get_barrier_semaphore()

    def greet(k, carry):
        peer = lax.rem(me + k, n)
        pl.semaphore_signal(barrier, inc=1, device_id={axis: peer}, device_id_type=MESH_ID)
        return carry

    lax.fori_loop(1, n, greet, 0)
    pl.semaphore_wait(barrier, n - 1)

    def part(index, peer):
        width = widths[index]
        if width is None:
            return x_refs[index]
        return x_refs[index].at[:, pl.ds(pl.multiple_of(peer * width, width), width)]

    def copy(index, k):
        peer = lax.rem(me + k, n)
        return pltpu.make_async_remote_copy(
            src_ref=part(index, peer),
            dst_ref=held[index].at[me],
            send_sem=send_sem.at[index, k],
            recv_sem=recv_sem.at[index, k],
            device_id={axis: peer},
            device_id_type=MESH_ID,
        )

    def start(k, carry):
        for index in range(count):
            copy(index, k).start()
        return carry

    lax.fori_loop(1, n, start, 0)
    for index in range(count):
        held[index][me] = part(index, me)[...]

    def finish(k, carry):
        for index in range(count):
            copy(index, k).wait()
        return carry

    lax.fori_loop(1, n, finish, 0)
    for index in range(count):
        o_refs[index][...] = held[index][...]


def exchange(payloads, axis, n, collective_id):
    widths = tuple(width for _, width in payloads)
    shapes = []
    for x, width in payloads:
        block = x.shape if width is None else (x.shape[0], width)
        shapes.append(jax.ShapeDtypeStruct((n,) + block, x.dtype))
    count = len(payloads)
    vmem = pl.BlockSpec(memory_space=pltpu.VMEM)
    return pl.pallas_call(
        functools.partial(_exchange_kernel, axis, n, widths),
        out_shape=tuple(shapes),
        in_specs=[vmem] * count,
        out_specs=tuple([vmem] * count),
        scratch_shapes=[pltpu.VMEM(shape.shape, shape.dtype) for shape in shapes]
        + [pltpu.SemaphoreType.DMA((count, n)), pltpu.SemaphoreType.DMA((count, n))],
        compiler_params=pltpu.CompilerParams(collective_id=collective_id, has_side_effects=True),
    )(*[x for x, _ in payloads])


def _stats_kernel(dom_n, orient_n, width, stats_ref, part_ref, stats_out, part_out,
                  stats_held, part_held, orient_send, orient_recv, dom_send, dom_recv):
    me = lax.axis_index("dom")
    mine = lax.axis_index("orient")
    barrier = pltpu.get_barrier_semaphore()

    def greet_dom(k, carry):
        peer = lax.rem(me + k, dom_n)
        pl.semaphore_signal(barrier, inc=1, device_id={"dom": peer}, device_id_type=MESH_ID)
        return carry

    def greet_orient(k, carry):
        peer = lax.rem(mine + k, orient_n)
        pl.semaphore_signal(barrier, inc=1, device_id={"orient": peer}, device_id_type=MESH_ID)
        return carry

    lax.fori_loop(1, orient_n, greet_orient, 0)
    lax.fori_loop(1, dom_n, greet_dom, 0)
    pl.semaphore_wait(barrier, dom_n + orient_n - 2)

    def orient_copy(k):
        peer = lax.rem(mine + k, orient_n)
        return pltpu.make_async_remote_copy(
            src_ref=stats_ref,
            dst_ref=stats_held.at[mine],
            send_sem=orient_send.at[k],
            recv_sem=orient_recv.at[k],
            device_id={"orient": peer},
            device_id_type=MESH_ID,
        )

    def columns(peer):
        return part_ref.at[:, pl.ds(pl.multiple_of(peer * width, width), width)]

    def dom_copy(k):
        peer = lax.rem(me + k, dom_n)
        return pltpu.make_async_remote_copy(
            src_ref=columns(peer),
            dst_ref=part_held.at[me],
            send_sem=dom_send.at[k],
            recv_sem=dom_recv.at[k],
            device_id={"dom": peer},
            device_id_type=MESH_ID,
        )

    def orient_start(k, carry):
        orient_copy(k).start()
        return carry

    def dom_start(k, carry):
        dom_copy(k).start()
        return carry

    lax.fori_loop(1, orient_n, orient_start, 0)
    lax.fori_loop(1, dom_n, dom_start, 0)
    stats_held[mine] = stats_ref[...]
    part_held[me] = columns(me)[...]

    def orient_finish(k, carry):
        orient_copy(k).wait()
        return carry

    def dom_finish(k, carry):
        dom_copy(k).wait()
        return carry

    lax.fori_loop(1, orient_n, orient_finish, 0)
    lax.fori_loop(1, dom_n, dom_finish, 0)
    stats_out[...] = stats_held[...]
    part_out[...] = part_held[...]


def stats_and_columns(stats, part_rows, dom_n, orient_n, width, collective_id):
    shapes = (
        jax.ShapeDtypeStruct((orient_n,) + stats.shape, stats.dtype),
        jax.ShapeDtypeStruct((dom_n, part_rows.shape[0], width), part_rows.dtype),
    )
    vmem = pl.BlockSpec(memory_space=pltpu.VMEM)
    return pl.pallas_call(
        functools.partial(_stats_kernel, dom_n, orient_n, width),
        out_shape=shapes,
        in_specs=[vmem] * 2,
        out_specs=(vmem, vmem),
        scratch_shapes=[
            pltpu.VMEM(shapes[0].shape, shapes[0].dtype),
            pltpu.VMEM(shapes[1].shape, shapes[1].dtype),
            pltpu.SemaphoreType.DMA((orient_n,)),
            pltpu.SemaphoreType.DMA((orient_n,)),
            pltpu.SemaphoreType.DMA((dom_n,)),
            pltpu.SemaphoreType.DMA((dom_n,)),
        ],
        compiler_params=pltpu.CompilerParams(collective_id=collective_id, has_side_effects=True),
    )(stats, part_rows)


def _spread_kernel(dom_n, orient_n, lead, packed_ref, packed_out, terms_out,
                   packed_held, summed, terms_held, send_sem, recv_sem, orient_send, orient_recv):
    me = lax.axis_index("dom")
    mine = lax.axis_index("orient")
    barrier = pltpu.get_barrier_semaphore()

    def greet_dom(k, carry):
        peer = lax.rem(me + k, dom_n)
        pl.semaphore_signal(barrier, inc=1, device_id={"dom": peer}, device_id_type=MESH_ID)
        return carry

    def greet_orient(k, carry):
        peer = lax.rem(mine + k, orient_n)
        pl.semaphore_signal(barrier, inc=1, device_id={"orient": peer}, device_id_type=MESH_ID)
        return carry

    lax.fori_loop(1, dom_n, greet_dom, 0)
    lax.fori_loop(1, orient_n, greet_orient, 0)
    pl.semaphore_wait(barrier, dom_n + orient_n - 2)

    def copy(k):
        peer = lax.rem(me + k, dom_n)
        return pltpu.make_async_remote_copy(
            src_ref=packed_ref,
            dst_ref=packed_held.at[me],
            send_sem=send_sem.at[k],
            recv_sem=recv_sem.at[k],
            device_id={"dom": peer},
            device_id_type=MESH_ID,
        )

    def start(k, carry):
        copy(k).start()
        return carry

    lax.fori_loop(1, dom_n, start, 0)
    packed_held[me] = packed_ref[...]

    def finish(k, carry):
        copy(k).wait()
        return carry

    lax.fori_loop(1, dom_n, finish, 0)
    summed[...] = jnp.sum(packed_held[:, lead:, :], axis=0)

    def orient_copy(k):
        peer = lax.rem(mine + k, orient_n)
        return pltpu.make_async_remote_copy(
            src_ref=summed,
            dst_ref=terms_held.at[mine],
            send_sem=orient_send.at[k],
            recv_sem=orient_recv.at[k],
            device_id={"orient": peer},
            device_id_type=MESH_ID,
        )

    def orient_start(k, carry):
        orient_copy(k).start()
        return carry

    lax.fori_loop(1, orient_n, orient_start, 0)
    terms_held[mine] = summed[...]

    def orient_finish(k, carry):
        orient_copy(k).wait()
        return carry

    lax.fori_loop(1, orient_n, orient_finish, 0)
    packed_out[...] = packed_held[...]
    terms_out[...] = terms_held[...]


def spread(packed, lead, dom_n, orient_n, collective_id):
    small_shape = (packed.shape[0] - lead, packed.shape[1])
    shapes = (
        jax.ShapeDtypeStruct((dom_n,) + packed.shape, packed.dtype),
        jax.ShapeDtypeStruct((orient_n,) + small_shape, packed.dtype),
    )
    vmem = pl.BlockSpec(memory_space=pltpu.VMEM)
    return pl.pallas_call(
        functools.partial(_spread_kernel, dom_n, orient_n, lead),
        out_shape=shapes,
        in_specs=[vmem],
        out_specs=(vmem, vmem),
        scratch_shapes=[
            pltpu.VMEM(shapes[0].shape, shapes[0].dtype),
            pltpu.VMEM(small_shape, packed.dtype),
            pltpu.VMEM(shapes[1].shape, shapes[1].dtype),
            pltpu.SemaphoreType.DMA((dom_n,)),
            pltpu.SemaphoreType.DMA((dom_n,)),
            pltpu.SemaphoreType.DMA((orient_n,)),
            pltpu.SemaphoreType.DMA((orient_n,)),
        ],
        compiler_params=pltpu.CompilerParams(collective_id=collective_id, has_side_effects=True),
    )(packed)


def make_images(planes, ctf_pix, cosine, sine_part):
    real_part = planes[:, 0][:, None, :]
    imag_part = planes[:, 1][:, None, :]
    shifted_real = real_part * cosine[None] - imag_part * sine_part[None]
    shifted_imag = real_part * sine_part[None] + imag_part * cosine[None]
    factor = ctf_pix[:, None, :]
    return jnp.stack([factor * shifted_real, factor * shifted_imag], axis=2).astype(jnp.bfloat16)


def pad_rows(rows, lanes):
    r, c = rows.shape
    height = -(-r // 8) * 8
    return jnp.pad(rows, ((0, height - r), (0, lanes - c)))


def on_device(particles, references, phases, mask, ctf_group, ctf_table, shell_index, sigma2):
    highest = lax.Precision.HIGHEST
    part_dev = particles.shape[0]
    ori_dev = references.shape[0]
    pixels = shell_index.shape[0]
    shells = ctf_table.shape[1]
    trans_count = phases.shape[0]
    dom_size = lax.axis_size("dom")
    orient_size = lax.axis_size("orient")
    width = pixels // dom_size
    dom_index = lax.axis_index("dom")

    shell_pick = (shell_index[:, None] == jnp.arange(shells, dtype=jnp.int32)[None, :]).astype(
        jnp.float32
    )
    group_pick = (
        ctf_group[:, None] == jnp.arange(ctf_table.shape[0], dtype=jnp.int32)[None, :]
    ).astype(jnp.float32)
    ctf_all = jnp.dot(group_pick, ctf_table, precision=highest)
    ctf_rows = lax.dynamic_slice_in_dim(ctf_all, dom_index * part_dev, part_dev, 0)
    per_pixel = jnp.dot(
        jnp.concatenate([ctf_rows, sigma2[None]], axis=0), shell_pick.T, precision=highest
    )
    ctf_pix = per_pixel[:part_dev]
    sigma_pix = per_pixel[part_dev]
    refs_wide = references.astype(jnp.float32)
    weighted = (refs_wide / sigma_pix).astype(jnp.bfloat16)
    planes = particles.astype(jnp.float32)
    norms = jnp.dot(
        jnp.concatenate([jnp.sum(refs_wide * refs_wide, axis=1), jnp.sum(planes * planes, axis=1)], axis=0),
        shell_pick,
        precision=highest,
    )
    ref_norm = norms[:ori_dev]
    part_norm = norms[ori_dev:]
    energy = ref_norm / sigma2
    ctf_square = ctf_rows * ctf_rows
    quadratic = 0.5 * jnp.dot(ctf_square, energy.T, precision=highest)
    cosines = jnp.cos(phases)
    sine_rows = jnp.sin(phases)

    images = make_images(planes, ctf_pix, cosines, sine_rows)
    cross = jnp.einsum("itpk,jpk->itj", images, weighted, preferred_element_type=jnp.float32)
    scores = cross - quadratic[:, None, :]
    scores = jnp.where((mask == 1)[:, None, :], scores, -1e30)
    local_peak = jnp.max(scores, axis=(1, 2))
    local_total = jnp.sum(jnp.exp(scores - local_peak[:, None, None]), axis=(1, 2))

    stats, columns = stats_and_columns(
        pad_rows(jnp.stack([local_peak, local_total]), 128),
        particles.reshape(part_dev * 2, pixels),
        dom_size,
        orient_size,
        width,
        1,
    )
    peaks = stats[:, 0, :part_dev]
    totals = stats[:, 1, :part_dev]
    peak = jnp.max(peaks, axis=0)
    total = jnp.sum(totals * jnp.exp(peaks - peak[None, :]), axis=0)
    posterior = jnp.exp(scores - peak[:, None, None]) / total[:, None, None]
    post_half = posterior.astype(jnp.bfloat16)

    weight_rows = jnp.sum(posterior, axis=1)
    ctf_part = jnp.dot(weight_rows.T, ctf_square, precision=highest)
    term_one = jnp.sum(part_norm * jnp.sum(weight_rows, axis=1)[:, None], axis=0)
    term_three = jnp.sum(ctf_part * ref_norm, axis=0)
    local_sums = jnp.einsum("itj,itpk->jpk", post_half, images, preferred_element_type=jnp.float32)
    term_two = -2.0 * jnp.dot(jnp.sum(local_sums * refs_wide, axis=(0, 1)), shell_pick, precision=highest)
    terms = term_one + term_two + term_three

    term_cols = -(-shells // part_dev)
    term_rows = jnp.pad(terms, (0, term_cols * part_dev - shells)).reshape(part_dev, term_cols)
    small = jnp.concatenate([weight_rows, term_rows], axis=1)
    small = jnp.pad(small, ((0, 0), (0, -(-small.shape[1] // 128) * 128 - small.shape[1])))
    half_rows = post_half.reshape(-1, 128)
    lead = half_rows.shape[0]
    packed_all, orient_small = spread(
        jnp.concatenate([half_rows.astype(jnp.float32), small], axis=0), lead, dom_size, orient_size, 2
    )
    half_all = packed_all[:, :lead, :].astype(jnp.bfloat16)
    small_all = packed_all[:, lead:, :]
    post_all = half_all.reshape(dom_size * part_dev, trans_count, ori_dev)
    weight_all = small_all[:, :, :ori_dev].reshape(dom_size * part_dev, ori_dev)
    shell_total = jnp.sum(
        orient_small[:, :, ori_dev : ori_dev + term_cols].reshape(orient_size, part_dev * term_cols)[:, :shells],
        axis=0,
    )

    ctf_weights = jnp.dot(weight_all.T, ctf_all * ctf_all, precision=highest)

    start_pix = dom_index * width
    pick_cols = lax.dynamic_slice_in_dim(shell_pick, start_pix, width, 0)
    ctf_cols = jnp.dot(ctf_all, pick_cols.T, precision=highest)
    cos_cols = lax.dynamic_slice_in_dim(cosines, start_pix, width, 1)
    sin_cols = lax.dynamic_slice_in_dim(sine_rows, start_pix, width, 1)
    col_planes = columns.reshape(dom_size * part_dev, 2, width).astype(jnp.float32)
    col_images = make_images(col_planes, ctf_cols, cos_cols, sin_cols)
    image_sums = jnp.einsum(
        "itj,itpk->jpk", post_all, col_images, preferred_element_type=jnp.float32
    )

    divisor = part_dev * dom_size * pixels / shells
    return (posterior, image_sums, ctf_weights, shell_total / divisor)


def solution(mesh):
    return jax.shard_map(
        on_device,
        mesh=mesh,
        in_specs=(
            P("dom", None, None),
            P("orient", None, None),
            P(),
            P("dom", "orient"),
            P(),
            P(),
            P(),
            P(),
        ),
        out_specs=(P("dom", None, "orient"), P("orient", None, "dom"), P("orient", None), P()),
        check_vma=False,
    )
```

```python
import functools

import jax
import jax.numpy as jnp
from jax import lax
from jax.experimental import pallas as pl
from jax.experimental.pallas import tpu as pltpu
from jax.sharding import PartitionSpec as P

MESH_ID = pl.DeviceIdType.MESH


def _exchange_kernel(axis, n, widths, *refs):
    count = len(widths)
    x_refs = refs[:count]
    o_refs = refs[count : 2 * count]
    held = refs[2 * count : 3 * count]
    send_sem, recv_sem = refs[3 * count :]
    me = lax.axis_index(axis)
    barrier = pltpu.get_barrier_semaphore()

    def greet(k, carry):
        peer = lax.rem(me + k, n)
        pl.semaphore_signal(barrier, inc=1, device_id={axis: peer}, device_id_type=MESH_ID)
        return carry

    lax.fori_loop(1, n, greet, 0)
    pl.semaphore_wait(barrier, n - 1)

    def part(index, peer):
        width = widths[index]
        if width is None:
            return x_refs[index]
        return x_refs[index].at[:, pl.ds(pl.multiple_of(peer * width, width), width)]

    def copy(index, k):
        peer = lax.rem(me + k, n)
        return pltpu.make_async_remote_copy(
            src_ref=part(index, peer),
            dst_ref=held[index].at[me],
            send_sem=send_sem.at[index, k],
            recv_sem=recv_sem.at[index, k],
            device_id={axis: peer},
            device_id_type=MESH_ID,
        )

    def start(k, carry):
        for index in range(count):
            copy(index, k).start()
        return carry

    lax.fori_loop(1, n, start, 0)
    for index in range(count):
        held[index][me] = part(index, me)[...]

    def finish(k, carry):
        for index in range(count):
            copy(index, k).wait()
        return carry

    lax.fori_loop(1, n, finish, 0)
    for index in range(count):
        o_refs[index][...] = held[index][...]


def exchange(payloads, axis, n, collective_id):
    widths = tuple(width for _, width in payloads)
    shapes = []
    for x, width in payloads:
        block = x.shape if width is None else (x.shape[0], width)
        shapes.append(jax.ShapeDtypeStruct((n,) + block, x.dtype))
    count = len(payloads)
    vmem = pl.BlockSpec(memory_space=pltpu.VMEM)
    return pl.pallas_call(
        functools.partial(_exchange_kernel, axis, n, widths),
        out_shape=tuple(shapes),
        in_specs=[vmem] * count,
        out_specs=tuple([vmem] * count),
        scratch_shapes=[pltpu.VMEM(shape.shape, shape.dtype) for shape in shapes]
        + [pltpu.SemaphoreType.DMA((count, n)), pltpu.SemaphoreType.DMA((count, n))],
        compiler_params=pltpu.CompilerParams(collective_id=collective_id, has_side_effects=True),
    )(*[x for x, _ in payloads])


def _stats_kernel(dom_n, orient_n, width, stats_ref, part_ref, stats_out, part_out,
                  stats_held, part_held, orient_send, orient_recv, dom_send, dom_recv):
    me = lax.axis_index("dom")
    mine = lax.axis_index("orient")
    barrier = pltpu.get_barrier_semaphore()

    def greet_dom(k, carry):
        peer = lax.rem(me + k, dom_n)
        pl.semaphore_signal(barrier, inc=1, device_id={"dom": peer}, device_id_type=MESH_ID)
        return carry

    def greet_orient(k, carry):
        peer = lax.rem(mine + k, orient_n)
        pl.semaphore_signal(barrier, inc=1, device_id={"orient": peer}, device_id_type=MESH_ID)
        return carry

    lax.fori_loop(1, orient_n, greet_orient, 0)
    lax.fori_loop(1, dom_n, greet_dom, 0)
    pl.semaphore_wait(barrier, dom_n + orient_n - 2)

    def orient_copy(k):
        peer = lax.rem(mine + k, orient_n)
        return pltpu.make_async_remote_copy(
            src_ref=stats_ref,
            dst_ref=stats_held.at[mine],
            send_sem=orient_send.at[k],
            recv_sem=orient_recv.at[k],
            device_id={"orient": peer},
            device_id_type=MESH_ID,
        )

    def columns(peer):
        return part_ref.at[:, :, pl.ds(pl.multiple_of(peer * width, width), width)]

    def dom_copy(k):
        peer = lax.rem(me + k, dom_n)
        return pltpu.make_async_remote_copy(
            src_ref=columns(peer),
            dst_ref=part_held.at[me],
            send_sem=dom_send.at[k],
            recv_sem=dom_recv.at[k],
            device_id={"dom": peer},
            device_id_type=MESH_ID,
        )

    def orient_start(k, carry):
        orient_copy(k).start()
        return carry

    def dom_start(k, carry):
        dom_copy(k).start()
        return carry

    lax.fori_loop(1, orient_n, orient_start, 0)
    lax.fori_loop(1, dom_n, dom_start, 0)
    stats_held[mine] = stats_ref[...]
    part_held[me] = columns(me)[...]

    def orient_finish(k, carry):
        orient_copy(k).wait()
        return carry

    def dom_finish(k, carry):
        dom_copy(k).wait()
        return carry

    lax.fori_loop(1, orient_n, orient_finish, 0)
    lax.fori_loop(1, dom_n, dom_finish, 0)
    stats_out[...] = stats_held[...]
    part_out[...] = part_held[...]


def stats_and_columns(stats, part_rows, dom_n, orient_n, width, collective_id):
    shapes = (
        jax.ShapeDtypeStruct((orient_n,) + stats.shape, stats.dtype),
        jax.ShapeDtypeStruct((dom_n,) + part_rows.shape[:2] + (width,), part_rows.dtype),
    )
    vmem = pl.BlockSpec(memory_space=pltpu.VMEM)
    return pl.pallas_call(
        functools.partial(_stats_kernel, dom_n, orient_n, width),
        out_shape=shapes,
        in_specs=[vmem] * 2,
        out_specs=(vmem, vmem),
        scratch_shapes=[
            pltpu.VMEM(shapes[0].shape, shapes[0].dtype),
            pltpu.VMEM(shapes[1].shape, shapes[1].dtype),
            pltpu.SemaphoreType.DMA((orient_n,)),
            pltpu.SemaphoreType.DMA((orient_n,)),
            pltpu.SemaphoreType.DMA((dom_n,)),
            pltpu.SemaphoreType.DMA((dom_n,)),
        ],
        compiler_params=pltpu.CompilerParams(collective_id=collective_id, has_side_effects=True),
    )(stats, part_rows)


def _spread_kernel(dom_n, orient_n, half_ref, small_ref,
                   half_out, small_out, terms_out,
                   half_held, small_held, summed, terms_held,
                   send_sem, recv_sem, orient_send, orient_recv):
    me = lax.axis_index("dom")
    mine = lax.axis_index("orient")
    barrier = pltpu.get_barrier_semaphore()

    def greet_dom(k, carry):
        peer = lax.rem(me + k, dom_n)
        pl.semaphore_signal(barrier, inc=1, device_id={"dom": peer}, device_id_type=MESH_ID)
        return carry

    def greet_orient(k, carry):
        peer = lax.rem(mine + k, orient_n)
        pl.semaphore_signal(barrier, inc=1, device_id={"orient": peer}, device_id_type=MESH_ID)
        return carry

    lax.fori_loop(1, dom_n, greet_dom, 0)
    lax.fori_loop(1, orient_n, greet_orient, 0)
    pl.semaphore_wait(barrier, dom_n + orient_n - 2)

    sources = (half_ref, small_ref)
    held = (half_held, small_held)

    def copy(index, k):
        peer = lax.rem(me + k, dom_n)
        return pltpu.make_async_remote_copy(
            src_ref=sources[index],
            dst_ref=held[index].at[me],
            send_sem=send_sem.at[index, k],
            recv_sem=recv_sem.at[index, k],
            device_id={"dom": peer},
            device_id_type=MESH_ID,
        )

    def start(k, carry):
        for index in (1, 0):
            copy(index, k).start()
        return carry

    lax.fori_loop(1, dom_n, start, 0)
    for index in range(2):
        held[index][me] = sources[index][...]

    def finish(index):
        def body(k, carry):
            copy(index, k).wait()
            return carry

        lax.fori_loop(1, dom_n, body, 0)

    finish(1)
    summed[...] = jnp.sum(small_held[...], axis=0)
    finish(0)

    def orient_copy(k):
        peer = lax.rem(mine + k, orient_n)
        return pltpu.make_async_remote_copy(
            src_ref=summed,
            dst_ref=terms_held.at[mine],
            send_sem=orient_send.at[k],
            recv_sem=orient_recv.at[k],
            device_id={"orient": peer},
            device_id_type=MESH_ID,
        )

    def orient_start(k, carry):
        orient_copy(k).start()
        return carry

    lax.fori_loop(1, orient_n, orient_start, 0)
    terms_held[mine] = summed[...]

    def orient_finish(k, carry):
        orient_copy(k).wait()
        return carry

    lax.fori_loop(1, orient_n, orient_finish, 0)
    half_out[...] = half_held[...]
    small_out[...] = small_held[...]
    terms_out[...] = terms_held[...]


def spread(half_rows, small, dom_n, orient_n, collective_id):
    shapes = (
        jax.ShapeDtypeStruct((dom_n,) + half_rows.shape, half_rows.dtype),
        jax.ShapeDtypeStruct((dom_n,) + small.shape, small.dtype),
        jax.ShapeDtypeStruct((orient_n,) + small.shape, small.dtype),
    )
    vmem = pl.BlockSpec(memory_space=pltpu.VMEM)
    return pl.pallas_call(
        functools.partial(_spread_kernel, dom_n, orient_n),
        out_shape=shapes,
        in_specs=[vmem] * 2,
        out_specs=(vmem,) * 3,
        scratch_shapes=[
            pltpu.VMEM(shapes[0].shape, shapes[0].dtype),
            pltpu.VMEM(shapes[1].shape, shapes[1].dtype),
            pltpu.VMEM(small.shape, small.dtype),
            pltpu.VMEM(shapes[2].shape, shapes[2].dtype),
            pltpu.SemaphoreType.DMA((2, dom_n)),
            pltpu.SemaphoreType.DMA((2, dom_n)),
            pltpu.SemaphoreType.DMA((orient_n,)),
            pltpu.SemaphoreType.DMA((orient_n,)),
        ],
        compiler_params=pltpu.CompilerParams(collective_id=collective_id, has_side_effects=True),
    )(half_rows, small)


def make_images(planes, ctf_pix, cosine, sine_part):
    real_part = planes[:, 0][:, None, :]
    imag_part = planes[:, 1][:, None, :]
    shifted_real = real_part * cosine[None] - imag_part * sine_part[None]
    shifted_imag = real_part * sine_part[None] + imag_part * cosine[None]
    factor = ctf_pix[:, None, :]
    return jnp.stack([factor * shifted_real, factor * shifted_imag], axis=2).astype(jnp.bfloat16)


def pad_rows(rows, lanes):
    r, c = rows.shape
    height = -(-r // 8) * 8
    return jnp.pad(rows, ((0, height - r), (0, lanes - c)))


def on_device(particles, references, phases, mask, ctf_group, ctf_table, shell_index, sigma2):
    highest = lax.Precision.HIGHEST
    part_dev = particles.shape[0]
    ori_dev = references.shape[0]
    pixels = shell_index.shape[0]
    shells = ctf_table.shape[1]
    trans_count = phases.shape[0]
    dom_size = lax.axis_size("dom")
    orient_size = lax.axis_size("orient")
    width = pixels // dom_size
    dom_index = lax.axis_index("dom")

    shell_pick = (shell_index[:, None] == jnp.arange(shells, dtype=jnp.int32)[None, :]).astype(
        jnp.float32
    )
    group_pick = (
        ctf_group[:, None] == jnp.arange(ctf_table.shape[0], dtype=jnp.int32)[None, :]
    ).astype(jnp.float32)
    ctf_all = jnp.dot(group_pick, ctf_table, precision=highest)
    ctf_rows = lax.dynamic_slice_in_dim(ctf_all, dom_index * part_dev, part_dev, 0)
    per_pixel = jnp.dot(
        jnp.concatenate([ctf_rows, sigma2[None]], axis=0), shell_pick.T, precision=highest
    )
    ctf_pix = per_pixel[:part_dev]
    sigma_pix = per_pixel[part_dev]
    refs_wide = references.astype(jnp.float32)
    weighted = (refs_wide / sigma_pix).astype(jnp.bfloat16)
    planes = particles.astype(jnp.float32)
    norms = jnp.dot(
        jnp.concatenate([jnp.sum(refs_wide * refs_wide, axis=1), jnp.sum(planes * planes, axis=1)], axis=0),
        shell_pick,
        precision=highest,
    )
    ref_norm = norms[:ori_dev]
    part_norm = norms[ori_dev:]
    energy = ref_norm / sigma2
    ctf_square = ctf_rows * ctf_rows
    quadratic = 0.5 * jnp.dot(ctf_square, energy.T, precision=highest)
    cosines = jnp.cos(phases)
    sine_rows = jnp.sin(phases)

    images = make_images(planes, ctf_pix, cosines, sine_rows)
    cross = jnp.einsum("itpk,jpk->itj", images, weighted, preferred_element_type=jnp.float32)
    scores = cross - quadratic[:, None, :]
    scores = jnp.where((mask == 1)[:, None, :], scores, -1e30)
    local_peak = jnp.max(scores, axis=(1, 2))
    local_total = jnp.sum(jnp.exp(scores - local_peak[:, None, None]), axis=(1, 2))

    stats, columns = stats_and_columns(
        pad_rows(jnp.stack([local_peak, local_total]), 128),
        particles,
        dom_size,
        orient_size,
        width,
        1,
    )
    peaks = stats[:, 0, :part_dev]
    totals = stats[:, 1, :part_dev]
    peak = jnp.max(peaks, axis=0)
    total = jnp.sum(totals * jnp.exp(peaks - peak[None, :]), axis=0)
    posterior = jnp.exp(scores - peak[:, None, None]) / total[:, None, None]
    post_half = posterior.astype(jnp.bfloat16)

    weight_rows = jnp.sum(posterior, axis=1)
    ctf_part = jnp.dot(weight_rows.T, ctf_square, precision=highest)
    term_one = jnp.sum(part_norm * jnp.sum(weight_rows, axis=1)[:, None], axis=0)
    term_three = jnp.sum(ctf_part * ref_norm, axis=0)
    local_sums = jnp.einsum("itj,itpk->jpk", post_half, images, preferred_element_type=jnp.float32)
    term_two = -2.0 * jnp.dot(jnp.sum(local_sums * refs_wide, axis=(0, 1)), shell_pick, precision=highest)
    terms = term_one + term_two + term_three

    term_cols = -(-shells // part_dev)
    term_rows = jnp.pad(terms, (0, term_cols * part_dev - shells)).reshape(part_dev, term_cols)
    small = jnp.concatenate([weight_rows, term_rows], axis=1)
    small = jnp.pad(small, ((0, 0), (0, -(-small.shape[1] // 128) * 128 - small.shape[1])))
    half_rows = post_half.reshape(-1, 128)
    half_all, small_all, orient_small = spread(half_rows, small, dom_size, orient_size, 2)
    post_all = half_all.reshape(dom_size * part_dev, trans_count, ori_dev)
    weight_all = small_all[:, :, :ori_dev].reshape(dom_size * part_dev, ori_dev)
    shell_total = jnp.sum(
        orient_small[:, :, ori_dev : ori_dev + term_cols].reshape(orient_size, part_dev * term_cols)[:, :shells],
        axis=0,
    )

    ctf_weights = jnp.dot(weight_all.T, ctf_all * ctf_all, precision=highest)

    start_pix = dom_index * width
    pick_cols = lax.dynamic_slice_in_dim(shell_pick, start_pix, width, 0)
    ctf_cols = jnp.dot(ctf_all, pick_cols.T, precision=highest)
    cos_cols = lax.dynamic_slice_in_dim(cosines, start_pix, width, 1)
    sin_cols = lax.dynamic_slice_in_dim(sine_rows, start_pix, width, 1)
    col_planes = columns.reshape(dom_size * part_dev, 2, width).astype(jnp.float32)
    col_images = make_images(col_planes, ctf_cols, cos_cols, sin_cols)
    image_sums = jnp.einsum(
        "itj,itpk->jpk", post_all, col_images, preferred_element_type=jnp.float32
    )

    divisor = part_dev * dom_size * pixels / shells
    return (posterior, image_sums, ctf_weights, shell_total / divisor)


def solution(mesh):
    return jax.shard_map(
        on_device,
        mesh=mesh,
        in_specs=(
            P("dom", None, None),
            P("orient", None, None),
            P(),
            P("dom", "orient"),
            P(),
            P(),
            P(),
            P(),
        ),
        out_specs=(P("dom", None, "orient"), P("orient", None, "dom"), P("orient", None), P()),
        check_vma=False,
    )
```
